32 devices in a mesh: dp: 8 (over z, y), tensor: 4 (over x, core).
Axes of the slice: x: 2, y: 2, z: 4, core: 2. Of those that a mesh axis runs over, the one named last changes fastest.
Arguments:
- block_input: bfloat16 [25088, 768], P(('dp', 'tensor')), may hold values from -6 to 6
- cotangent: bfloat16 [25088, 768], P(('dp', 'tensor')), may hold values from -6 to 6
- pad_mask: int32 [128, 196], replicated, may hold values from 0 to 1, as said below
- slot_window: int32 [128], P('dp'), may hold values from -1 to 127, as said below
- qkv_w: bfloat16 [3, 768, 768], P(None, 'dp', 'tensor'), may hold values from -0.21875 to 0.21875
- proj_w: bfloat16 [768, 768], P('tensor', 'dp'), may hold values from -1.25 to 1.25
- fc1_w: bfloat16 [768, 3072], P('dp', 'tensor'), may hold values from -0.21875 to 0.21875
- fc2_w: bfloat16 [3072, 768], P('tensor', 'dp'), may hold values from -0.109375 to 0.109375
- norm1_gain: float32 [768], replicated, may hold values from 0.5 to 1.5
- norm1_bias: float32 [768], replicated, may hold values from -3 to 3
- q_bias: float32 [768], replicated, may hold values from -3 to 3
- v_bias: float32 [768], replicated, may hold values from -3 to 3
- rel_h: float32 [27, 64], replicated, may hold values from -0.9 to 0.9
- rel_w: float32 [27, 64], replicated, may hold values from -0.9 to 0.9
- proj_bias: float32 [768], replicated, may hold values from -3 to 3
- norm2_gain: float32 [768], replicated, may hold values from 0.5 to 1.5
- norm2_bias: float32 [768], replicated, may hold values from -3 to 3
- fc1_bias: float32 [3072], replicated, may hold values from -3 to 3
- fc2_bias: float32 [768], replicated, may hold values from -3 to 3
Outputs:
- result: bfloat16 [25088, 768], P(('dp', 'tensor'))
- grad_x: bfloat16 [25088, 768], P(('dp', 'tensor'))
- grad_qkv_w: float32 [3, 768, 768], P(None, 'dp', 'tensor')
- grad_proj_w: float32 [768, 768], P('tensor', 'dp')
- grad_fc1_w: float32 [768, 3072], P('dp', 'tensor')
- grad_fc2_w: float32 [3072, 768], P('tensor', 'dp')
- grad_norm1_gain: float32 [768], replicated
- grad_norm1_bias: float32 [768], replicated
- grad_q_bias: float32 [768], replicated
- grad_v_bias: float32 [768], replicated
- grad_rel_h: float32 [27, 64], replicated
- grad_rel_w: float32 [27, 64], replicated
- grad_proj_bias: float32 [768], replicated
- grad_norm2_gain: float32 [768], replicated
- grad_norm2_bias: float32 [768], replicated
- grad_fc1_bias: float32 [3072], replicated
- grad_fc2_bias: float32 [768], replicated
The draws below stay inside these ranges and needn't reach their ends.
Inputs may be any that keep to these rules, and one draw needn't show every extreme that they name: In each window the tokens with pad_mask 1 form a rectangle of 4 to 14 rows by 4 to 14 columns at the window's first row and column. `slot_window`: on each index of dp the first slots hold windows and the rest are empty (-1); each index of dp holds 8 to 16 windows, and some index holds 16; no window is named twice.
All inputs are finite; a program needn't handle non-finite values.
Results may differ from the reference program's by a relative error of at most 0.019.
Values may be sent and summed in bfloat16 or wider, within the bound.
A program may use at most 192 MiB of HBM per device.

```python
from functools import partial
import jax
import jax.numpy as jnp
from jax import lax

D = 768
HEADS = 12
HD = 64
FF = 3072
WS = 14
WT = 196
REL = 27
WIN_DEV = 16
NWIN = 128


def draw_pad_mask(key, part):
    first, second, third = jax.random.split(jax.random.fold_in(key, 11), 3)
    whole = jax.random.randint(first, (NWIN,), 0, 2)
    height = jnp.where(whole == 1, WS, jax.random.randint(second, (NWIN,), 4, WS + 1))
    breadth = jnp.where(whole == 1, WS, jax.random.randint(third, (NWIN,), 4, WS + 1))
    places = jnp.arange(WT)
    inside = (places[None, :] // WS < height[:, None]) & (places[None, :] % WS < breadth[:, None])
    return inside.astype(jnp.int32)


def draw_slot_window(key, part):
    first, second, third = jax.random.split(jax.random.fold_in(key, 23), 3)
    groups = NWIN // WIN_DEV
    counts = jax.random.randint(first, (groups,), WIN_DEV // 2, WIN_DEV + 1)
    fullest = jax.random.randint(second, (), 0, groups)
    counts = jnp.where(jnp.arange(groups) == fullest, WIN_DEV, counts)
    order = jax.random.permutation(third, NWIN).astype(jnp.int32).reshape(groups, WIN_DEV)
    alive = jnp.arange(WIN_DEV)[None, :] < counts[:, None]
    return jnp.where(alive, order, -1).reshape(NWIN).astype(jnp.int32)


def shard_levels(rng, extent, cuts, low, high):
    def one(dim, blocks):
        draws = jax.random.uniform(jax.random.fold_in(jax.random.fold_in(rng, 6), dim), (blocks,), jnp.float32, low / len(cuts), high / len(cuts))
        return jnp.repeat(jnp.exp(draws), extent[dim] // blocks).reshape((-1,) + (1,) * (len(extent) - dim - 1))

    level = one(*cuts[0])
    for cut in cuts[1:]:
        level = level * one(*cut)
    return level


def gaussian(key, shape, spread, most, cuts=(), dtype=jnp.bfloat16):
    entries = jax.random.normal(key, shape, jnp.float32) * spread
    if len(cuts) > 0:
        entries = shard_levels(key, shape, cuts, -0.22, 0.18) * entries
    return jnp.clip(entries, min=-most, max=most).astype(dtype)


def setup_inputs(seed: int = 0) -> dict:
    seeds = jax.random.split(jax.random.key(seed), 20)
    return {
        "block_input": gaussian(seeds[0], (NWIN * WT, D), 1.0, 6.0, ((0, 32),)),
        "cotangent": gaussian(seeds[1], (NWIN * WT, D), 1.0, 6.0, ((0, 32),)),
        "pad_mask": draw_pad_mask(jax.random.fold_in(seeds[19], 71), 0),
        "slot_window": draw_slot_window(jax.random.fold_in(seeds[19], 71), 0),
        "qkv_w": gaussian(seeds[4], (3, D, D), D ** -0.5, 0.21875, ((1, 8), (2, 4))),
        "proj_w": gaussian(seeds[5], (D, D), (D // 32) ** -0.5, 1.25, ((0, 4), (1, 8))),
        "fc1_w": gaussian(seeds[6], (D, FF), D ** -0.5, 0.21875, ((0, 8), (1, 4))),
        "fc2_w": gaussian(seeds[7], (FF, D), FF ** -0.5, 0.109375, ((0, 4), (1, 8))),
        "norm1_gain": jnp.clip(1.0 + 0.1 * jax.random.normal(seeds[8], (D,), jnp.float32), 0.5, 1.5),
        "norm1_bias": gaussian(seeds[9], (D,), 0.5, 3.0, (), jnp.float32),
        "q_bias": gaussian(seeds[10], (D,), 0.5, 3.0, (), jnp.float32),
        "v_bias": gaussian(seeds[11], (D,), 0.5, 3.0, (), jnp.float32),
        "rel_h": gaussian(seeds[12], (REL, HD), 0.15, 0.9, (), jnp.float32),
        "rel_w": gaussian(seeds[13], (REL, HD), 0.15, 0.9, (), jnp.float32),
        "proj_bias": gaussian(seeds[14], (D,), 0.5, 3.0, (), jnp.float32),
        "norm2_gain": jnp.clip(1.0 + 0.1 * jax.random.normal(seeds[15], (D,), jnp.float32), 0.5, 1.5),
        "norm2_bias": gaussian(seeds[16], (D,), 0.5, 3.0, (), jnp.float32),
        "fc1_bias": gaussian(seeds[17], (FF,), 0.5, 3.0, (), jnp.float32),
        "fc2_bias": gaussian(seeds[18], (D,), 0.5, 3.0, (), jnp.float32),
    }


EPSILON = 1e-06
NEGATIVE = -1e+30
HIGH = lax.Precision.HIGHEST

@jax.custom_vjp
def low(v):
    return lax.optimization_barrier(v.astype(jnp.bfloat16)).astype(jnp.float32)

@jax.custom_vjp
def low_back(v):
    return v

def low_keep(v):
    return (low(v), None)

def low_pass(kept, grad):
    return (grad,)

def back_keep(v):
    return (v, None)

def back_low(kept, grad):
    return (low(grad),)
low.defvjp(low_keep, low_pass)
low_back.defvjp(back_keep, back_low)

def normalize(values, gain, shift):
    center = values - lax.optimization_barrier(jnp.mean(values, -1, keepdims=True))
    return center * lax.rsqrt(lax.optimization_barrier(jnp.mean(center * center, -1, keepdims=True)) + EPSILON) * gain + shift

def offsets(size):
    places = jnp.arange(size)
    index = places[:, None] - places[None, :] + size - 1
    return (index[:, :, None] == jnp.arange(2 * size - 1)[None, None, :]).astype(jnp.float32)

def window_block(inputs, table_h, table_w):
    query, key_low, value, valid = inputs
    blocks, length, heads, depth = query.shape
    size = table_h.shape[0]
    base = jnp.einsum('gqhd,gkhd->ghqk', query, key_low, precision=HIGH) * depth ** (-0.5)
    wide = query.reshape(blocks, size, size, heads, depth)
    bias_h = jnp.einsum('gachd,abd->ghacb', wide, table_h, precision=HIGH)
    bias_w = jnp.einsum('gachd,ced->ghace', wide, table_w, precision=HIGH)
    total = base.reshape(blocks, heads, size, size, size, size) + bias_h[..., :, None] + bias_w[..., None, :]
    total = total.reshape(blocks, heads, length, length)
    scores = low_back(jnp.where(valid[:, None, None, :] > 0, total, NEGATIVE))
    top = lax.optimization_barrier(jnp.max(scores, -1, keepdims=True))
    expo = jnp.exp(scores - top)
    weights = low(expo / lax.optimization_barrier(jnp.sum(expo, -1, keepdims=True)))
    return jnp.einsum('ghqk,gkhd->gqhd', weights, value, precision=HIGH)

def reference(block_input, cotangent, pad_mask, slot_window, qkv_w, proj_w, fc1_w, fc2_w, norm1_gain, norm1_bias, q_bias, v_bias, rel_h, rel_w, proj_bias, norm2_gain, norm2_bias, fc1_bias, fc2_bias):
    alive = (slot_window >= 0).astype(jnp.int32)
    chosen = jnp.take(pad_mask, jnp.maximum(slot_window, 0).astype(jnp.int32), axis=0) * alive[:, None]
    valid = chosen.reshape(NWIN // 16, 16, WT)
    live_rows = jnp.repeat(alive.astype(jnp.float32), WT)[:, None]

    def forward(wide_x, w_qkv, w_proj, w_up, w_down, gain1, shift1, bias_q, bias_v, tab_h, tab_w, bias_proj, gain2, shift2, bias_up, bias_down):
        rows1 = low(normalize(wide_x, gain1, shift1))
        query = low(low_back(jnp.dot(rows1, w_qkv[0], precision=HIGH) + bias_q))
        key_low = low(low_back(jnp.dot(rows1, w_qkv[1], precision=HIGH)))
        value = low(low_back(jnp.dot(rows1, w_qkv[2], precision=HIGH) + bias_v))
        table_h = jnp.einsum('abk,kd->abd', offsets(WS), tab_h, precision=HIGH)
        table_w = jnp.einsum('abk,kd->abd', offsets(WS), tab_w, precision=HIGH)
        block_shape = (NWIN // 16, 16, WT, HEADS, HD)
        mixed = lax.map(jax.checkpoint(partial(window_block, table_h=table_h, table_w=table_w)), (query.reshape(block_shape), key_low.reshape(block_shape), value.reshape(block_shape), valid))
        mixed = low(low_back(mixed.reshape(NWIN * WT, D)))
        attn_branch = low_back(jnp.dot(mixed, w_proj, precision=HIGH) + bias_proj)
        middle = wide_x + attn_branch
        rows2 = low(normalize(middle, gain2, shift2))
        upper = low_back(jnp.dot(rows2, w_up, precision=HIGH) + bias_up)
        active = low(jax.nn.gelu(upper, approximate=False))
        mlp_branch = low_back(jnp.dot(active, w_down, precision=HIGH) + bias_down)
        return (middle + mlp_branch) * live_rows
    inputs = (block_input.astype(jnp.float32), qkv_w.astype(jnp.float32), proj_w.astype(jnp.float32), fc1_w.astype(jnp.float32), fc2_w.astype(jnp.float32), norm1_gain, norm1_bias, q_bias, v_bias, rel_h, rel_w, proj_bias, norm2_gain, norm2_bias, fc1_bias, fc2_bias)
    result, pull = jax.vjp(forward, *inputs)
    grads = pull(cotangent.astype(jnp.float32))
    return (result.astype(jnp.bfloat16), grads[0].astype(jnp.bfloat16), grads[1], grads[2], grads[3], grads[4], grads[5], grads[6], grads[7], grads[8], grads[9], grads[10], grads[11], grads[12], grads[13], grads[14], grads[15])
```

```python
from functools import partial

import jax
import jax.numpy as jnp
import numpy as np
from jax import lax
from jax.experimental import pallas as pl
from jax.experimental.pallas import tpu as pltpu
from jax.sharding import PartitionSpec as P

HD = 64
EPSILON = 1e-06
NEGATIVE = -1e30
F32, BF = jnp.float32, jnp.bfloat16
AXES = ("dp", "tensor")
VMEM_LIMIT = 60 * 1024 * 1024


def nn(left, right):
    return lax.dot_general(left, right, (((1,), (0,)), ((), ())), preferred_element_type=F32)


def nt(left, right):
    return lax.dot_general(left, right, (((1,), (1,)), ((), ())), preferred_element_type=F32)


def tn(left, right):
    return lax.dot_general(left, right, (((0,), (0,)), ((), ())), preferred_element_type=F32)


def normed_of(values):
    center = values - jnp.mean(values, -1, keepdims=True)
    inverse = lax.rsqrt(jnp.mean(center * center, -1, keepdims=True) + EPSILON)
    return center * inverse, inverse


def norm_back(grad, normed, inverse, gain):
    scaled = grad * gain
    inner = (
        scaled
        - jnp.mean(scaled, -1, keepdims=True)
        - normed * jnp.mean(scaled * normed, -1, keepdims=True)
    )
    return inverse * inner


def lanes_of(shape):
    return lax.broadcasted_iota(jnp.int32, shape, 1)


def shift_lanes(values, amounts, left):
    for bit in (1, 2, 4, 8):
        moved = pltpu.roll(values, 128 - bit if left else bit, 1)
        values = jnp.where((amounts & bit) != 0, moved, values)
    return values


def attend_kernel(
    x_ref, wa_ref, wb_ref, gain_ref, shift_ref, bias_ref, table_ref, key_feat_ref, amount_ref,
    query_ref, key_ref, value_ref, out_ref, acc_ref, h1_ref, qk_ref, vv_ref,
    *, windows, padded, keys,
):
    step = pl.program_id(0)

    @pl.when(step == 0)
    def _():
        normed, _ = normed_of(x_ref[...].astype(F32))
        h1_ref[...] = (normed * gain_ref[...] + shift_ref[...]).astype(BF)
        acc_ref[...] = jnp.zeros_like(acc_ref)

    h1 = h1_ref[...]
    qk_ref[...] = (nn(h1, wa_ref[...]) + bias_ref[0:1, :384]).astype(BF)
    vv_ref[...] = (nn(h1, wb_ref[:, :256]) + bias_ref[0:1, 384:640]).astype(BF)
    lane = lanes_of((padded, 128))
    low = lane < 64
    field = lane & 31
    amounts = amount_ref[...]
    pad_lane = lanes_of((keys - padded, 128))
    pad_key = jnp.where(pad_lane == 79, NEGATIVE, 0.0).astype(BF)

    def window(w, carry):
        rows = pl.ds(pl.multiple_of(w * padded, 16), padded)
        qk = qk_ref[rows, :]
        vv = vv_ref[rows, :]
        spread = nn(qk[:, :256], table_ref[0]) + nn(qk[:, :256], table_ref[1])
        wide = qk.astype(F32)
        wide_v = vv.astype(F32)
        parts = [wide[:, :128], wide[:, 128:256], wide[:, 256:384]]
        turned = [pltpu.roll(part, 64, 1) for part in parts]
        queries = [parts[0], turned[0], parts[1]]
        keys_low = [turned[1], parts[2], turned[2]]
        values = [wide_v[:, :128], pltpu.roll(wide_v[:, :128], 64, 1), wide_v[:, 128:256]]
        key_feat = key_feat_ref[rows, :].astype(F32)
        ones = jnp.where((lane == 64) | (lane == 65), 1.0, 0.0)
        outs = []
        for head in range(3):
            moved = shift_lanes(spread[:, head * 128 : head * 128 + 128], amounts, True)
            high = moved.astype(BF).astype(F32)
            rest = pltpu.roll(moved - high, 16, 1)
            feat = jnp.where(field < 16, high, rest)
            feat = jnp.where(field < 14, feat, jnp.where((field >= 16) & (field < 30), feat, 0.0))
            feat = jnp.where(lane == 79, 1.0, feat)
            query = jnp.where(low, queries[head] * 0.125, feat)
            key_ref[0, head, w, :padded, :] = jnp.where(low, keys_low[head], key_feat).astype(BF)
            key_ref[0, head, w, padded:, :] = pad_key
            value_ref[0, head, w, :padded, :] = jnp.where(low, values[head], ones).astype(BF)
            value_ref[0, head, w, padded:, :] = jnp.zeros((keys - padded, 128), BF)
            scores = nt(query.astype(BF), key_ref[0, head, w])
            top = jnp.max(scores, -1, keepdims=True)
            expo = jnp.exp(scores - top).astype(BF)
            mixed = nn(expo, value_ref[0, head, w])
            total = mixed[:, 64:65]
            outs.append(mixed / total)
            logsum = -(top + jnp.log(total))
            first = logsum.astype(BF).astype(F32)
            second = (logsum - first).astype(BF).astype(F32)
            third = logsum - first - second
            query = jnp.where(lane == 78, first, query)
            query = jnp.where(lane == 94, second, query)
            query = jnp.where(lane == 95, third, query)
            query_ref[0, head, rows, :] = query.astype(BF)
        out_ref[0, rows, :128] = jnp.where(low, 0.0, pltpu.roll(outs[0], 64, 1)).astype(BF)
        out_ref[0, rows, 128:] = jnp.where(low, outs[1], pltpu.roll(outs[2], 64, 1)).astype(BF)
        return carry

    lax.fori_loop(0, windows, window, 0)
    acc_ref[...] += nt(out_ref[0], wb_ref[:, 128:])


def mlp_kernel(
    x_ref, attn_ref, gy_ref, live_ref, up_ref, down_ref, bias_up_ref, gain_ref, shift_ref, bias_proj_ref, bias_down_ref,
    result_ref, gx1_ref, grad_up_ref, grad_down_ref, gbias_up_ref, small_ref,
    x1_ref, h2_ref, h2t_ref, gyt_ref, y_ref, dh_ref,
):
    step = pl.program_id(0)
    last = pl.num_programs(0) - 1

    @pl.when(step == 0)
    def _():
        x1 = x_ref[...].astype(F32) + (attn_ref[...] + bias_proj_ref[...])
        x1_ref[...] = x1
        normed, _ = normed_of(x1)
        h2 = (normed * gain_ref[...] + shift_ref[...]).astype(BF)
        h2_ref[...] = h2
        h2t_ref[...] = h2.T
        gyt_ref[...] = gy_ref[...].T
        y_ref[...] = jnp.zeros_like(y_ref)
        dh_ref[...] = jnp.zeros_like(dh_ref)

    up, down = up_ref[...], down_ref[...]
    upper = nn(h2_ref[...], up) + bias_up_ref[0]
    half = 0.5 * (1.0 + lax.erf(upper * np.float32(np.sqrt(0.5))))
    slope = half + upper * (np.float32(1.0 / np.sqrt(2 * np.pi)) * jnp.exp(-0.5 * upper * upper))
    active = (upper * half).astype(BF)
    grad_upper = (nn(gy_ref[...], down) * slope).astype(BF)
    y_ref[...] += nt(active, down)
    dh_ref[...] += nt(grad_upper, up)
    grad_down_ref[0] = nn(gyt_ref[...], active).astype(grad_down_ref.dtype)
    grad_up_ref[0] = nn(h2t_ref[...], grad_upper).astype(grad_up_ref.dtype)
    gbias_up_ref[0] = jnp.sum(grad_upper.astype(F32), 0, keepdims=True)

    @pl.when(step == last)
    def _():
        x1 = x1_ref[...]
        result = live_ref[...][:, :1] * (x1 + (y_ref[...] + bias_down_ref[...]))
        result_ref[...] = result.astype(BF)
        normed, inverse = normed_of(x1)
        gy = gy_ref[...].astype(F32)
        dh = dh_ref[...]
        gx1_ref[...] = gy + norm_back(dh, normed, inverse, gain_ref[...])
        small_ref[0:1, :] = jnp.sum(dh * normed, 0, keepdims=True)
        small_ref[1:2, :] = jnp.sum(dh, 0, keepdims=True)
        small_ref[2:3, :] = jnp.sum(gy, 0, keepdims=True)
        small_ref[3:8, :] = jnp.zeros_like(small_ref[3:8, :])


def attend_back_kernel(
    x_ref, gx1_ref, wa_ref, wb_ref, gain_ref, shift_ref, table_ref, amount_ref,
    query_ref, key_ref, value_ref, out_ref,
    grad_x_ref, grad_ref, small_ref, gbias_ref, grel_ref,
    h1t_ref, gbt_ref, gb_ref, dh_ref, do_ref, gqk_ref, gv_ref, spread_ref,
    *, windows, padded, keys,
):
    step = pl.program_id(0)
    last = pl.num_programs(0) - 1

    @pl.when(step == 0)
    def _():
        normed, _ = normed_of(x_ref[...].astype(F32))
        h1t_ref[...] = (normed * gain_ref[...] + shift_ref[...]).astype(BF).T
        gb = gx1_ref[...].astype(BF)
        gb_ref[...] = gb
        gbt_ref[...] = gb.T
        dh_ref[...] = jnp.zeros_like(dh_ref)
        grel_ref[...] = jnp.zeros_like(grel_ref)
        small_ref[0:1, :] = jnp.sum(gb.astype(F32), 0, keepdims=True)

    do_ref[...] = nn(gb_ref[...], wb_ref[:, 128:]).astype(BF)
    lane = lanes_of((padded, 128))
    low = lane < 64
    field = lane & 31
    amounts = amount_ref[...]
    kept = (lane >= 64) & (field < 14)

    def window(w, carry):
        rows = pl.ds(pl.multiple_of(w * padded, 16), padded)
        do = do_ref[rows, :].astype(F32)
        out = out_ref[0, rows, :].astype(F32)
        product = do * out
        grads = [pltpu.roll(do[:, :128], 64, 1), do[:, 128:], pltpu.roll(do[:, 128:], 64, 1)]
        sums = [
            jnp.sum(jnp.where(low, 0.0, product[:, :128]), -1, keepdims=True),
            jnp.sum(jnp.where(low, product[:, 128:], 0.0), -1, keepdims=True),
            jnp.sum(jnp.where(low, 0.0, product[:, 128:]), -1, keepdims=True),
        ]
        gq, gk, gv = [], [], []
        for head in range(3):
            delta = -sums[head]
            first = delta.astype(BF).astype(F32)
            grad_out = jnp.where(low, grads[head], jnp.where(lane == 64, first, jnp.where(lane == 65, delta - first, 0.0))).astype(BF)
            query, key, value = query_ref[0, head, rows, :], key_ref[0, head, w], value_ref[0, head, w]
            prob = jnp.exp(nt(query, key))
            grad_scores = (prob * nt(grad_out, value)).astype(BF)
            gv.append(tn(prob.astype(BF), grad_out)[:padded])
            gk.append(tn(grad_scores, query)[:padded])
            both = nn(grad_scores, key)
            back = shift_lanes(jnp.where(kept, both, 0.0), amounts, False)
            high = back.astype(BF).astype(F32)
            pack = jnp.where(low, pltpu.roll(back - high, 64, 1), high).astype(BF)
            spread_ref[head, rows, :] = pack
            gq.append(both * 0.125 + nn(pack, table_ref[...]))
        gqk_ref[rows, :128] = jnp.where(low, gq[0], pltpu.roll(gq[1], 64, 1)).astype(BF)
        gqk_ref[rows, 128:256] = jnp.where(low, gq[2], pltpu.roll(gk[0], 64, 1)).astype(BF)
        gqk_ref[rows, 256:] = jnp.where(low, gk[1], pltpu.roll(gk[2], 64, 1)).astype(BF)
        gv_ref[rows, :128] = jnp.where(low, gv[0], pltpu.roll(gv[1], 64, 1)).astype(BF)
        gv_ref[rows, 128:] = jnp.where(low, gv[2], 0.0).astype(BF)
        return carry

    lax.fori_loop(0, windows, window, 0)
    for head in range(3):
        grel_ref[...] += tn(spread_ref[head], query_ref[0, head])
    gqk, gv = gqk_ref[...], gv_ref[...]
    gbias_ref[0, :, :384] = jnp.sum(gqk.astype(F32), 0, keepdims=True)
    gbias_ref[0, :, 384:] = jnp.sum(gv.astype(F32), 0, keepdims=True)
    dh_ref[...] += nt(gqk, wa_ref[...]) + nt(gv, wb_ref[:, :256])
    h1t = h1t_ref[...]
    grad_ref[0, 0] = nn(h1t, gqk).astype(grad_ref.dtype)
    one, two = nn(h1t, gv), nn(gbt_ref[...], out_ref[0])
    grad_ref[0, 1, :, :128] = one[:, :128].astype(grad_ref.dtype)
    grad_ref[0, 1, :, 128:256] = (one[:, 128:] + two[:, :128]).astype(grad_ref.dtype)
    grad_ref[0, 1, :, 256:] = two[:, 128:].astype(grad_ref.dtype)

    @pl.when(step == last)
    def _():
        normed, inverse = normed_of(x_ref[...].astype(F32))
        dh = dh_ref[...]
        grad_x_ref[...] = (gx1_ref[...] + norm_back(dh, normed, inverse, gain_ref[...])).astype(BF)
        small_ref[1:2, :] = jnp.sum(dh * normed, 0, keepdims=True)
        small_ref[2:3, :] = jnp.sum(dh, 0, keepdims=True)
        small_ref[3:8, :] = jnp.zeros_like(small_ref[3:8, :])


def whole(shape):
    return pl.BlockSpec(shape, lambda *index: (0,) * len(shape))


def once(shape):
    return pl.BlockSpec(shape, lambda *index: (0,) * len(shape), pipeline_mode=pl.Buffered(1))


def shards(
    block_input, cotangent, pad_mask, slot_window, qkv_w, proj_w, fc1_w, fc2_w,
    norm1_gain, norm1_bias, q_bias, v_bias, rel_h, rel_w, proj_bias,
    norm2_gain, norm2_bias, fc1_bias, fc2_bias,
):
    part = lax.axis_index("tensor")
    count_dp, count_t = lax.axis_size("dp"), lax.axis_size("tensor")
    length = pad_mask.shape[1]
    local_rows, width = block_input.shape
    windows = local_rows // length
    size = rel_h.shape[0] // 2 + 1
    padded = -(-length // 16) * 16
    keys = -(-length // 128) * 128
    rows = windows * padded
    strip = width // count_dp

    mine = lax.dynamic_slice_in_dim(slot_window, part * windows, windows)
    alive = mine >= 0
    valid = jnp.take(pad_mask, jnp.maximum(mine, 0), axis=0)
    usable = (valid > 0) & alive[:, None]
    usable = jnp.pad(usable, ((0, 0), (0, padded - length)))
    mask = jnp.where(usable, 0.0, NEGATIVE).reshape(rows, 1)
    live = jnp.pad(jnp.broadcast_to(alive.astype(F32)[:, None], (windows, length)), ((0, 0), (0, padded - length)))
    live = jnp.broadcast_to(live.reshape(rows, 1), (rows, 128))

    def pad_rows(values):
        return jnp.pad(values.reshape(windows, length, width), ((0, 0), (0, padded - length), (0, 0))).reshape(rows, width)

    def cut_rows(values):
        return values.reshape(windows, padded, width)[:, :length].reshape(local_rows, width)

    x = pad_rows(block_input)
    gy = pad_rows(
        jnp.where(alive[:, None, None], cotangent.reshape(windows, length, width), jnp.zeros((), BF)).reshape(local_rows, width)
    )

    place = np.arange(padded)
    row_of, col_of = place // size, place % size
    inside = place < length
    amount = np.zeros((padded, 128), np.int32)
    amount[:, :] = np.where(
        (np.arange(128) % 64 < 32)[None, :], (size - 1 - row_of)[:, None], (size - 1 - col_of)[:, None]
    ) * inside[:, None]
    amount = jnp.asarray(amount)
    feat = np.zeros((padded, 128), np.float32)
    for a in range(size):
        for base, pos in ((64, row_of), (96, col_of)):
            feat[:, base + a] = (pos == a) & inside
            feat[:, base + 16 + a] = (pos == a) & inside
    feat[:, [78, 94, 95]] = 1.0
    key_feat = jnp.where(np.arange(128)[None, :] == 79, mask, jnp.tile(jnp.asarray(feat), (windows, 1))).astype(BF)

    span = rel_h.shape[0]
    table = jnp.zeros((64, HD), F32).at[:span].set(rel_h[::-1]).at[32 : 32 + span].set(rel_w[::-1])
    table_hi = table.astype(BF)
    table_lo = (table - table_hi.astype(F32)).astype(BF)

    def block_diag(piece):
        big = jnp.zeros((256, 384), BF)
        for head in range(3):
            big = big.at[head * 64 : head * 64 + 64, head * 128 + 64 : head * 128 + 128].set(piece.T)
        return big

    spread_table = jnp.stack([block_diag(table_hi), block_diag(table_lo)])
    back_table = jnp.zeros((128, 128), BF).at[:64, :64].set(table_hi).at[64:, :64].set(table_hi)

    q_w, k_w, v_w = qkv_w[0], qkv_w[1], qkv_w[2]
    shard = jnp.stack(
        [
            jnp.concatenate([q_w, k_w], 1),
            jnp.concatenate([v_w, proj_w.T], 1),
            fc1_w[:, :384],
            fc1_w[:, 384:],
            fc2_w.T[:, :384],
            fc2_w.T[:, 384:],
        ]
    )
    gathered_a = lax.all_gather(shard[:2], AXES, axis=0, tiled=False).reshape(count_dp, count_t, 2, strip, 384)
    gathered_m = lax.all_gather(shard[2:], AXES, axis=0, tiled=False).reshape(count_dp, count_t, 4, strip, 384)
    w_att = gathered_a.transpose(1, 2, 0, 3, 4).reshape(count_t, 2, width, 384)
    w_mlp = gathered_m.transpose(2, 1, 0, 3, 4).reshape(2, 2, count_t, width, 384).transpose(0, 2, 1, 3, 4)
    w_up = w_mlp[0].reshape(count_t * 2, width, 384)
    w_down = w_mlp[1].reshape(count_t * 2, width, 384)

    row = lambda v: v.reshape(1, -1)
    bias_att = jnp.zeros((count_t, 1, 640), F32)
    bias_att = bias_att.at[:, 0, :192].set(q_bias.reshape(count_t, 192)).at[:, 0, 384:576].set(v_bias.reshape(count_t, 192))
    params = pltpu.CompilerParams(dimension_semantics=("arbitrary",), vmem_limit_bytes=VMEM_LIMIT)

    query, key, value, out, attn = pl.pallas_call(
        partial(attend_kernel, windows=windows, padded=padded, keys=keys),
        grid=(count_t,),
        in_specs=[
            once((rows, width)),
            pl.BlockSpec((None, None, width, 384), lambda t: (t, 0, 0, 0)),
            pl.BlockSpec((None, None, width, 384), lambda t: (t, 1, 0, 0)),
            once((1, width)), once((1, width)),
            pl.BlockSpec((None, 1, 640), lambda t: (t, 0, 0)),
            once((2, 256, 384)), once((rows, 128)), once((padded, 128)),
        ],
        out_specs=[
            pl.BlockSpec((1, 3, rows, 128), lambda t: (t, 0, 0, 0)),
            pl.BlockSpec((1, 3, windows, keys, 128), lambda t: (t, 0, 0, 0, 0)),
            pl.BlockSpec((1, 3, windows, keys, 128), lambda t: (t, 0, 0, 0, 0)),
            pl.BlockSpec((1, rows, 256), lambda t: (t, 0, 0)),
            whole((rows, width)),
        ],
        out_shape=[
            jax.ShapeDtypeStruct((count_t, 3, rows, 128), BF),
            jax.ShapeDtypeStruct((count_t, 3, windows, keys, 128), BF),
            jax.ShapeDtypeStruct((count_t, 3, windows, keys, 128), BF),
            jax.ShapeDtypeStruct((count_t, rows, 256), BF),
            jax.ShapeDtypeStruct((rows, width), F32),
        ],
        scratch_shapes=[pltpu.VMEM((rows, width), BF), pltpu.VMEM((rows, 384), BF), pltpu.VMEM((rows, 256), BF)],
        compiler_params=params,
        name="attend",
    )(x, w_att, w_att, row(norm1_gain), row(norm1_bias), bias_att, spread_table, key_feat, amount)

    tiles = 2 * count_t
    result, gx1, grad_up, grad_down, gbias_up, small2 = pl.pallas_call(
        mlp_kernel,
        grid=(tiles,),
        in_specs=[
            once((rows, width)), once((rows, width)), once((rows, width)), once((rows, 128)),
            pl.BlockSpec((None, width, 384), lambda j: (j, 0, 0)),
            pl.BlockSpec((None, width, 384), lambda j: (j, 0, 0)),
            pl.BlockSpec((1, 1, 384), lambda j: (j, 0, 0)),
            once((1, width)), once((1, width)), once((1, width)), once((1, width)),
        ],
        out_specs=[
            whole((rows, width)), whole((rows, width)),
            pl.BlockSpec((1, width, 384), lambda j: (j, 0, 0)),
            pl.BlockSpec((1, width, 384), lambda j: (j, 0, 0)),
            pl.BlockSpec((1, 1, 384), lambda j: (j, 0, 0)),
            whole((8, width)),
        ],
        out_shape=[
            jax.ShapeDtypeStruct((rows, width), BF),
            jax.ShapeDtypeStruct((rows, width), F32),
            jax.ShapeDtypeStruct((tiles, width, 384), BF),
            jax.ShapeDtypeStruct((tiles, width, 384), BF),
            jax.ShapeDtypeStruct((tiles, 1, 384), F32),
            jax.ShapeDtypeStruct((8, width), F32),
        ],
        scratch_shapes=[
            pltpu.VMEM((rows, width), F32), pltpu.VMEM((rows, width), BF),
            pltpu.VMEM((width, rows), BF), pltpu.VMEM((width, rows), BF),
            pltpu.VMEM((rows, width), F32), pltpu.VMEM((rows, width), F32),
        ],
        compiler_params=params,
        name="mlp",
    )(
        x, attn, gy, live, w_up, w_down, fc1_bias.reshape(tiles, 1, 384),
        row(norm2_gain), row(norm2_bias), row(proj_bias), row(fc2_bias),
    )

    grad_x, grad_att, small1, gbias_att, grel = pl.pallas_call(
        partial(attend_back_kernel, windows=windows, padded=padded, keys=keys),
        grid=(count_t,),
        in_specs=[
            once((rows, width)), once((rows, width)),
            pl.BlockSpec((None, None, width, 384), lambda t: (t, 0, 0, 0)),
            pl.BlockSpec((None, None, width, 384), lambda t: (t, 1, 0, 0)),
            once((1, width)), once((1, width)), once((128, 128)), once((padded, 128)),
            pl.BlockSpec((1, 3, rows, 128), lambda t: (t, 0, 0, 0)),
            pl.BlockSpec((1, 3, windows, keys, 128), lambda t: (t, 0, 0, 0, 0)),
            pl.BlockSpec((1, 3, windows, keys, 128), lambda t: (t, 0, 0, 0, 0)),
            pl.BlockSpec((1, rows, 256), lambda t: (t, 0, 0)),
        ],
        out_specs=[
            whole((rows, width)),
            pl.BlockSpec((1, 2, width, 384), lambda t: (t, 0, 0, 0)),
            whole((8, width)),
            pl.BlockSpec((1, 1, 640), lambda t: (t, 0, 0)),
            whole((128, 128)),
        ],
        out_shape=[
            jax.ShapeDtypeStruct((rows, width), BF),
            jax.ShapeDtypeStruct((count_t, 2, width, 384), BF),
            jax.ShapeDtypeStruct((8, width), F32),
            jax.ShapeDtypeStruct((count_t, 1, 640), F32),
            jax.ShapeDtypeStruct((128, 128), F32),
        ],
        scratch_shapes=[
            pltpu.VMEM((width, rows), BF), pltpu.VMEM((width, rows), BF), pltpu.VMEM((rows, width), BF),
            pltpu.VMEM((rows, width), F32), pltpu.VMEM((rows, 256), BF),
            pltpu.VMEM((rows, 384), BF), pltpu.VMEM((rows, 256), BF), pltpu.VMEM((3, rows, 128), BF),
        ],
        compiler_params=params,
        name="attend_back",
    )(
        x, gx1, w_att, w_att, row(norm1_gain), row(norm1_bias), back_table, amount, query, key, value, out
    )

    grad_up = grad_up.reshape(count_t, 2, count_dp, strip, 384).transpose(2, 0, 1, 3, 4)
    grad_down = grad_down.reshape(count_t, 2, count_dp, strip, 384).transpose(2, 0, 1, 3, 4)
    grad_mlp = jnp.concatenate([grad_up, grad_down], 2).reshape(count_dp * count_t, 4, strip, 384)
    grad_att = grad_att.reshape(count_t, 2, count_dp, strip, 384).transpose(2, 0, 1, 3, 4)
    grad_att = grad_att.reshape(count_dp * count_t, 2, strip, 384)
    sum_mlp = lax.psum_scatter(grad_mlp, AXES, scatter_dimension=0, tiled=False).astype(F32)
    sum_att = lax.psum_scatter(grad_att, AXES, scatter_dimension=0, tiled=False).astype(F32)
    grad_rel = 8.0 * (grel[64:, :64])
    small = lax.psum((small1[:3], small2[:3], gbias_att, gbias_up, grad_rel), AXES)
    small1, small2, gbias_att, gbias_up, grad_rel = small
    head_q, head_k = sum_att[0, :, :192], sum_att[0, :, 192:]
    head_v, head_p = sum_att[1, :, :192], sum_att[1, :, 192:]
    return (
        cut_rows(result),
        cut_rows(grad_x),
        jnp.stack([head_q, head_k, head_v]),
        head_p.T,
        jnp.concatenate([sum_mlp[0], sum_mlp[1]], 1),
        jnp.concatenate([sum_mlp[2], sum_mlp[3]], 1).T,
        small1[1],
        small1[2],
        gbias_att[:, 0, :192].reshape(-1),
        gbias_att[:, 0, 384:576].reshape(-1),
        grad_rel[:span][::-1],
        grad_rel[32 : 32 + span][::-1],
        small1[0],
        small2[0],
        small2[1],
        gbias_up.reshape(-1),
        small2[2],
    )


def solution(mesh):
    return jax.shard_map(
        shards,
        mesh=mesh,
        in_specs=(
            P(AXES, None), P(AXES, None), P(), P("dp"),
            P(None, "dp", "tensor"), P("tensor", "dp"), P("dp", "tensor"), P("tensor", "dp"),
        )
        + (P(),) * 11,
        out_specs=(
            P(AXES, None), P(AXES, None),
            P(None, "dp", "tensor"), P("tensor", "dp"), P("dp", "tensor"), P("tensor", "dp"),
        )
        + (P(),) * 11,
        check_vma=False,
    )
```

```python
from functools import partial

import jax
import jax.numpy as jnp
import numpy as np
from jax import lax
from jax.experimental import pallas as pl
from jax.experimental.pallas import tpu as pltpu
from jax.sharding import PartitionSpec as P

HD = 64
EPSILON = 1e-06
NEGATIVE = -1e30
F32, BF = jnp.float32, jnp.bfloat16
AXES = ("dp", "tensor")
VMEM_LIMIT = 60 * 1024 * 1024
MLP_PARTS = 1
MLP_BEGIN = (11,)
MLP_SLOTS = tuple(int(i * 2.8) for i in range(15))


def nn(left, right):
    return lax.dot_general(left, right, (((1,), (0,)), ((), ())), preferred_element_type=F32)


def nt(left, right):
    return lax.dot_general(left, right, (((1,), (1,)), ((), ())), preferred_element_type=F32)


def tn(left, right):
    return lax.dot_general(left, right, (((0,), (0,)), ((), ())), preferred_element_type=F32)


def normed_of(values):
    center = values - jnp.mean(values, -1, keepdims=True)
    inverse = lax.rsqrt(jnp.mean(center * center, -1, keepdims=True) + EPSILON)
    return center * inverse, inverse


def norm_back(grad, normed, inverse, gain):
    scaled = grad * gain
    inner = (
        scaled
        - jnp.mean(scaled, -1, keepdims=True)
        - normed * jnp.mean(scaled * normed, -1, keepdims=True)
    )
    return inverse * inner


def spread_rows(source_ref, target_ref, windows, padded, scale=None):
    length = source_ref.shape[0] // windows
    for w in range(windows):
        tail = w * padded + length // 16 * 16
        target_ref[tail : w * padded + padded, :] = jnp.zeros((w * padded + padded - tail, target_ref.shape[1]), target_ref.dtype)
        values = source_ref[w * length : w * length + length, :]
        if scale is not None:
            values = jnp.where(scale(w) > 0.5, values.astype(F32), 0.0).astype(values.dtype)
        target_ref[w * padded : w * padded + length, :] = values


def row(ref):
    return ref[...].reshape(1, -1)


def flat(values):
    return values.reshape(-1, values.shape[-1])


def lanes_of(shape):
    return lax.broadcasted_iota(jnp.int32, shape, 1)


def of_slot(values, slot):
    return jnp.sum(jnp.where(lanes_of(values.shape) == slot, values, 0.0), -1, keepdims=True)


def alive_of(slots_ref, slot):
    return of_slot(jnp.where(slots_ref[...] >= 0, 1.0, 0.0), slot)


def shift_lanes(values, amounts, left):
    for bit in (1, 2, 4, 8):
        moved = pltpu.roll(values, 128 - bit if left else bit, 1)
        values = jnp.where((amounts & bit) != 0, moved, values)
    return values


MESH = pl.DeviceIdType.MESH


class Place:
    def __init__(self, height):
        self.height = height
        self.dp, self.tensor = lax.axis_index("dp"), lax.axis_index("tensor")
        self.z, self.y = lax.div(self.dp, 2), lax.rem(self.dp, 2)
        self.x, self.c = lax.div(self.tensor, 2), lax.rem(self.tensor, 2)

    def plane(self, colour, a, b):
        return lax.rem(self.y + (1 - colour) * b + colour * a, 2), lax.rem(self.x + (1 - colour) * a + colour * b, 2)

    def shard(self, colour, a, b, z):
        y, x = self.plane(colour, a, b)
        return z * 2 + y, x * 2 + colour

    def near(self, k):
        upper = lax.div(self.z, self.height // 2)
        zz = self.z + upper * (self.height - 1 - 2 * self.z)
        q = (zz, 1 - zz, 2, 3)[k]
        return q + upper * (self.height - 1 - 2 * q)

    def peer(self, kind):
        if kind == "core":
            return self.dp, self.x * 2 + 1 - self.c
        if kind in ("z1", "z2", "z3"):
            return self.near(int(kind[1])) * 2 + self.y, self.tensor
        if kind == "up":
            return self.dp + 2, self.tensor
        if kind == "down":
            return self.dp - 2, self.tensor
        if kind == "y":
            return self.z * 2 + 1 - self.y, self.tensor
        if kind == "x":
            return self.dp, (1 - self.x) * 2 + self.c
        if kind == "pair":
            return (self.z + 1 - 2 * lax.rem(self.z, 2)) * 2 + self.y, self.tensor
        if kind == "half":
            return lax.rem(self.z + 2, 4) * 2 + self.y, self.tensor
        return self.shard(self.c, int(kind == "far"), int(kind == "near"), self.z)

    def has(self, kind):
        if kind == "up":
            return self.z < self.height - 1
        if kind == "down":
            return self.z > 0
        return None

    def greet(self):
        barrier = pltpu.get_barrier_semaphore()
        for kind in ("core", "near", "far", "z1", "z2", "z3"):
            pl.semaphore_signal(barrier, inc=1, device_id=self.peer(kind), device_id_type=MESH)
        pl.semaphore_wait(barrier, 6)


def under(condition, action):
    if condition is None:
        action()
    else:
        pl.when(condition)(action)


def both(one, two):
    return two if one is None else one if two is None else jnp.logical_and(one, two)


class Gather:
    SENDS = 36

    def __init__(self, at, own_ref, all_ref, send_sem, recv_sem, first=0, count=None):
        self.at, self.own_ref = at, own_ref
        self.all_ref = all_ref if count is None else all_ref.at[:, :, first : first + count]
        self.send_sem, self.recv_sem = send_sem, recv_sem
        z = [lambda k=k: self.step(("z", k)) for k in range(4)]
        near = [lambda k=k: self.step(("near", k)) for k in range(4)]
        far = [[lambda b=b, k=k: self.step(("far", b, k)) for k in range(4)] for b in range(2)]
        self.steps = [
            near[0], z[1], far[0][0], near[1], far[1][0], z[2], far[0][1],
            near[2], far[1][1], z[3], far[0][2], near[3], far[1][2], far[0][3], far[1][3],
        ]
        slot = 0
        self.slots = {}
        for key in [("z", k) for k in range(4)] + [("near", k) for k in range(4)] + [("far", b, k) for b in range(2) for k in range(4)]:
            self.slots[key] = slot
            slot += len(self.kinds(key))

    def kinds(self, key):
        return {"z": ("up", "down", "near", "far", "core"), "near": ("far", "core"), "far": ("core",)}[key[0]]

    def shard(self, key):
        at = self.at
        if key[0] == "z":
            return at.shard(at.c, 0, 0, at.near(key[1]))
        if key[0] == "near":
            return at.shard(at.c, 0, 1, at.near(key[1]))
        return at.shard(at.c, 1, key[1], at.near(key[2]))

    def copy(self, source, shard, kind, slot):
        dp, tensor = shard
        return pltpu.make_async_remote_copy(
            src_ref=source, dst_ref=self.all_ref.at[dp, tensor], send_sem=self.send_sem.at[slot],
            recv_sem=self.recv_sem.at[dp * 4 + tensor], device_id=self.at.peer(kind), device_id_type=MESH)

    def sends(self, key):
        shard = self.shard(key)
        source = self.own_ref if key == ("z", 0) else self.all_ref.at[shard[0], shard[1]]
        away = self.at.near(key[1]) - self.at.z if key[0] == "z" else 0
        sends = []
        for i, kind in enumerate(self.kinds(key)):
            condition = self.at.has(kind)
            if kind in ("up", "down"):
                condition = jnp.logical_and(condition, away <= 0 if kind == "up" else away >= 0)
            sends.append((condition, self.copy(source, shard, kind, self.slots[key] + i)))
        return sends

    def take(self, shard):
        self.copy(self.all_ref.at[shard[0], shard[1]], shard, "core", 0).wait_recv()

    def begin(self):
        for condition, copy in self.sends(("z", 0)):
            under(condition, copy.start)

    def step(self, key):
        self.take(self.shard(key))
        for condition, copy in self.sends(key):
            under(condition, copy.start)

    def arrive(self):
        at = self.at
        for a in range(2):
            for b in range(2):
                for k in range(4):
                    self.take(at.shard(1 - at.c, a, b, at.near(k)))

    def finish(self):
        for key in self.slots:
            for condition, copy in self.sends(key):
                under(condition, copy.wait_send)


def gather_scratch():
    return [pltpu.SemaphoreType.DMA((Gather.SENDS,)), pltpu.SemaphoreType.DMA((32,))]


class Scatter:
    def __init__(self, all_ref, own_ref, held, core_in, far_in, near_in, up_in, down_in, sems, height=4):
        self.all_ref, self.own_ref, self.held, self.core_in = all_ref, own_ref, held, core_in
        self.far_in, self.near_in, self.up_in, self.down_in, self.sems = far_in, near_in, up_in, down_in, sems
        self.at = Place(height)
        core = {(a, b): (lambda a=a, b=b: self.from_core(a, b)) for a in range(2) for b in range(2)}
        far = [[lambda b=b, k=k: self.from_far(b, k) for k in range(4)] for b in range(2)]
        near = [lambda k=k: self.from_near(k) for k in range(4)]
        line = [lambda k=k: self.from_line(k) for k in range(4)]
        self.steps = [
            [self.begin], [core[1, 1], core[1, 0]], [core[0, 1], core[0, 0]], [far[1][3]], [far[1][2]],
            [far[1][1], near[3]], [far[1][0], near[2]], [far[0][3], near[1]], [far[0][2], line[3]], [near[0], far[0][1]],
            [line[2]], [far[0][0]], [line[1]], [], [],
        ]
        self.last = line[0]

    def remote(self, source, target, name, index, kind):
        send, recv = self.sems[name]
        return pltpu.make_async_remote_copy(
            src_ref=source, dst_ref=target, send_sem=send.at[index], recv_sem=recv.at[index],
            device_id=self.at.peer(kind), device_id_type=MESH)

    def core_copy(self, a, b):
        at = self.at
        y, x = at.plane(1 - at.c, a, b)
        source = self.all_ref.at[:, y, x * 2 + 1 - at.c]
        return self.remote(source, self.core_in.at[a, b], "core", a * 2 + b, "core")

    def local_copy(self, a, b):
        at = self.at
        y, x = at.plane(at.c, a, b)
        return pltpu.make_async_copy(self.all_ref.at[:, y, x * 2 + at.c], self.held.at[a, b], self.sems["local"].at[a * 2 + b])

    def far_copy(self, b, z):
        return self.remote(self.held.at[1, b, z], self.far_in.at[b, z], "far", b * 4 + z, "far")

    def near_copy(self, z):
        return self.remote(self.held.at[0, 1, z], self.near_in.at[z], "near", z, "near")

    def down_copy(self, z):
        return self.remote(self.held.at[0, 0, z], self.down_in.at[z], "down", z, "down")

    def up_copy(self, z):
        return self.remote(self.held.at[0, 0, z], self.up_in.at[z], "up", z, "up")

    def begin(self):
        self.at.greet()
        for a in (1, 0):
            for b in (1, 0):
                self.core_copy(a, b).start()
                self.local_copy(a, b).start()

    def from_core(self, a, b):
        self.local_copy(a, b).wait()
        self.core_copy(a, b).wait_recv()
        for z in range(4):
            self.held[a, b, z] = self.held[a, b, z] + self.core_in[a, b, z]
        if a == 1:
            for k in (3, 2, 1, 0):
                self.far_copy(b, self.at.near(k)).start()

    def from_far(self, b, k):
        z = self.at.near(k)
        self.far_copy(b, z).wait_recv()
        self.held[0, b, z] = self.held[0, b, z] + self.far_in[b, z]
        if b == 1:
            self.near_copy(z).start()

    def from_near(self, k):
        z = self.at.near(k)
        self.near_copy(z).wait_recv()
        self.held[0, 0, z] = self.held[0, 0, z] + self.near_in[z]

    def from_line(self, k):
        at = self.at
        if k > 0:
            z = at.near(k)

            def downward():
                def add():
                    self.down_copy(z).wait_recv()
                    self.held[0, 0, z] = self.held[0, 0, z] + self.down_in[z]

                under(at.has("up"), add)
                self.down_copy(z).start()

            def upward():
                def add():
                    self.up_copy(z).wait_recv()
                    self.held[0, 0, z] = self.held[0, 0, z] + self.up_in[z]

                under(at.has("down"), add)
                self.up_copy(z).start()

            pl.when(z < at.z)(downward)
            pl.when(z > at.z)(upward)
            return
        self.own_ref[...] = self.held[0, 0, at.z].astype(F32)

        def add_down():
            self.down_copy(at.z).wait_recv()
            self.own_ref[...] += self.down_in[at.z].astype(F32)

        def add_up():
            self.up_copy(at.z).wait_recv()
            self.own_ref[...] += self.up_in[at.z].astype(F32)

        under(at.has("up"), add_down)
        under(at.has("down"), add_up)

    def finish(self):
        at = self.at
        self.last()
        for a in range(2):
            for b in range(2):
                self.core_copy(a, b).wait_send()
        for b in range(2):
            for z in range(4):
                self.far_copy(b, z).wait_send()
        for z in range(4):
            self.near_copy(z).wait_send()
            pl.when(z < at.z)(lambda: self.down_copy(z).wait_send())
            pl.when(z > at.z)(lambda: self.up_copy(z).wait_send())


def scatter_scratch(pieces, strip, columns):
    block = (pieces, strip, columns)
    shapes = [(2, 2, 4), (2, 2, 4), (2, 4), (4,), (4,), (4,)]
    sems = [4, 4, 8, 8, 4, 4, 4, 4, 4, 4, 4]
    return [pltpu.VMEM(lead + block, BF) for lead in shapes] + [pltpu.SemaphoreType.DMA((n,)) for n in sems]


SCATTER_REFS = 17


def make_scatter(all_ref, own_ref, refs):
    held, core_in, far_in, near_in, up_in, down_in = refs[:6]
    core_s, core_r, far_s, far_r, near_s, near_r, up_s, up_r, down_s, down_r, local = refs[6:]
    sems = {
        "core": (core_s, core_r), "far": (far_s, far_r), "near": (near_s, near_r),
        "up": (up_s, up_r), "down": (down_s, down_r), "local": local,
    }
    return Scatter(all_ref, own_ref, held, core_in, far_in, near_in, up_in, down_in, sems)


def packed(refs):
    small1_ref, small2_ref, gbias_att_ref, gbias_up_ref = refs
    places = []
    for ref, rows in ((small1_ref, range(3)), (small2_ref, range(3))):
        places += [(ref, (row, lane)) for row in rows for lane in range(0, ref.shape[1], 128)]
    for ref in (gbias_att_ref, gbias_up_ref):
        places += [(ref, (row, 0, lane)) for row in range(ref.shape[0]) for lane in range(0, ref.shape[2], 128)]
    return places


def reduce_kernel(
    all_ref, small1_ref, small2_ref, gbias_att_ref, gbias_up_ref, grel_ref,
    own_ref, total_ref, small_ref, small_in, small_send, small_recv, *refs,
):
    scatter = make_scatter(all_ref, own_ref, refs)
    at = scatter.at
    rounds = ("core", "y", "x", "pair", "half")

    def exchange(index):
        return pltpu.make_async_remote_copy(
            src_ref=small_ref if index == 0 else small_in.at[5 + index], dst_ref=small_in.at[index],
            send_sem=small_send.at[index], recv_sem=small_recv.at[index],
            device_id=at.peer(rounds[index]), device_id_type=MESH)

    def fold(index):
        exchange(index).wait_recv()
        own = small_ref[...] if index == 0 else small_in[5 + index]
        if index < 4:
            small_in[6 + index] = own + small_in[index]
            exchange(index + 1).start()
        else:
            total_ref[...] = own + small_in[index]

    scatter.begin()
    for row, (ref, index) in enumerate(packed((small1_ref, small2_ref, gbias_att_ref, gbias_up_ref))):
        if len(index) == 2:
            small_ref[row : row + 1, :] = ref[index[0] : index[0] + 1, index[1] : index[1] + 128]
        else:
            small_ref[row : row + 1, :] = ref[index[0], 0:1, index[2] : index[2] + 128]
    small_ref[small_ref.shape[0] - 64 :, :] = grel_ref[64:, :]
    exchange(0).start()
    for step in scatter.steps[1]:
        step()
    fold(0)
    for step in scatter.steps[2]:
        step()
    fold(1)
    for number, steps in enumerate(scatter.steps[3:]):
        for step in steps:
            step()
        if number in (0, 2, 4):
            fold(2 + number // 2)
    scatter.finish()
    for index in range(5):
        exchange(index).wait_send()


def attend_kernel(*refs, windows, padded, keys, size, linked):
    step = pl.program_id(0)
    duties = {}
    refs = list(refs)
    if linked:
        own_ref, att_ref, mlp_ref, w_ref, keep_sem = refs[10], refs[17], refs[18], refs[25], refs[-1]
        at = Place(4)
        att = Gather(at, own_ref.at[:2], w_ref, *refs[26:28])
        share = 4 // MLP_PARTS
        mlp = [
            Gather(at, own_ref.at[2 + i * share : 2 + i * share + share], mlp_ref, *refs[28 + 2 * i : 30 + 2 * i], i * share, share)
            for i in range(MLP_PARTS)
        ]
        todo = [act for acts in zip(*[part.steps for part in mlp]) for act in acts]
        mine = pltpu.make_async_copy(own_ref.at[2:], mlp_ref.at[at.dp, at.tensor], keep_sem.at[0])
        keep = pltpu.make_async_copy(w_ref, att_ref, keep_sem.at[1])
        refs = refs[:1] + [w_ref] + refs[1:10] + refs[11:17] + refs[19:25]

        @pl.when(step == 0)
        def _():
            at.greet()
            att.begin()
            w_ref[at.dp, at.tensor] = own_ref[:2]
            mine.start()

        duties = {slot: [todo[i] for i in range(len(todo)) if MLP_SLOTS[i] == slot] for slot in MLP_SLOTS}
    (
        raw_ref, w_ref, gain_ref, shift_ref, query_bias_ref, value_bias_ref, rel_ref, slots_ref, pad_ref, feat_ref, amount_ref,
        query_ref, key_ref, value_ref, out_ref, acc_ref, x_ref,
        h1_ref, qk_ref, vv_ref, table_ref, key_feat_ref, bias_ref,
    ) = refs

    @pl.when(step == 0)
    def _():
        length = pad_ref.shape[0]
        spread_rows(raw_ref, x_ref, windows, padded)
        normed, _ = normed_of(x_ref[...].astype(F32))
        h1_ref[...] = (normed * row(gain_ref) + row(shift_ref)).astype(BF)
        acc_ref[...] = jnp.zeros_like(acc_ref)

        span = 2 * size - 1
        place = lax.broadcasted_iota(jnp.int32, (64, 128), 0)
        lane = lanes_of((64, 128))
        wanted = jnp.where(place < span, 64 + span - 1 - place, jnp.where(place < 2 * span, 96 + 2 * span - 1 - place, -1))
        chosen = jnp.where(lane == wanted, 1.0, 0.0).astype(BF)
        rel = rel_ref[...]
        high = rel.astype(BF)
        rest = (rel - high.astype(F32)).astype(BF)
        table_ref[...] = jnp.zeros_like(table_ref)
        for number, piece in enumerate((high, rest)):
            turned = tn(piece, chosen)[:64].astype(BF)
            for head in range(3):
                table_ref[number, head * 64 : head * 64 + 64, head * 128 : head * 128 + 128] = turned

        part = lax.axis_index("tensor")
        count = pad_ref.shape[1]
        picked = jnp.where(lax.broadcasted_iota(jnp.int32, (count, 128), 0) == slots_ref[...], 1.0, 0.0).astype(BF)
        usable = nn(pad_ref[...].astype(F32).astype(BF), picked)
        for w in range(windows):
            mask = jnp.where(of_slot(usable, part * windows + w) > 0.5, 0.0, NEGATIVE)
            start = w * padded
            key_feat_ref[start : start + padded, :] = feat_ref[...]
            key_feat_ref[start : start + length, :] = jnp.where(
                lanes_of((length, 128)) == 79, mask, feat_ref[:length, :].astype(F32)).astype(BF)
        bias_ref[...] = jnp.zeros_like(bias_ref)
        for t in range(bias_ref.shape[0]):
            bias_ref[t, 0:1, 0:192] = row(query_bias_ref)[:, t * 192 : t * 192 + 192]
            bias_ref[t, 0:1, 384:576] = row(value_bias_ref)[:, t * 192 : t * 192 + 192]

        if linked:
            for number, act in enumerate(att.steps):
                act()
                if number in MLP_BEGIN:
                    mlp[MLP_BEGIN.index(number)].begin()
            att.arrive()
            keep.start()

    h1 = h1_ref[...]
    chunk = step if linked else 0
    wa, wb = flat(w_ref[:, chunk, 0]), flat(w_ref[:, chunk, 1])
    qk_ref[...] = (nn(h1, wa) + bias_ref[step, 0:1, :384]).astype(BF)
    vv_ref[...] = (nn(h1, wb[:, :256]) + bias_ref[step, 0:1, 384:640]).astype(BF)
    lane = lanes_of((padded, 128))
    low = lane < 64
    field = lane & 31
    amounts = amount_ref[...]
    pad_lane = lanes_of((keys - padded, 128))
    pad_key = jnp.where(pad_lane == 79, NEGATIVE, 0.0).astype(BF)

    def window(w, carry):
        rows = pl.ds(pl.multiple_of(w * padded, 16), padded)
        qk = qk_ref[rows, :]
        vv = vv_ref[rows, :]
        spread = nn(qk[:, :256], table_ref[0]) + nn(qk[:, :256], table_ref[1])
        wide = qk.astype(F32)
        wide_v = vv.astype(F32)
        parts = [wide[:, :128], wide[:, 128:256], wide[:, 256:384]]
        turned = [pltpu.roll(part, 64, 1) for part in parts]
        queries = [parts[0], turned[0], parts[1]]
        keys_low = [turned[1], parts[2], turned[2]]
        values = [wide_v[:, :128], pltpu.roll(wide_v[:, :128], 64, 1), wide_v[:, 128:256]]
        key_feat = key_feat_ref[rows, :].astype(F32)
        ones = jnp.where((lane == 64) | (lane == 65), 1.0, 0.0)
        outs = []
        for head in range(3):
            for slot in duties:
                if slot % 3 == head:
                    for act in duties[slot]:
                        pl.when(step * windows + w == slot // 3)(act)
            moved = shift_lanes(spread[:, head * 128 : head * 128 + 128], amounts, True)
            high = moved.astype(BF).astype(F32)
            rest = pltpu.roll(moved - high, 16, 1)
            feat = jnp.where(field < 16, high, rest)
            feat = jnp.where(field < 14, feat, jnp.where((field >= 16) & (field < 30), feat, 0.0))
            feat = jnp.where(lane == 79, 1.0, feat)
            query = jnp.where(low, queries[head] * 0.125, feat)
            key_ref[0, head, w, :padded, :] = jnp.where(low, keys_low[head], key_feat).astype(BF)
            key_ref[0, head, w, padded:, :] = pad_key
            value_ref[0, head, w, :padded, :] = jnp.where(low, values[head], ones).astype(BF)
            value_ref[0, head, w, padded:, :] = jnp.zeros((keys - padded, 128), BF)
            scores = nt(query.astype(BF), key_ref[0, head, w])
            top = jnp.max(scores, -1, keepdims=True)
            expo = jnp.exp(scores - top).astype(BF)
            mixed = nn(expo, value_ref[0, head, w])
            total = mixed[:, 64:65]
            outs.append(mixed / total)
            logsum = -(top + jnp.log(total))
            first = logsum.astype(BF).astype(F32)
            second = (logsum - first).astype(BF).astype(F32)
            third = logsum - first - second
            query = jnp.where(lane == 78, first, query)
            query = jnp.where(lane == 94, second, query)
            query = jnp.where(lane == 95, third, query)
            query_ref[0, head, rows, :] = query.astype(BF)
        out_ref[0, rows, :128] = jnp.where(low, 0.0, pltpu.roll(outs[0], 64, 1)).astype(BF)
        out_ref[0, rows, 128:] = jnp.where(low, outs[1], pltpu.roll(outs[2], 64, 1)).astype(BF)
        return carry

    lax.fori_loop(0, windows, window, 0)
    acc_ref[...] += nt(out_ref[0], flat(w_ref[:, chunk, 1])[:, 128:])
    if linked:

        @pl.when(step == pl.num_programs(0) - 1)
        def _():
            for part in mlp:
                part.arrive()
            mine.wait()
            keep.wait()
            for part in [att] + mlp:
                part.finish()


def mlp_kernel(
    x_ref, attn_ref, cotangent_ref, slots_ref, w_ref, bias_proj_ref, gain_ref, shift_ref, bias_down_ref, bias_up_ref,
    result_ref, gx1_ref, grad_ref, gbias_up_ref, small_ref,
    x1_ref, h2_ref, h2t_ref, gyt_ref, y_ref, dh_ref, gy_ref, bias_ref,
    *, windows, padded,
):
    first = lax.axis_index("tensor") * windows
    columns = w_ref.shape[5]
    step = pl.program_id(0)
    last = pl.num_programs(0) - 1

    @pl.when(step == 0)
    def _():
        spread_rows(cotangent_ref, gy_ref, windows, padded, lambda w: alive_of(slots_ref, first + w))
        x1 = x_ref[...].astype(F32) + (attn_ref[...] + row(bias_proj_ref))
        x1_ref[...] = x1
        normed, _ = normed_of(x1)
        h2 = (normed * row(gain_ref) + row(shift_ref)).astype(BF)
        for tile in range(bias_ref.shape[0]):
            bias_ref[tile] = row(bias_up_ref)[:, tile * columns : tile * columns + columns]
        h2_ref[...] = h2
        h2t_ref[...] = h2.T
        gyt_ref[...] = gy_ref[...].T
        y_ref[...] = jnp.zeros_like(y_ref)
        dh_ref[...] = jnp.zeros_like(dh_ref)

    up, down = flat(w_ref[:, 0, 0, 0]), flat(w_ref[:, 0, 1, 0])
    strips = (grad_ref.shape[0], grad_ref.shape[4], up.shape[1])
    upper = nn(h2_ref[...], up) + bias_ref[step]
    half = 0.5 * (1.0 + lax.erf(upper * np.float32(np.sqrt(0.5))))
    slope = half + upper * (np.float32(1.0 / np.sqrt(2 * np.pi)) * jnp.exp(-0.5 * upper * upper))
    active = (upper * half).astype(BF)
    grad_upper = (nn(gy_ref[...], down) * slope).astype(BF)
    y_ref[...] += nt(active, down)
    dh_ref[...] += nt(grad_upper, up)
    grad_ref[:, 0, 1, 0] = nn(gyt_ref[...], active).astype(BF).reshape(strips)
    grad_ref[:, 0, 0, 0] = nn(h2t_ref[...], grad_upper).astype(BF).reshape(strips)
    gbias_up_ref[0] = jnp.sum(grad_upper.astype(F32), 0, keepdims=True)

    @pl.when(step == last)
    def _():
        x1 = x1_ref[...]
        result = x1 + (y_ref[...] + row(bias_down_ref))
        length = result_ref.shape[0] // windows
        for w in range(windows):
            part = alive_of(slots_ref, first + w) * result[w * padded : w * padded + length]
            result_ref[w * length : w * length + length, :] = part.astype(BF)
        normed, inverse = normed_of(x1)
        gy = gy_ref[...].astype(F32)
        dh = dh_ref[...]
        gx1_ref[...] = gy + norm_back(dh, normed, inverse, row(gain_ref))
        small_ref[0:1, :] = jnp.sum(dh * normed, 0, keepdims=True)
        small_ref[1:2, :] = jnp.sum(dh, 0, keepdims=True)
        small_ref[2:3, :] = jnp.sum(gy, 0, keepdims=True)
        small_ref[3:8, :] = jnp.zeros_like(small_ref[3:8, :])


def attend_back_kernel(*refs, windows, padded, keys, size, linked):
    step = pl.program_id(0)
    last = pl.num_programs(0) - 1
    scatter = None
    if linked:
        scatter = make_scatter(refs[11], refs[17], refs[27:])
        refs = refs[:11] + refs[12:17] + refs[18:27]
        pl.when(step == 0)(scatter.begin)
    (
        x_ref, gx1_ref, w_ref, gain_ref, shift_ref, rel_ref, amount_ref,
        query_ref, key_ref, value_ref, out_ref,
        grad_x_ref, grad_ref, small_ref, gbias_ref, grel_ref,
        h1t_ref, gbt_ref, gb_ref, dh_ref, do_ref, gqk_ref, gv_ref, spread_ref, table_ref,
    ) = refs

    @pl.when(step == 0)
    def _():
        normed, _ = normed_of(x_ref[...].astype(F32))
        h1t_ref[...] = (normed * row(gain_ref) + row(shift_ref)).astype(BF).T
        span = 2 * size - 1
        place = lax.broadcasted_iota(jnp.int32, (64, 128), 0)
        wanted = jnp.where(place < span, span - 1 - place, jnp.where(place < 2 * span, 32 + 2 * span - 1 - place, -1))
        chosen = jnp.where((lanes_of((64, 128)) & 63) == wanted, 1.0, 0.0).astype(BF)
        table_ref[...] = tn(chosen, rel_ref[...].astype(BF)).astype(BF)
        gb = gx1_ref[...].astype(BF)
        gb_ref[...] = gb
        gbt_ref[...] = gb.T
        dh_ref[...] = jnp.zeros_like(dh_ref)
        grel_ref[...] = jnp.zeros_like(grel_ref)
        small_ref[0:1, :] = jnp.sum(gb.astype(F32), 0, keepdims=True)

    do_ref[...] = nn(gb_ref[...], flat(w_ref[:, 0, 1])[:, 128:]).astype(BF)
    lane = lanes_of((padded, 128))
    low = lane < 64
    field = lane & 31
    amounts = amount_ref[...]
    kept = (lane >= 64) & (field < 14)

    def window(w, carry):
        if linked:
            for number in range(1, len(scatter.steps)):
                for action in scatter.steps[number]:
                    pl.when(step * windows + w == number)(action)
        rows = pl.ds(pl.multiple_of(w * padded, 16), padded)
        do = do_ref[rows, :].astype(F32)
        out = out_ref[0, rows, :].astype(F32)
        product = do * out
        grads = [pltpu.roll(do[:, :128], 64, 1), do[:, 128:], pltpu.roll(do[:, 128:], 64, 1)]
        sums = [
            jnp.sum(jnp.where(low, 0.0, product[:, :128]), -1, keepdims=True),
            jnp.sum(jnp.where(low, product[:, 128:], 0.0), -1, keepdims=True),
            jnp.sum(jnp.where(low, 0.0, product[:, 128:]), -1, keepdims=True),
        ]
        gq, gk, gv = [], [], []
        for head in range(3):
            delta = -sums[head]
            first = delta.astype(BF).astype(F32)
            grad_out = jnp.where(low, grads[head], jnp.where(lane == 64, first, jnp.where(lane == 65, delta - first, 0.0))).astype(BF)
            query, key, value = query_ref[0, head, rows, :], key_ref[0, head, w], value_ref[0, head, w]
            prob = jnp.exp(nt(query, key))
            grad_scores = (prob * nt(grad_out, value)).astype(BF)
            gv.append(tn(prob.astype(BF), grad_out)[:padded])
            gk.append(tn(grad_scores, query)[:padded])
            both = nn(grad_scores, key)
            back = shift_lanes(jnp.where(kept, both, 0.0), amounts, False)
            high = back.astype(BF).astype(F32)
            pack = jnp.where(low, pltpu.roll(back - high, 64, 1), high).astype(BF)
            spread_ref[head, rows, :] = pack
            gq.append(both * 0.125 + nn(pack, table_ref[...]))
        gqk_ref[rows, :128] = jnp.where(low, gq[0], pltpu.roll(gq[1], 64, 1)).astype(BF)
        gqk_ref[rows, 128:256] = jnp.where(low, gq[2], pltpu.roll(gk[0], 64, 1)).astype(BF)
        gqk_ref[rows, 256:] = jnp.where(low, gk[1], pltpu.roll(gk[2], 64, 1)).astype(BF)
        gv_ref[rows, :128] = jnp.where(low, gv[0], pltpu.roll(gv[1], 64, 1)).astype(BF)
        gv_ref[rows, 128:] = jnp.where(low, gv[2], 0.0).astype(BF)
        return carry

    lax.fori_loop(0, windows, window, 0)
    for head in range(3):
        grel_ref[...] += tn(spread_ref[head], query_ref[0, head])
    gqk, gv = gqk_ref[...], gv_ref[...]
    gbias_ref[0, :, :384] = jnp.sum(gqk.astype(F32), 0, keepdims=True)
    gbias_ref[0, :, 384:] = jnp.sum(gv.astype(F32), 0, keepdims=True)
    dh_ref[...] += nt(gqk, flat(w_ref[:, 0, 0])) + nt(gv, flat(w_ref[:, 0, 1])[:, :256])
    h1t = h1t_ref[...]
    strips = (grad_ref.shape[0], grad_ref.shape[3], -1)
    grad_ref[:, 0, 0] = nn(h1t, gqk).astype(BF).reshape(strips)
    one, two = nn(h1t, gv), nn(gbt_ref[...], out_ref[0])
    grad_ref[:, 0, 1, :, :128] = one[:, :128].astype(BF).reshape(strips)
    grad_ref[:, 0, 1, :, 128:256] = (one[:, 128:] + two[:, :128]).astype(BF).reshape(strips)
    grad_ref[:, 0, 1, :, 256:] = two[:, 128:].astype(BF).reshape(strips)

    @pl.when(step == last)
    def _():
        normed, inverse = normed_of(x_ref[...].astype(F32))
        dh = dh_ref[...]
        grad_x = (gx1_ref[...] + norm_back(dh, normed, inverse, row(gain_ref))).astype(BF)
        length = grad_x_ref.shape[0] // windows
        for w in range(windows):
            grad_x_ref[w * length : w * length + length, :] = grad_x[w * padded : w * padded + length]
        small_ref[1:2, :] = jnp.sum(dh * normed, 0, keepdims=True)
        small_ref[2:3, :] = jnp.sum(dh, 0, keepdims=True)
        small_ref[3:8, :] = jnp.zeros_like(small_ref[3:8, :])
        if linked:
            scatter.finish()


def unpack_kernel(
    total_ref, att_ref, mlp_ref,
    qkv_ref, proj_ref, up_ref, down_ref, gain1_ref, shift1_ref, q_ref, v_ref, rel_h_ref, rel_w_ref,
    proj_bias_ref, gain2_ref, shift2_ref, up_bias_ref, down_bias_ref,
    *, span,
):
    qkv_ref[0] = att_ref[0, :, :192]
    qkv_ref[1] = att_ref[0, :, 192:]
    qkv_ref[2] = att_ref[1, :, :192]
    proj_ref[...] = att_ref[1, :, 192:].T
    up_ref[:, :384] = mlp_ref[0]
    up_ref[:, 384:] = mlp_ref[1]
    down_ref[:, :384] = mlp_ref[2]
    down_ref[:, 384:] = mlp_ref[3]
    for first, ref in ((0, proj_bias_ref), (6, gain1_ref), (12, shift1_ref), (18, gain2_ref), (24, shift2_ref), (30, down_bias_ref), (56, up_bias_ref)):
        for lane in range(0, ref.shape[0], 128):
            ref[pl.ds(lane, 128)] = total_ref[first + lane // 128]
    for start, ref in ((36, q_ref), (39, v_ref)):
        pieces = []
        for t in range(ref.shape[0] // 192):
            first = start + 5 * t
            pieces.append((total_ref[first : first + 1, :], total_ref[first + 1 : first + 2, :]))
        for pair in range(len(pieces) // 2):
            one, two = pieces[2 * pair], pieces[2 * pair + 1]
            low = lanes_of((1, 128)) < 64
            turned = [pltpu.roll(jnp.broadcast_to(v, (8, 128)), 64, 1)[:1] for v in two]
            parts = [one[0], jnp.where(low, one[1], turned[0]), jnp.where(low, turned[0], turned[1])]
            for i, values in enumerate(parts):
                ref[pl.ds(pair * 384 + i * 128, 128)] = values[0]
    rel = total_ref[total_ref.shape[0] - 64 :, :]
    high = rel.astype(BF)
    middle = (rel - high.astype(F32)).astype(BF)
    rest = (rel - high.astype(F32) - middle.astype(F32)).astype(BF)
    for ref, first in ((rel_h_ref, 0), (rel_w_ref, 32)):
        place = lax.broadcasted_iota(jnp.int32, (32, 64), 0)
        chosen = jnp.where(lanes_of((32, 64)) == first + span - 1 - place, 1.0, 0.0).astype(BF)
        values = nn(chosen, high) + nn(chosen, middle) + nn(chosen, rest)
        ref[...] = 8.0 * values[:span, :64]


def whole(shape):
    return pl.BlockSpec(shape, lambda *index: (0,) * len(shape))


def once(shape):
    return pl.BlockSpec(shape, lambda *index: (0,) * len(shape), pipeline_mode=pl.Buffered(1))


def shards(
    block_input, cotangent, pad_mask, slot_window, qkv_w, proj_w, fc1_w, fc2_w,
    norm1_gain, norm1_bias, q_bias, v_bias, rel_h, rel_w, proj_bias,
    norm2_gain, norm2_bias, fc1_bias, fc2_bias,
):
    part = lax.axis_index("tensor")
    count_dp, count_t = lax.axis_size("dp"), lax.axis_size("tensor")
    length = pad_mask.shape[1]
    local_rows, width = block_input.shape
    windows = local_rows // length
    size = rel_h.shape[0] // 2 + 1
    padded = -(-length // 16) * 16
    keys = -(-length // 128) * 128
    rows = windows * padded
    strip = width // count_dp

    slots = jnp.pad(slot_window, (0, 128 - slot_window.shape[0]), constant_values=-1).reshape(1, 128)
    rel = jnp.pad(jnp.concatenate([rel_h, rel_w]), ((0, 64 - 2 * rel_h.shape[0]), (0, 64)))

    place = np.arange(padded)
    row_of, col_of = place // size, place % size
    inside = place < length
    amount = np.zeros((padded, 128), np.int32)
    amount[:, :] = np.where(
        (np.arange(128) % 64 < 32)[None, :], (size - 1 - row_of)[:, None], (size - 1 - col_of)[:, None]
    ) * inside[:, None]
    amount = jnp.asarray(amount)
    feat = np.zeros((padded, 128), np.float32)
    for a in range(size):
        for base, pos in ((64, row_of), (96, col_of)):
            feat[:, base + a] = (pos == a) & inside
            feat[:, base + 16 + a] = (pos == a) & inside
    feat[:, [78, 94, 95]] = 1.0
    feat[:, 79] = np.where(inside, 0.0, NEGATIVE)
    feat = jnp.asarray(feat.astype(BF))
    span = rel_h.shape[0]

    q_w, k_w, v_w = qkv_w[0], qkv_w[1], qkv_w[2]
    shard = jnp.stack(
        [
            jnp.concatenate([q_w, k_w], 1),
            jnp.concatenate([v_w, proj_w.T], 1),
            fc1_w[:, :384],
            fc1_w[:, 384:],
            fc2_w.T[:, :384],
            fc2_w.T[:, 384:],
        ]
    )
    linked = count_dp == 8 and count_t == 4 and strip % 16 == 0 and windows == 4
    any_spec, vmem_spec = pl.BlockSpec(memory_space=pl.ANY), pl.BlockSpec(memory_space=pltpu.VMEM)
    blocks, depth = (count_dp, strip) if linked else (1, width)

    def talk(number, **more):
        return pltpu.CompilerParams(
            vmem_limit_bytes=VMEM_LIMIT, collective_id=number, has_side_effects=True, **more)

    def gather_all(pieces):
        every = lax.all_gather(pieces, AXES, axis=0, tiled=False).reshape(count_dp, count_t, -1, strip, 384)
        return every.transpose(1, 2, 0, 3, 4).reshape(1, count_t, -1, width, 384)

    if not linked:
        w_att, w_mlp = gather_all(shard[:2]), gather_all(shard[2:])

    vec = once((width,))
    params = pltpu.CompilerParams(dimension_semantics=("arbitrary",), vmem_limit_bytes=VMEM_LIMIT)

    query, key, value, out, attn, x, *rest = pl.pallas_call(
        partial(attend_kernel, windows=windows, padded=padded, keys=keys, size=size, linked=linked),
        grid=(count_t,),
        in_specs=[
            once((local_rows, width)),
        ] + [pl.BlockSpec((blocks, 1, 2, depth, 384), lambda t: (0, t, 0, 0, 0))] * (not linked) + [
            vec, vec, vec, vec, once((64, 128)), once((1, 128)), once(pad_mask.shape[::-1]),
            once((padded, 128)), once((padded, 128)),
        ] + [once((6, strip, 384))] * linked,
        out_specs=[
            pl.BlockSpec((1, 3, rows, 128), lambda t: (t, 0, 0, 0)),
            pl.BlockSpec((1, 3, windows, keys, 128), lambda t: (t, 0, 0, 0, 0)),
            pl.BlockSpec((1, 3, windows, keys, 128), lambda t: (t, 0, 0, 0, 0)),
            pl.BlockSpec((1, rows, 256), lambda t: (t, 0, 0)),
            whole((rows, width)), whole((rows, width)),
        ] + [any_spec, any_spec] * linked,
        out_shape=[
            jax.ShapeDtypeStruct((count_t, 3, rows, 128), BF),
            jax.ShapeDtypeStruct((count_t, 3, windows, keys, 128), BF),
            jax.ShapeDtypeStruct((count_t, 3, windows, keys, 128), BF),
            jax.ShapeDtypeStruct((count_t, rows, 256), BF),
            jax.ShapeDtypeStruct((rows, width), F32),
            jax.ShapeDtypeStruct((rows, width), BF),
        ] + [jax.ShapeDtypeStruct((count_dp, count_t, pieces, strip, 384), BF) for pieces in (2, 4)] * linked,
        scratch_shapes=[
            pltpu.VMEM((rows, width), BF), pltpu.VMEM((rows, 384), BF), pltpu.VMEM((rows, 256), BF),
            pltpu.VMEM((2, 256, 384), BF), pltpu.VMEM((rows, 128), BF), pltpu.VMEM((count_t, 1, 640), F32),
        ]
        + ([pltpu.VMEM((count_dp, count_t, 2, strip, 384), BF)] + gather_scratch() * (1 + MLP_PARTS) + [pltpu.SemaphoreType.DMA((2,))]) * linked,
        compiler_params=talk(2, dimension_semantics=("arbitrary",)) if linked else params,
        name="attend",
    )(
        block_input, *([] if linked else [w_att]), norm1_gain, norm1_bias, q_bias, v_bias, rel, slots, pad_mask.T, feat, amount,
        *([shard] * linked)
    )
    if linked:
        w_att, w_mlp = rest
    w_mlp = w_mlp.reshape(blocks, count_t, 2, 2, depth, 384)

    tiles = 2 * count_t
    mlp_block = pl.BlockSpec((blocks, 1, 2, 1, depth, 384), lambda j: (0, j // 2, 0, j % 2, 0, 0))
    result, gx1, grad_mlp, gbias_up, small2 = pl.pallas_call(
        partial(mlp_kernel, windows=windows, padded=padded),
        grid=(tiles,),
        in_specs=[
            once((rows, width)), once((rows, width)), once((local_rows, width)), once((1, 128)),
            mlp_block, vec, vec, vec, vec, once(fc1_bias.shape),
        ],
        out_specs=[
            whole((local_rows, width)), whole((rows, width)),
            mlp_block,
            pl.BlockSpec((1, 1, 384), lambda j: (j, 0, 0)),
            whole((8, width)),
        ],
        out_shape=[
            jax.ShapeDtypeStruct((local_rows, width), BF),
            jax.ShapeDtypeStruct((rows, width), F32),
            jax.ShapeDtypeStruct((blocks, count_t, 2, 2, depth, 384), BF),
            jax.ShapeDtypeStruct((tiles, 1, 384), F32),
            jax.ShapeDtypeStruct((8, width), F32),
        ],
        scratch_shapes=[
            pltpu.VMEM((rows, width), F32), pltpu.VMEM((rows, width), BF),
            pltpu.VMEM((width, rows), BF), pltpu.VMEM((width, rows), BF),
            pltpu.VMEM((rows, width), F32), pltpu.VMEM((rows, width), F32), pltpu.VMEM((rows, width), BF),
            pltpu.VMEM((tiles, 1, 384), F32),
        ],
        compiler_params=params,
        name="mlp",
    )(x, attn, cotangent, slots, w_mlp, proj_bias, norm2_gain, norm2_bias, fc2_bias, fc1_bias)

    grad_x, grad_att, small1, gbias_att, grel, *rest = pl.pallas_call(
        partial(attend_back_kernel, windows=windows, padded=padded, keys=keys, size=size, linked=linked),
        grid=(count_t,),
        in_specs=[
            once((rows, width)), once((rows, width)),
            pl.BlockSpec((blocks, 1, 2, depth, 384), lambda t: (0, t, 0, 0, 0)),
            vec, vec, once((64, 128)), once((padded, 128)),
            pl.BlockSpec((1, 3, rows, 128), lambda t: (t, 0, 0, 0)),
            pl.BlockSpec((1, 3, windows, keys, 128), lambda t: (t, 0, 0, 0, 0)),
            pl.BlockSpec((1, 3, windows, keys, 128), lambda t: (t, 0, 0, 0, 0)),
            pl.BlockSpec((1, rows, 256), lambda t: (t, 0, 0)),
        ] + [any_spec] * linked,
        out_specs=[
            whole((local_rows, width)),
            pl.BlockSpec((blocks, 1, 2, depth, 384), lambda t: (0, t, 0, 0, 0)),
            whole((8, width)),
            pl.BlockSpec((1, 1, 640), lambda t: (t, 0, 0)),
            whole((128, 128)),
        ] + [whole((4, strip, 384))] * linked,
        out_shape=[
            jax.ShapeDtypeStruct((local_rows, width), BF),
            jax.ShapeDtypeStruct((blocks, count_t, 2, depth, 384), BF),
            jax.ShapeDtypeStruct((8, width), F32),
            jax.ShapeDtypeStruct((count_t, 1, 640), F32),
            jax.ShapeDtypeStruct((128, 128), F32),
        ] + [jax.ShapeDtypeStruct((4, strip, 384), F32)] * linked,
        scratch_shapes=[
            pltpu.VMEM((width, rows), BF), pltpu.VMEM((width, rows), BF), pltpu.VMEM((rows, width), BF),
            pltpu.VMEM((rows, width), F32), pltpu.VMEM((rows, 256), BF),
            pltpu.VMEM((rows, 384), BF), pltpu.VMEM((rows, 256), BF), pltpu.VMEM((3, rows, 128), BF),
            pltpu.VMEM((128, 128), BF),
        ] + (scatter_scratch(4, strip, 384) if linked else []),
        compiler_params=talk(3, dimension_semantics=("arbitrary",)) if linked else params,
        name="attend_back",
    )(
        x, gx1, w_att, norm1_gain, norm1_bias, rel, amount, query, key, value, out,
        *([grad_mlp.reshape(count_dp // 2, 2, count_t, 4, strip, 384)] * linked if linked else [])
    )

    if linked:
        sum_mlp = rest[0]
        count = 36 + 5 * count_t + 3 * tiles + 64
        sum_att, total = pl.pallas_call(
            reduce_kernel,
            in_specs=[any_spec] + [vmem_spec] * 5, out_specs=[vmem_spec, vmem_spec],
            out_shape=[jax.ShapeDtypeStruct((2, strip, 384), F32), jax.ShapeDtypeStruct((count, 128), F32)],
            scratch_shapes=[
                pltpu.VMEM((count, 128), F32), pltpu.VMEM((10, count, 128), F32),
                pltpu.SemaphoreType.DMA((5,)), pltpu.SemaphoreType.DMA((5,)),
            ] + scatter_scratch(2, strip, 384),
            compiler_params=talk(4),
            name="reduce_attention",
        )(grad_att.reshape(count_dp // 2, 2, count_t, 2, strip, 384), small1, small2, gbias_att, gbias_up, grel)
        like = (
            qkv_w, proj_w, fc1_w, fc2_w.T, norm1_gain, norm1_bias, q_bias, v_bias, rel_h, rel_w,
            proj_bias, norm2_gain, norm2_bias, fc1_bias, fc2_bias,
        )
        shapes = [jax.ShapeDtypeStruct(v.shape, F32) for v in like]
        outs = pl.pallas_call(
            partial(unpack_kernel, span=span),
            in_specs=[vmem_spec] * 3, out_specs=[vmem_spec] * len(shapes), out_shape=shapes,
            compiler_params=pltpu.CompilerParams(vmem_limit_bytes=VMEM_LIMIT),
            name="unpack",
        )(total, sum_att, sum_mlp)
        return (result, grad_x, *outs[:3], outs[3].T, *outs[4:])
    parts = [
        small1[:3].reshape(-1, 128), small2[:3].reshape(-1, 128), gbias_att.reshape(-1, 128), gbias_up.reshape(-1, 128), grel[64:],
    ]
    def scatter_all(grads):
        grads = grads.reshape(count_t, -1, count_dp, strip, 384).transpose(2, 0, 1, 3, 4)
        grads = grads.reshape(count_dp * count_t, -1, strip, 384)
        return lax.psum_scatter(grads, AXES, scatter_dimension=0, tiled=False).astype(F32)

    sum_mlp, sum_att = scatter_all(grad_mlp), scatter_all(grad_att)
    small = lax.psum(jnp.concatenate(parts), AXES)
    cuts = np.cumsum([part.shape[0] for part in parts])[:-1]
    small1, small2, gbias_att, gbias_up, grad_rel = jnp.split(small, cuts)
    small1, small2 = small1.reshape(3, width), small2.reshape(3, width)
    gbias_att = gbias_att.reshape(count_t, 1, 640)
    grad_rel = 8.0 * grad_rel[:, :64]
    head_q, head_k = sum_att[0, :, :192], sum_att[0, :, 192:]
    head_v, head_p = sum_att[1, :, :192], sum_att[1, :, 192:]
    return (
        result,
        grad_x,
        jnp.stack([head_q, head_k, head_v]),
        head_p.T,
        jnp.concatenate([sum_mlp[0], sum_mlp[1]], 1),
        jnp.concatenate([sum_mlp[2], sum_mlp[3]], 1).T,
        small1[1],
        small1[2],
        gbias_att[:, 0, :192].reshape(-1),
        gbias_att[:, 0, 384:576].reshape(-1),
        grad_rel[:span][::-1],
        grad_rel[32 : 32 + span][::-1],
        small1[0],
        small2[0],
        small2[1],
        gbias_up.reshape(-1),
        small2[2],
    )


def solution(mesh):
    return jax.shard_map(
        shards,
        mesh=mesh,
        in_specs=(
            P(AXES, None), P(AXES, None), P(), P("dp"),
            P(None, "dp", "tensor"), P("tensor", "dp"), P("dp", "tensor"), P("tensor", "dp"),
        )
        + (P(),) * 11,
        out_specs=(
            P(AXES, None), P(AXES, None),
            P(None, "dp", "tensor"), P("tensor", "dp"), P("dp", "tensor"), P("tensor", "dp"),
        )
        + (P(),) * 11,
        check_vma=False,
    )
```

```python
from functools import partial

import jax
import jax.numpy as jnp
import numpy as np
from jax import lax
from jax.experimental import pallas as pl
from jax.experimental.pallas import tpu as pltpu
from jax.sharding import PartitionSpec as P

HD = 64
EPSILON = 1e-06
NEGATIVE = -1e30
F32, BF = jnp.float32, jnp.bfloat16
AXES = ("dp", "tensor")
VMEM_LIMIT = 60 * 1024 * 1024
MLP_BEGIN = 11
MLP_SLOTS = tuple(range(3, 48, 3))
SUM_SLOTS = (3, 3, 6, 6, 9, 12, 15, 15, 18, 18, 21, 21, 24, 24, 27, 27, 30, 33, 36)


def nn(left, right):
    return lax.dot_general(left, right, (((1,), (0,)), ((), ())), preferred_element_type=F32)


def nt(left, right):
    return lax.dot_general(left, right, (((1,), (1,)), ((), ())), preferred_element_type=F32)


def tn(left, right):
    return lax.dot_general(left, right, (((0,), (0,)), ((), ())), preferred_element_type=F32)


def normed_of(values):
    center = values - jnp.mean(values, -1, keepdims=True)
    inverse = lax.rsqrt(jnp.mean(center * center, -1, keepdims=True) + EPSILON)
    return center * inverse, inverse


def norm_back(grad, normed, inverse, gain):
    scaled = grad * gain
    inner = (
        scaled
        - jnp.mean(scaled, -1, keepdims=True)
        - normed * jnp.mean(scaled * normed, -1, keepdims=True)
    )
    return inverse * inner


def spread_rows(source_ref, target_ref, w, length, padded, live=None):
    tail = w * padded + length // 16 * 16
    target_ref[tail : w * padded + padded, :] = jnp.zeros((w * padded + padded - tail, target_ref.shape[1]), target_ref.dtype)
    values = source_ref[w * length : w * length + length, :]
    if live is not None:
        values = jnp.where(live > 0.5, values.astype(F32), 0.0).astype(values.dtype)
    target_ref[w * padded : w * padded + length, :] = values


def row(ref):
    return ref[...].reshape(1, -1)


def flat(values):
    return values.reshape(-1, values.shape[-1])


def lanes_of(shape):
    return lax.broadcasted_iota(jnp.int32, shape, 1)


def of_slot(values, slot):
    return jnp.sum(jnp.where(lanes_of(values.shape) == slot, values, 0.0), -1, keepdims=True)


def alive_of(slots_ref, slot):
    return of_slot(jnp.where(slots_ref[...] >= 0, 1.0, 0.0), slot)


def shift_lanes(values, amounts, left):
    for bit in (1, 2, 4, 8):
        moved = pltpu.roll(values, 128 - bit if left else bit, 1)
        values = jnp.where((amounts & bit) != 0, moved, values)
    return values


MESH = pl.DeviceIdType.MESH


class Place:
    def __init__(self, height):
        self.height = height
        self.dp, self.tensor = lax.axis_index("dp"), lax.axis_index("tensor")
        self.z, self.y = lax.div(self.dp, 2), lax.rem(self.dp, 2)
        self.x, self.c = lax.div(self.tensor, 2), lax.rem(self.tensor, 2)

    def plane(self, colour, a, b):
        return lax.rem(self.y + (1 - colour) * b + colour * a, 2), lax.rem(self.x + (1 - colour) * a + colour * b, 2)

    def shard(self, colour, a, b, z):
        y, x = self.plane(colour, a, b)
        return z * 2 + y, x * 2 + colour

    def near(self, k):
        upper = lax.div(self.z, self.height // 2)
        zz = self.z + upper * (self.height - 1 - 2 * self.z)
        q = (zz, 1 - zz, 2, 3)[k]
        return q + upper * (self.height - 1 - 2 * q)

    def peer(self, kind):
        if kind == "core":
            return self.dp, self.x * 2 + 1 - self.c
        if kind in ("z1", "z2", "z3"):
            return self.near(int(kind[1])) * 2 + self.y, self.tensor
        if kind == "up":
            return self.dp + 2, self.tensor
        if kind == "down":
            return self.dp - 2, self.tensor
        if kind == "y":
            return self.z * 2 + 1 - self.y, self.tensor
        if kind == "x":
            return self.dp, (1 - self.x) * 2 + self.c
        if kind == "pair":
            return (self.z + 1 - 2 * lax.rem(self.z, 2)) * 2 + self.y, self.tensor
        if kind == "half":
            return lax.rem(self.z + 2, 4) * 2 + self.y, self.tensor
        return self.shard(self.c, int(kind == "far"), int(kind == "near"), self.z)

    def has(self, kind):
        if kind == "up":
            return self.z < self.height - 1
        if kind == "down":
            return self.z > 0
        return None

    def greet(self):
        barrier = pltpu.get_barrier_semaphore()
        for kind in ("core", "near", "far", "z1", "z2", "z3"):
            pl.semaphore_signal(barrier, inc=1, device_id=self.peer(kind), device_id_type=MESH)
        pl.semaphore_wait(barrier, 6)


def under(condition, action):
    if condition is None:
        action()
    else:
        pl.when(condition)(action)


def both(one, two):
    return two if one is None else one if two is None else jnp.logical_and(one, two)


class Gather:
    SENDS = 36

    def __init__(self, at, own_ref, all_ref, send_sem, recv_sem, first=0, count=None):
        self.at, self.own_ref = at, own_ref
        self.all_ref = all_ref if count is None else all_ref.at[:, :, first : first + count]
        self.send_sem, self.recv_sem = send_sem, recv_sem
        z = [lambda k=k: self.step(("z", k)) for k in range(4)]
        near = [lambda k=k: self.step(("near", k)) for k in range(4)]
        far = [[lambda b=b, k=k: self.step(("far", b, k)) for k in range(4)] for b in range(2)]
        self.steps = [
            near[0], z[1], far[0][0], near[1], far[1][0], z[2], far[0][1],
            near[2], far[1][1], z[3], far[0][2], near[3], far[1][2], far[0][3], far[1][3],
        ]
        slot = 0
        self.slots = {}
        for key in [("z", k) for k in range(4)] + [("near", k) for k in range(4)] + [("far", b, k) for b in range(2) for k in range(4)]:
            self.slots[key] = slot
            slot += len(self.kinds(key))

    def kinds(self, key):
        return {"z": ("up", "down", "near", "far", "core"), "near": ("far", "core"), "far": ("core",)}[key[0]]

    def shard(self, key):
        at = self.at
        if key[0] == "z":
            return at.shard(at.c, 0, 0, at.near(key[1]))
        if key[0] == "near":
            return at.shard(at.c, 0, 1, at.near(key[1]))
        return at.shard(at.c, 1, key[1], at.near(key[2]))

    def copy(self, source, shard, kind, slot):
        dp, tensor = shard
        return pltpu.make_async_remote_copy(
            src_ref=source, dst_ref=self.all_ref.at[dp, tensor], send_sem=self.send_sem.at[slot],
            recv_sem=self.recv_sem.at[dp * 4 + tensor], device_id=self.at.peer(kind), device_id_type=MESH)

    def sends(self, key):
        shard = self.shard(key)
        source = self.own_ref if key == ("z", 0) else self.all_ref.at[shard[0], shard[1]]
        away = self.at.near(key[1]) - self.at.z if key[0] == "z" else 0
        sends = []
        for i, kind in enumerate(self.kinds(key)):
            condition = self.at.has(kind)
            if kind in ("up", "down"):
                condition = jnp.logical_and(condition, away <= 0 if kind == "up" else away >= 0)
            sends.append((condition, self.copy(source, shard, kind, self.slots[key] + i)))
        return sends

    def take(self, shard):
        self.copy(self.all_ref.at[shard[0], shard[1]], shard, "core", 0).wait_recv()

    def begin(self):
        for condition, copy in self.sends(("z", 0)):
            under(condition, copy.start)

    def step(self, key):
        self.take(self.shard(key))
        for condition, copy in self.sends(key):
            under(condition, copy.start)

    def arrive(self):
        at = self.at
        for a in range(2):
            for b in range(2):
                for k in range(4):
                    self.take(at.shard(1 - at.c, a, b, at.near(k)))

    def finish(self):
        for key in self.slots:
            for condition, copy in self.sends(key):
                under(condition, copy.wait_send)


def gather_scratch():
    return [pltpu.SemaphoreType.DMA((Gather.SENDS,)), pltpu.SemaphoreType.DMA((32,))]


class Scatter:
    def __init__(self, all_ref, own_ref, held, core_in, far_in, near_in, up_in, down_in, sems, height=4):
        self.all_ref, self.own_ref, self.held, self.core_in = all_ref, own_ref, held, core_in
        self.far_in, self.near_in, self.up_in, self.down_in, self.sems = far_in, near_in, up_in, down_in, sems
        self.at = Place(height)
        core = {(a, b): (lambda a=a, b=b: self.from_core(a, b)) for a in range(2) for b in range(2)}
        far = [[lambda b=b, k=k: self.from_far(b, k) for k in range(4)] for b in range(2)]
        near = [lambda k=k: self.from_near(k) for k in range(4)]
        line = [lambda k=k: self.from_line(k) for k in range(4)]
        self.steps = [
            core[1, 1], core[1, 0], core[0, 1], core[0, 0], far[1][3], far[1][2], far[1][1], near[3], far[1][0], near[2],
            far[0][3], near[1], far[0][2], line[3], near[0], far[0][1], line[2], far[0][0], line[1],
        ]
        self.last = line[0]

    def remote(self, source, target, name, index, kind):
        send, recv = self.sems[name]
        return pltpu.make_async_remote_copy(
            src_ref=source, dst_ref=target, send_sem=send.at[index], recv_sem=recv.at[index],
            device_id=self.at.peer(kind), device_id_type=MESH)

    def core_copy(self, a, b):
        at = self.at
        y, x = at.plane(1 - at.c, a, b)
        source = self.all_ref.at[:, y, x * 2 + 1 - at.c]
        return self.remote(source, self.core_in.at[a, b], "core", a * 2 + b, "core")

    def local_copy(self, a, b):
        at = self.at
        y, x = at.plane(at.c, a, b)
        return pltpu.make_async_copy(self.all_ref.at[:, y, x * 2 + at.c], self.held.at[a, b], self.sems["local"].at[a * 2 + b])

    def far_copy(self, b, z):
        return self.remote(self.held.at[1, b, z], self.far_in.at[b, z], "far", b * 4 + z, "far")

    def near_copy(self, z):
        return self.remote(self.held.at[0, 1, z], self.near_in.at[z], "near", z, "near")

    def down_copy(self, z):
        return self.remote(self.held.at[0, 0, z], self.down_in.at[z], "down", z, "down")

    def up_copy(self, z):
        return self.remote(self.held.at[0, 0, z], self.up_in.at[z], "up", z, "up")

    def begin(self):
        self.at.greet()
        for a in (1, 0):
            for b in (1, 0):
                self.core_copy(a, b).start()
                self.local_copy(a, b).start()

    def from_core(self, a, b):
        self.local_copy(a, b).wait()
        self.core_copy(a, b).wait_recv()
        for z in range(4):
            self.held[a, b, z] = self.held[a, b, z] + self.core_in[a, b, z]
        if a == 1:
            for k in (3, 2, 1, 0):
                self.far_copy(b, self.at.near(k)).start()

    def from_far(self, b, k):
        z = self.at.near(k)
        self.far_copy(b, z).wait_recv()
        self.held[0, b, z] = self.held[0, b, z] + self.far_in[b, z]
        if b == 1:
            self.near_copy(z).start()

    def from_near(self, k):
        z = self.at.near(k)
        self.near_copy(z).wait_recv()
        self.held[0, 0, z] = self.held[0, 0, z] + self.near_in[z]

    def from_line(self, k):
        at = self.at
        if k > 0:
            z = at.near(k)

            def downward():
                def add():
                    self.down_copy(z).wait_recv()
                    self.held[0, 0, z] = self.held[0, 0, z] + self.down_in[z]

                under(at.has("up"), add)
                self.down_copy(z).start()

            def upward():
                def add():
                    self.up_copy(z).wait_recv()
                    self.held[0, 0, z] = self.held[0, 0, z] + self.up_in[z]

                under(at.has("down"), add)
                self.up_copy(z).start()

            pl.when(z < at.z)(downward)
            pl.when(z > at.z)(upward)
            return
        self.own_ref[...] = self.held[0, 0, at.z].astype(F32)

        def add_down():
            self.down_copy(at.z).wait_recv()
            self.own_ref[...] += self.down_in[at.z].astype(F32)

        def add_up():
            self.up_copy(at.z).wait_recv()
            self.own_ref[...] += self.up_in[at.z].astype(F32)

        under(at.has("up"), add_down)
        under(at.has("down"), add_up)

    def finish(self):
        at = self.at
        self.last()
        for a in range(2):
            for b in range(2):
                self.core_copy(a, b).wait_send()
        for b in range(2):
            for z in range(4):
                self.far_copy(b, z).wait_send()
        for z in range(4):
            self.near_copy(z).wait_send()
            pl.when(z < at.z)(lambda: self.down_copy(z).wait_send())
            pl.when(z > at.z)(lambda: self.up_copy(z).wait_send())


def scatter_scratch(pieces, strip, columns):
    block = (pieces, strip, columns)
    shapes = [(2, 2, 4), (2, 2, 4), (2, 4), (4,), (4,), (4,)]
    sems = [4, 4, 8, 8, 4, 4, 4, 4, 4, 4, 4]
    return [pltpu.VMEM(lead + block, BF) for lead in shapes] + [pltpu.SemaphoreType.DMA((n,)) for n in sems]


SCATTER_REFS = 17


def make_scatter(all_ref, own_ref, refs):
    held, core_in, far_in, near_in, up_in, down_in = refs[:6]
    core_s, core_r, far_s, far_r, near_s, near_r, up_s, up_r, down_s, down_r, local = refs[6:]
    sems = {
        "core": (core_s, core_r), "far": (far_s, far_r), "near": (near_s, near_r),
        "up": (up_s, up_r), "down": (down_s, down_r), "local": local,
    }
    return Scatter(all_ref, own_ref, held, core_in, far_in, near_in, up_in, down_in, sems)


def packed(refs):
    small1_ref, small2_ref, gbias_att_ref, gbias_up_ref = refs
    places = []
    for ref, rows in ((small1_ref, range(3)), (small2_ref, range(3))):
        places += [(ref, (row, lane)) for row in rows for lane in range(0, ref.shape[1], 128)]
    for ref in (gbias_att_ref, gbias_up_ref):
        places += [(ref, (row, 0, lane)) for row in range(ref.shape[0]) for lane in range(0, ref.shape[2], 128)]
    return places


def reduce_kernel(
    all_ref, small1_ref, small2_ref, gbias_att_ref, gbias_up_ref, grel_ref,
    own_ref, total_ref, small_ref, small_in, small_send, small_recv, *refs,
):
    scatter = make_scatter(all_ref, own_ref, refs)
    at = scatter.at
    rounds = ("core", "y", "x", "pair", "half")

    def exchange(index):
        return pltpu.make_async_remote_copy(
            src_ref=small_ref if index == 0 else small_in.at[5 + index], dst_ref=small_in.at[index],
            send_sem=small_send.at[index], recv_sem=small_recv.at[index],
            device_id=at.peer(rounds[index]), device_id_type=MESH)

    def fold(index):
        exchange(index).wait_recv()
        own = small_ref[...] if index == 0 else small_in[5 + index]
        if index < 4:
            small_in[6 + index] = own + small_in[index]
            exchange(index + 1).start()
        else:
            total_ref[...] = own + small_in[index]

    scatter.begin()
    for row, (ref, index) in enumerate(packed((small1_ref, small2_ref, gbias_att_ref, gbias_up_ref))):
        if len(index) == 2:
            small_ref[row : row + 1, :] = ref[index[0] : index[0] + 1, index[1] : index[1] + 128]
        else:
            small_ref[row : row + 1, :] = ref[index[0], 0:1, index[2] : index[2] + 128]
    small_ref[small_ref.shape[0] - 64 :, :] = grel_ref[64:, :]
    exchange(0).start()
    for number, step in enumerate(scatter.steps):
        step()
        if number in (1, 3, 4, 7, 10):
            fold((1, 3, 4, 7, 10).index(number))
    scatter.finish()
    for index in range(5):
        exchange(index).wait_send()


def attend_kernel(*refs, windows, padded, keys, size, linked):
    step = pl.program_id(0)
    duties = {}
    refs = list(refs)
    if linked:
        own_ref, more_ref, att_ref, mlp_ref, w_ref, keep_sem = refs[10], refs[11], refs[18], refs[19], refs[26], refs[-1]
        at = Place(4)
        att = Gather(at, own_ref, w_ref, *refs[27:29])
        mlp = Gather(at, more_ref, mlp_ref, *refs[29:31])
        mine = pltpu.make_async_copy(more_ref, mlp_ref.at[at.dp, at.tensor], keep_sem.at[0])
        keep = pltpu.make_async_copy(w_ref, att_ref, keep_sem.at[1])
        refs = refs[:1] + [w_ref] + refs[1:10] + refs[12:18] + refs[20:26]

        @pl.when(step == 0)
        def _():
            at.greet()
            att.begin()
            w_ref[at.dp, at.tensor] = own_ref[...]
            mine.start()

        duties = {slot: [act for act, when in zip(mlp.steps, MLP_SLOTS) if when == slot] for slot in MLP_SLOTS}
    (
        raw_ref, w_ref, gain_ref, shift_ref, query_bias_ref, value_bias_ref, rel_ref, slots_ref, pad_ref, feat_ref, amount_ref,
        query_ref, key_ref, value_ref, out_ref, acc_ref, x_ref,
        h1_ref, qk_ref, vv_ref, table_ref, key_feat_ref, bias_ref,
    ) = refs

    @pl.when(step == 0)
    def _():
        length, count = pad_ref.shape
        span = 2 * size - 1
        part = lax.axis_index("tensor")

        def norm_rows(w):
            spread_rows(raw_ref, x_ref, w, length, padded)
            here = slice(w * padded, w * padded + padded)
            normed, _ = normed_of(x_ref[here, :].astype(F32))
            h1_ref[here, :] = (normed * row(gain_ref) + row(shift_ref)).astype(BF)
            acc_ref[here, :] = jnp.zeros((padded, acc_ref.shape[1]), F32)

        def tables():
            place = lax.broadcasted_iota(jnp.int32, (64, 128), 0)
            lane = lanes_of((64, 128))
            wanted = jnp.where(place < span, 64 + span - 1 - place, jnp.where(place < 2 * span, 96 + 2 * span - 1 - place, -1))
            chosen = jnp.where(lane == wanted, 1.0, 0.0).astype(BF)
            rel = rel_ref[...]
            high = rel.astype(BF)
            rest = (rel - high.astype(F32)).astype(BF)
            table_ref[...] = jnp.zeros_like(table_ref)
            for number, piece in enumerate((high, rest)):
                turned = tn(piece, chosen)[:64].astype(BF)
                for head in range(3):
                    table_ref[number, head * 64 : head * 64 + 64, head * 128 : head * 128 + 128] = turned
            bias_ref[...] = jnp.zeros_like(bias_ref)
            for t in range(bias_ref.shape[0]):
                bias_ref[t, 0:1, 0:192] = row(query_bias_ref)[:, t * 192 : t * 192 + 192]
                bias_ref[t, 0:1, 384:576] = row(value_bias_ref)[:, t * 192 : t * 192 + 192]

        def features():
            picked = jnp.where(lax.broadcasted_iota(jnp.int32, (count, 128), 0) == slots_ref[...], 1.0, 0.0).astype(BF)
            usable = nn(pad_ref[...].astype(F32).astype(BF), picked)
            for w in range(windows):
                mask = jnp.where(of_slot(usable, part * windows + w) > 0.5, 0.0, NEGATIVE)
                start = w * padded
                key_feat_ref[start : start + padded, :] = feat_ref[...]
                key_feat_ref[start : start + length, :] = jnp.where(
                    lanes_of((length, 128)) == 79, mask, feat_ref[:length, :].astype(F32)).astype(BF)

        chores = [lambda w=w: norm_rows(w) for w in range(windows)] + [tables, features]
        if linked:
            for number, act in enumerate(att.steps):
                act()
                if number == MLP_BEGIN:
                    mlp.begin()
                if number < len(chores):
                    chores[number]()
            att.arrive()
            keep.start()
        else:
            for chore in chores:
                chore()

    h1 = h1_ref[...]
    chunk = step if linked else 0
    wa, wb = flat(w_ref[:, chunk, 0]), flat(w_ref[:, chunk, 1])
    qk_ref[...] = (nn(h1, wa) + bias_ref[step, 0:1, :384]).astype(BF)
    vv_ref[...] = (nn(h1, wb[:, :256]) + bias_ref[step, 0:1, 384:640]).astype(BF)
    lane = lanes_of((padded, 128))
    low = lane < 64
    field = lane & 31
    amounts = amount_ref[...]
    pad_lane = lanes_of((keys - padded, 128))
    pad_key = jnp.where(pad_lane == 79, NEGATIVE, 0.0).astype(BF)

    def window(w, carry):
        rows = pl.ds(pl.multiple_of(w * padded, 16), padded)
        qk = qk_ref[rows, :]
        vv = vv_ref[rows, :]
        spread = nn(qk[:, :256], table_ref[0]) + nn(qk[:, :256], table_ref[1])
        wide = qk.astype(F32)
        wide_v = vv.astype(F32)
        parts = [wide[:, :128], wide[:, 128:256], wide[:, 256:384]]
        turned = [pltpu.roll(part, 64, 1) for part in parts]
        queries = [parts[0], turned[0], parts[1]]
        keys_low = [turned[1], parts[2], turned[2]]
        values = [wide_v[:, :128], pltpu.roll(wide_v[:, :128], 64, 1), wide_v[:, 128:256]]
        key_feat = key_feat_ref[rows, :].astype(F32)
        ones = jnp.where((lane == 64) | (lane == 65), 1.0, 0.0)
        outs = []
        for head in range(3):
            for slot in duties:
                if slot % 3 == head:
                    for act in duties[slot]:
                        pl.when(step * windows + w == slot // 3)(act)
            moved = shift_lanes(spread[:, head * 128 : head * 128 + 128], amounts, True)
            high = moved.astype(BF).astype(F32)
            rest = pltpu.roll(moved - high, 16, 1)
            feat = jnp.where(field < 16, high, rest)
            feat = jnp.where(field < 14, feat, jnp.where((field >= 16) & (field < 30), feat, 0.0))
            feat = jnp.where(lane == 79, 1.0, feat)
            query = jnp.where(low, queries[head] * 0.125, feat)
            key_ref[0, head, w, :padded, :] = jnp.where(low, keys_low[head], key_feat).astype(BF)
            key_ref[0, head, w, padded:, :] = pad_key
            value_ref[0, head, w, :padded, :] = jnp.where(low, values[head], ones).astype(BF)
            value_ref[0, head, w, padded:, :] = jnp.zeros((keys - padded, 128), BF)
            scores = nt(query.astype(BF), key_ref[0, head, w])
            top = jnp.max(scores, -1, keepdims=True)
            expo = jnp.exp(scores - top).astype(BF)
            mixed = nn(expo, value_ref[0, head, w])
            total = mixed[:, 64:65]
            outs.append(mixed / total)
            logsum = -(top + jnp.log(total))
            first = logsum.astype(BF).astype(F32)
            second = (logsum - first).astype(BF).astype(F32)
            third = logsum - first - second
            query = jnp.where(lane == 78, first, query)
            query = jnp.where(lane == 94, second, query)
            query = jnp.where(lane == 95, third, query)
            query_ref[0, head, rows, :] = query.astype(BF)
        out_ref[0, rows, :128] = jnp.where(low, 0.0, pltpu.roll(outs[0], 64, 1)).astype(BF)
        out_ref[0, rows, 128:] = jnp.where(low, outs[1], pltpu.roll(outs[2], 64, 1)).astype(BF)
        return carry

    lax.fori_loop(0, windows, window, 0)
    acc_ref[...] += nt(out_ref[0], flat(w_ref[:, chunk, 1])[:, 128:])
    if linked:

        @pl.when(step == pl.num_programs(0) - 1)
        def _():
            for slot in duties:
                if slot >= 48:
                    for act in duties[slot]:
                        act()
            mlp.arrive()
            mine.wait()
            keep.wait()
            att.finish()
            mlp.finish()


def mlp_kernel(
    x_ref, attn_ref, cotangent_ref, slots_ref, w_ref, bias_proj_ref, gain_ref, shift_ref, bias_down_ref, bias_up_ref,
    result_ref, gx1_ref, grad_ref, gbias_up_ref, small_ref,
    x1_ref, h2_ref, h2t_ref, gyt_ref, y_ref, dh_ref, gy_ref, bias_ref,
    *, windows, padded,
):
    first = lax.axis_index("tensor") * windows
    columns = w_ref.shape[4]
    step = pl.program_id(0)
    last = pl.num_programs(0) - 1

    @pl.when(step == 0)
    def _():
        for w in range(windows):
            spread_rows(cotangent_ref, gy_ref, w, cotangent_ref.shape[0] // windows, padded, alive_of(slots_ref, first + w))
        x1 = x_ref[...].astype(F32) + (attn_ref[...] + row(bias_proj_ref))
        x1_ref[...] = x1
        normed, _ = normed_of(x1)
        h2 = (normed * row(gain_ref) + row(shift_ref)).astype(BF)
        for tile in range(bias_ref.shape[0]):
            bias_ref[tile] = row(bias_up_ref)[:, tile * columns : tile * columns + columns]
        h2_ref[...] = h2
        h2t_ref[...] = h2.T
        gyt_ref[...] = gy_ref[...].T
        y_ref[...] = jnp.zeros_like(y_ref)
        dh_ref[...] = jnp.zeros_like(dh_ref)

    up, down = flat(w_ref[:, 0, 0]), flat(w_ref[:, 0, 1])
    strips = (grad_ref.shape[0], grad_ref.shape[3], columns)
    upper = nn(h2_ref[...], up) + bias_ref[step]
    half = 0.5 * (1.0 + lax.erf(upper * np.float32(np.sqrt(0.5))))
    slope = half + upper * (np.float32(1.0 / np.sqrt(2 * np.pi)) * jnp.exp(-0.5 * upper * upper))
    active = (upper * half).astype(BF)
    grad_upper = (nn(gy_ref[...], down) * slope).astype(BF)
    y_ref[...] += nt(active, down)
    dh_ref[...] += nt(grad_upper, up)
    grad_ref[:, 0, 1] = nn(gyt_ref[...], active).astype(BF).reshape(strips)
    grad_ref[:, 0, 0] = nn(h2t_ref[...], grad_upper).astype(BF).reshape(strips)
    gbias_up_ref[0] = jnp.sum(grad_upper.astype(F32), 0, keepdims=True)

    @pl.when(step == last)
    def _():
        x1 = x1_ref[...]
        result = x1 + (y_ref[...] + row(bias_down_ref))
        length = result_ref.shape[0] // windows
        for w in range(windows):
            part = alive_of(slots_ref, first + w) * result[w * padded : w * padded + length]
            result_ref[w * length : w * length + length, :] = part.astype(BF)
        normed, inverse = normed_of(x1)
        gy = gy_ref[...].astype(F32)
        dh = dh_ref[...]
        gx1_ref[...] = gy + norm_back(dh, normed, inverse, row(gain_ref))
        small_ref[0:1, :] = jnp.sum(dh * normed, 0, keepdims=True)
        small_ref[1:2, :] = jnp.sum(dh, 0, keepdims=True)
        small_ref[2:3, :] = jnp.sum(gy, 0, keepdims=True)
        small_ref[3:8, :] = jnp.zeros_like(small_ref[3:8, :])


def attend_back_kernel(*refs, windows, padded, keys, size, linked):
    step = pl.program_id(0)
    last = pl.num_programs(0) - 1
    scatter = None
    if linked:
        scatter = make_scatter(refs[11], refs[17], refs[27:])
        refs = refs[:11] + refs[12:17] + refs[18:27]
        pl.when(step == 0)(scatter.begin)
    (
        x_ref, gx1_ref, w_ref, gain_ref, shift_ref, rel_ref, amount_ref,
        query_ref, key_ref, value_ref, out_ref,
        grad_x_ref, grad_ref, small_ref, gbias_ref, grel_ref,
        h1t_ref, gbt_ref, gb_ref, dh_ref, do_ref, gqk_ref, gv_ref, spread_ref, table_ref,
    ) = refs

    @pl.when(step == 0)
    def _():
        normed, _ = normed_of(x_ref[...].astype(F32))
        h1t_ref[...] = (normed * row(gain_ref) + row(shift_ref)).astype(BF).T
        span = 2 * size - 1
        place = lax.broadcasted_iota(jnp.int32, (64, 128), 0)
        wanted = jnp.where(place < span, span - 1 - place, jnp.where(place < 2 * span, 32 + 2 * span - 1 - place, -1))
        chosen = jnp.where((lanes_of((64, 128)) & 63) == wanted, 1.0, 0.0).astype(BF)
        table_ref[...] = tn(chosen, rel_ref[...].astype(BF)).astype(BF)
        gb = gx1_ref[...].astype(BF)
        gb_ref[...] = gb
        gbt_ref[...] = gb.T
        dh_ref[...] = jnp.zeros_like(dh_ref)
        grel_ref[...] = jnp.zeros_like(grel_ref)
        small_ref[0:1, :] = jnp.sum(gb.astype(F32), 0, keepdims=True)

    do_ref[...] = nn(gb_ref[...], flat(w_ref[:, 0, 1])[:, 128:]).astype(BF)
    lane = lanes_of((padded, 128))
    low = lane < 64
    field = lane & 31
    amounts = amount_ref[...]
    kept = (lane >= 64) & (field < 14)

    def window(w, carry):
        rows = pl.ds(pl.multiple_of(w * padded, 16), padded)
        do = do_ref[rows, :].astype(F32)
        out = out_ref[0, rows, :].astype(F32)
        product = do * out
        grads = [pltpu.roll(do[:, :128], 64, 1), do[:, 128:], pltpu.roll(do[:, 128:], 64, 1)]
        sums = [
            jnp.sum(jnp.where(low, 0.0, product[:, :128]), -1, keepdims=True),
            jnp.sum(jnp.where(low, product[:, 128:], 0.0), -1, keepdims=True),
            jnp.sum(jnp.where(low, 0.0, product[:, 128:]), -1, keepdims=True),
        ]
        gq, gk, gv = [], [], []
        for head in range(3):
            if linked:
                for slot, act in zip(SUM_SLOTS, scatter.steps):
                    if slot % 3 == head:
                        pl.when(step * windows + w == slot // 3)(act)
            delta = -sums[head]
            first = delta.astype(BF).astype(F32)
            grad_out = jnp.where(low, grads[head], jnp.where(lane == 64, first, jnp.where(lane == 65, delta - first, 0.0))).astype(BF)
            query, key, value = query_ref[0, head, rows, :], key_ref[0, head, w], value_ref[0, head, w]
            prob = jnp.exp(nt(query, key))
            grad_scores = (prob * nt(grad_out, value)).astype(BF)
            gv.append(tn(prob.astype(BF), grad_out)[:padded])
            gk.append(tn(grad_scores, query)[:padded])
            both = nn(grad_scores, key)
            back = shift_lanes(jnp.where(kept, both, 0.0), amounts, False)
            high = back.astype(BF).astype(F32)
            pack = jnp.where(low, pltpu.roll(back - high, 64, 1), high).astype(BF)
            spread_ref[head, rows, :] = pack
            gq.append(both * 0.125 + nn(pack, table_ref[...]))
        gqk_ref[rows, :128] = jnp.where(low, gq[0], pltpu.roll(gq[1], 64, 1)).astype(BF)
        gqk_ref[rows, 128:256] = jnp.where(low, gq[2], pltpu.roll(gk[0], 64, 1)).astype(BF)
        gqk_ref[rows, 256:] = jnp.where(low, gk[1], pltpu.roll(gk[2], 64, 1)).astype(BF)
        gv_ref[rows, :128] = jnp.where(low, gv[0], pltpu.roll(gv[1], 64, 1)).astype(BF)
        gv_ref[rows, 128:] = jnp.where(low, gv[2], 0.0).astype(BF)
        return carry

    lax.fori_loop(0, windows, window, 0)
    for head in range(3):
        grel_ref[...] += tn(spread_ref[head], query_ref[0, head])
    gqk, gv = gqk_ref[...], gv_ref[...]
    gbias_ref[0, :, :384] = jnp.sum(gqk.astype(F32), 0, keepdims=True)
    gbias_ref[0, :, 384:] = jnp.sum(gv.astype(F32), 0, keepdims=True)
    dh_ref[...] += nt(gqk, flat(w_ref[:, 0, 0])) + nt(gv, flat(w_ref[:, 0, 1])[:, :256])
    h1t = h1t_ref[...]
    strips = (grad_ref.shape[0], grad_ref.shape[3], -1)
    grad_ref[:, 0, 0] = nn(h1t, gqk).astype(BF).reshape(strips)
    one, two = nn(h1t, gv), nn(gbt_ref[...], out_ref[0])
    grad_ref[:, 0, 1, :, :128] = one[:, :128].astype(BF).reshape(strips)
    grad_ref[:, 0, 1, :, 128:256] = (one[:, 128:] + two[:, :128]).astype(BF).reshape(strips)
    grad_ref[:, 0, 1, :, 256:] = two[:, 128:].astype(BF).reshape(strips)

    @pl.when(step == last)
    def _():
        normed, inverse = normed_of(x_ref[...].astype(F32))
        dh = dh_ref[...]
        grad_x = (gx1_ref[...] + norm_back(dh, normed, inverse, row(gain_ref))).astype(BF)
        length = grad_x_ref.shape[0] // windows
        for w in range(windows):
            grad_x_ref[w * length : w * length + length, :] = grad_x[w * padded : w * padded + length]
        small_ref[1:2, :] = jnp.sum(dh * normed, 0, keepdims=True)
        small_ref[2:3, :] = jnp.sum(dh, 0, keepdims=True)
        small_ref[3:8, :] = jnp.zeros_like(small_ref[3:8, :])
        if linked:
            for slot, act in zip(SUM_SLOTS, scatter.steps):
                if slot >= 48:
                    act()
            scatter.finish()


def unpack_kernel(
    total_ref, att_ref, mlp_ref,
    qkv_ref, proj_ref, up_ref, down_ref, gain1_ref, shift1_ref, q_ref, v_ref, rel_h_ref, rel_w_ref,
    proj_bias_ref, gain2_ref, shift2_ref, up_bias_ref, down_bias_ref,
    *, span,
):
    qkv_ref[0] = att_ref[0, :, :192]
    qkv_ref[1] = att_ref[0, :, 192:]
    qkv_ref[2] = att_ref[1, :, :192]
    proj_ref[...] = att_ref[1, :, 192:].T
    up_ref[...] = mlp_ref[0]
    down_ref[...] = mlp_ref[1]
    for first, ref in ((0, proj_bias_ref), (6, gain1_ref), (12, shift1_ref), (18, gain2_ref), (24, shift2_ref), (30, down_bias_ref), (56, up_bias_ref)):
        for lane in range(0, ref.shape[0], 128):
            ref[pl.ds(lane, 128)] = total_ref[first + lane // 128]
    for start, ref in ((36, q_ref), (39, v_ref)):
        pieces = []
        for t in range(ref.shape[0] // 192):
            first = start + 5 * t
            pieces.append((total_ref[first : first + 1, :], total_ref[first + 1 : first + 2, :]))
        for pair in range(len(pieces) // 2):
            one, two = pieces[2 * pair], pieces[2 * pair + 1]
            low = lanes_of((1, 128)) < 64
            turned = [pltpu.roll(jnp.broadcast_to(v, (8, 128)), 64, 1)[:1] for v in two]
            parts = [one[0], jnp.where(low, one[1], turned[0]), jnp.where(low, turned[0], turned[1])]
            for i, values in enumerate(parts):
                ref[pl.ds(pair * 384 + i * 128, 128)] = values[0]
    rel = total_ref[total_ref.shape[0] - 64 :, :]
    high = rel.astype(BF)
    middle = (rel - high.astype(F32)).astype(BF)
    rest = (rel - high.astype(F32) - middle.astype(F32)).astype(BF)
    for ref, first in ((rel_h_ref, 0), (rel_w_ref, 32)):
        place = lax.broadcasted_iota(jnp.int32, (32, 64), 0)
        chosen = jnp.where(lanes_of((32, 64)) == first + span - 1 - place, 1.0, 0.0).astype(BF)
        values = nn(chosen, high) + nn(chosen, middle) + nn(chosen, rest)
        ref[...] = 8.0 * values[:span, :64]


def whole(shape):
    return pl.BlockSpec(shape, lambda *index: (0,) * len(shape))


def once(shape):
    return pl.BlockSpec(shape, lambda *index: (0,) * len(shape), pipeline_mode=pl.Buffered(1))


def shards(
    block_input, cotangent, pad_mask, slot_window, qkv_w, proj_w, fc1_w, fc2_w,
    norm1_gain, norm1_bias, q_bias, v_bias, rel_h, rel_w, proj_bias,
    norm2_gain, norm2_bias, fc1_bias, fc2_bias,
):
    part = lax.axis_index("tensor")
    count_dp, count_t = lax.axis_size("dp"), lax.axis_size("tensor")
    length = pad_mask.shape[1]
    local_rows, width = block_input.shape
    windows = local_rows // length
    size = rel_h.shape[0] // 2 + 1
    padded = -(-length // 16) * 16
    keys = -(-length // 128) * 128
    rows = windows * padded
    strip = width // count_dp

    slots = jnp.pad(slot_window, (0, 128 - slot_window.shape[0]), constant_values=-1).reshape(1, 128)
    rel = jnp.pad(jnp.concatenate([rel_h, rel_w]), ((0, 64 - 2 * rel_h.shape[0]), (0, 64)))

    place = np.arange(padded)
    row_of, col_of = place // size, place % size
    inside = place < length
    amount = np.zeros((padded, 128), np.int32)
    amount[:, :] = np.where(
        (np.arange(128) % 64 < 32)[None, :], (size - 1 - row_of)[:, None], (size - 1 - col_of)[:, None]
    ) * inside[:, None]
    amount = jnp.asarray(amount)
    feat = np.zeros((padded, 128), np.float32)
    for a in range(size):
        for base, pos in ((64, row_of), (96, col_of)):
            feat[:, base + a] = (pos == a) & inside
            feat[:, base + 16 + a] = (pos == a) & inside
    feat[:, [78, 94, 95]] = 1.0
    feat[:, 79] = np.where(inside, 0.0, NEGATIVE)
    feat = jnp.asarray(feat.astype(BF))
    span = rel_h.shape[0]

    q_w, k_w, v_w = qkv_w[0], qkv_w[1], qkv_w[2]
    shard_att = jnp.stack([jnp.concatenate([q_w, k_w], 1), jnp.concatenate([v_w, proj_w.T], 1)])
    shard_mlp = jnp.stack([fc1_w, fc2_w.T])
    columns = fc1_w.shape[1]
    linked = count_dp == 8 and count_t == 4 and strip % 16 == 0 and windows == 4
    any_spec, vmem_spec = pl.BlockSpec(memory_space=pl.ANY), pl.BlockSpec(memory_space=pltpu.VMEM)
    blocks, depth = (count_dp, strip) if linked else (1, width)

    def talk(number, **more):
        return pltpu.CompilerParams(
            vmem_limit_bytes=VMEM_LIMIT, collective_id=number, has_side_effects=True, **more)

    def gather_all(pieces):
        every = lax.all_gather(pieces, AXES, axis=0, tiled=False).reshape(count_dp, count_t, *pieces.shape)
        return every.transpose(1, 2, 0, 3, 4).reshape(1, count_t, 2, width, pieces.shape[2])

    if not linked:
        w_att, w_mlp = gather_all(shard_att), gather_all(shard_mlp)

    vec = once((width,))
    params = pltpu.CompilerParams(dimension_semantics=("arbitrary",), vmem_limit_bytes=VMEM_LIMIT)

    query, key, value, out, attn, x, *rest = pl.pallas_call(
        partial(attend_kernel, windows=windows, padded=padded, keys=keys, size=size, linked=linked),
        grid=(count_t,),
        in_specs=[
            once((local_rows, width)),
        ] + [pl.BlockSpec((blocks, 1, 2, depth, 384), lambda t: (0, t, 0, 0, 0))] * (not linked) + [
            vec, vec, vec, vec, once((64, 128)), once((1, 128)), once(pad_mask.shape[::-1]),
            once((padded, 128)), once((padded, 128)),
        ] + [once((2, strip, 384)), once((2, strip, columns))] * linked,
        out_specs=[
            pl.BlockSpec((1, 3, rows, 128), lambda t: (t, 0, 0, 0)),
            pl.BlockSpec((1, 3, windows, keys, 128), lambda t: (t, 0, 0, 0, 0)),
            pl.BlockSpec((1, 3, windows, keys, 128), lambda t: (t, 0, 0, 0, 0)),
            pl.BlockSpec((1, rows, 256), lambda t: (t, 0, 0)),
            whole((rows, width)), whole((rows, width)),
        ] + [any_spec, any_spec] * linked,
        out_shape=[
            jax.ShapeDtypeStruct((count_t, 3, rows, 128), BF),
            jax.ShapeDtypeStruct((count_t, 3, windows, keys, 128), BF),
            jax.ShapeDtypeStruct((count_t, 3, windows, keys, 128), BF),
            jax.ShapeDtypeStruct((count_t, rows, 256), BF),
            jax.ShapeDtypeStruct((rows, width), F32),
            jax.ShapeDtypeStruct((rows, width), BF),
        ] + [jax.ShapeDtypeStruct((count_dp, count_t, 2, strip, n), BF) for n in (384, columns)] * linked,
        scratch_shapes=[
            pltpu.VMEM((rows, width), BF), pltpu.VMEM((rows, 384), BF), pltpu.VMEM((rows, 256), BF),
            pltpu.VMEM((2, 256, 384), BF), pltpu.VMEM((rows, 128), BF), pltpu.VMEM((count_t, 1, 640), F32),
        ]
        + ([pltpu.VMEM((count_dp, count_t, 2, strip, 384), BF)] + gather_scratch() * 2 + [pltpu.SemaphoreType.DMA((2,))]) * linked,
        compiler_params=talk(2, dimension_semantics=("arbitrary",)) if linked else params,
        name="attend",
    )(
        block_input, *([] if linked else [w_att]), norm1_gain, norm1_bias, q_bias, v_bias, rel, slots, pad_mask.T, feat, amount,
        *([shard_att, shard_mlp] * linked)
    )
    if linked:
        w_att, w_mlp = rest

    mlp_block = pl.BlockSpec((blocks, 1, 2, depth, columns), lambda j: (0, j, 0, 0, 0))
    result, gx1, grad_mlp, gbias_up, small2 = pl.pallas_call(
        partial(mlp_kernel, windows=windows, padded=padded),
        grid=(count_t,),
        in_specs=[
            once((rows, width)), once((rows, width)), once((local_rows, width)), once((1, 128)),
            mlp_block, vec, vec, vec, vec, once(fc1_bias.shape),
        ],
        out_specs=[
            whole((local_rows, width)), whole((rows, width)),
            mlp_block,
            pl.BlockSpec((1, 1, columns), lambda j: (j, 0, 0)),
            whole((8, width)),
        ],
        out_shape=[
            jax.ShapeDtypeStruct((local_rows, width), BF),
            jax.ShapeDtypeStruct((rows, width), F32),
            jax.ShapeDtypeStruct((blocks, count_t, 2, depth, columns), BF),
            jax.ShapeDtypeStruct((count_t, 1, columns), F32),
            jax.ShapeDtypeStruct((8, width), F32),
        ],
        scratch_shapes=[
            pltpu.VMEM((rows, width), F32), pltpu.VMEM((rows, width), BF),
            pltpu.VMEM((width, rows), BF), pltpu.VMEM((width, rows), BF),
            pltpu.VMEM((rows, width), F32), pltpu.VMEM((rows, width), F32), pltpu.VMEM((rows, width), BF),
            pltpu.VMEM((count_t, 1, columns), F32),
        ],
        compiler_params=params,
        name="mlp",
    )(x, attn, cotangent, slots, w_mlp, proj_bias, norm2_gain, norm2_bias, fc2_bias, fc1_bias)

    grad_x, grad_att, small1, gbias_att, grel, *rest = pl.pallas_call(
        partial(attend_back_kernel, windows=windows, padded=padded, keys=keys, size=size, linked=linked),
        grid=(count_t,),
        in_specs=[
            once((rows, width)), once((rows, width)),
            pl.BlockSpec((blocks, 1, 2, depth, 384), lambda t: (0, t, 0, 0, 0)),
            vec, vec, once((64, 128)), once((padded, 128)),
            pl.BlockSpec((1, 3, rows, 128), lambda t: (t, 0, 0, 0)),
            pl.BlockSpec((1, 3, windows, keys, 128), lambda t: (t, 0, 0, 0, 0)),
            pl.BlockSpec((1, 3, windows, keys, 128), lambda t: (t, 0, 0, 0, 0)),
            pl.BlockSpec((1, rows, 256), lambda t: (t, 0, 0)),
        ] + [any_spec] * linked,
        out_specs=[
            whole((local_rows, width)),
            pl.BlockSpec((blocks, 1, 2, depth, 384), lambda t: (0, t, 0, 0, 0)),
            whole((8, width)),
            pl.BlockSpec((1, 1, 640), lambda t: (t, 0, 0)),
            whole((128, 128)),
        ] + [whole((2, strip, columns))] * linked,
        out_shape=[
            jax.ShapeDtypeStruct((local_rows, width), BF),
            jax.ShapeDtypeStruct((blocks, count_t, 2, depth, 384), BF),
            jax.ShapeDtypeStruct((8, width), F32),
            jax.ShapeDtypeStruct((count_t, 1, 640), F32),
            jax.ShapeDtypeStruct((128, 128), F32),
        ] + [jax.ShapeDtypeStruct((2, strip, columns), F32)] * linked,
        scratch_shapes=[
            pltpu.VMEM((width, rows), BF), pltpu.VMEM((width, rows), BF), pltpu.VMEM((rows, width), BF),
            pltpu.VMEM((rows, width), F32), pltpu.VMEM((rows, 256), BF),
            pltpu.VMEM((rows, 384), BF), pltpu.VMEM((rows, 256), BF), pltpu.VMEM((3, rows, 128), BF),
            pltpu.VMEM((128, 128), BF),
        ] + (scatter_scratch(2, strip, columns) if linked else []),
        compiler_params=talk(3, dimension_semantics=("arbitrary",)) if linked else params,
        name="attend_back",
    )(
        x, gx1, w_att, norm1_gain, norm1_bias, rel, amount, query, key, value, out,
        *([grad_mlp.reshape(count_dp // 2, 2, count_t, 2, strip, columns)] * linked if linked else [])
    )

    if linked:
        sum_mlp = rest[0]
        count = 36 + 5 * count_t + fc1_bias.shape[0] // 128 + 64
        sum_att, total = pl.pallas_call(
            reduce_kernel,
            in_specs=[any_spec] + [vmem_spec] * 5, out_specs=[vmem_spec, vmem_spec],
            out_shape=[jax.ShapeDtypeStruct((2, strip, 384), F32), jax.ShapeDtypeStruct((count, 128), F32)],
            scratch_shapes=[
                pltpu.VMEM((count, 128), F32), pltpu.VMEM((10, count, 128), F32),
                pltpu.SemaphoreType.DMA((5,)), pltpu.SemaphoreType.DMA((5,)),
            ] + scatter_scratch(2, strip, 384),
            compiler_params=talk(4),
            name="reduce_attention",
        )(grad_att.reshape(count_dp // 2, 2, count_t, 2, strip, 384), small1, small2, gbias_att, gbias_up, grel)
        like = (
            qkv_w, proj_w, fc1_w, fc2_w.T, norm1_gain, norm1_bias, q_bias, v_bias, rel_h, rel_w,
            proj_bias, norm2_gain, norm2_bias, fc1_bias, fc2_bias,
        )
        shapes = [jax.ShapeDtypeStruct(v.shape, F32) for v in like]
        outs = pl.pallas_call(
            partial(unpack_kernel, span=span),
            in_specs=[vmem_spec] * 3, out_specs=[vmem_spec] * len(shapes), out_shape=shapes,
            compiler_params=pltpu.CompilerParams(vmem_limit_bytes=VMEM_LIMIT),
            name="unpack",
        )(total, sum_att, sum_mlp)
        return (result, grad_x, *outs[:3], outs[3].T, *outs[4:])
    parts = [
        small1[:3].reshape(-1, 128), small2[:3].reshape(-1, 128), gbias_att.reshape(-1, 128), gbias_up.reshape(-1, 128), grel[64:],
    ]
    def scatter_all(grads):
        grads = grads.reshape(count_t, 2, count_dp, strip, grads.shape[4]).transpose(2, 0, 1, 3, 4)
        grads = grads.reshape(count_dp * count_t, *grads.shape[2:])
        return lax.psum_scatter(grads, AXES, scatter_dimension=0, tiled=False).astype(F32)

    sum_mlp, sum_att = scatter_all(grad_mlp), scatter_all(grad_att)
    small = lax.psum(jnp.concatenate(parts), AXES)
    cuts = np.cumsum([part.shape[0] for part in parts])[:-1]
    small1, small2, gbias_att, gbias_up, grad_rel = jnp.split(small, cuts)
    small1, small2 = small1.reshape(3, width), small2.reshape(3, width)
    gbias_att = gbias_att.reshape(count_t, 1, 640)
    grad_rel = 8.0 * grad_rel[:, :64]
    head_q, head_k = sum_att[0, :, :192], sum_att[0, :, 192:]
    head_v, head_p = sum_att[1, :, :192], sum_att[1, :, 192:]
    return (
        result,
        grad_x,
        jnp.stack([head_q, head_k, head_v]),
        head_p.T,
        sum_mlp[0],
        sum_mlp[1].T,
        small1[1],
        small1[2],
        gbias_att[:, 0, :192].reshape(-1),
        gbias_att[:, 0, 384:576].reshape(-1),
        grad_rel[:span][::-1],
        grad_rel[32 : 32 + span][::-1],
        small1[0],
        small2[0],
        small2[1],
        gbias_up.reshape(-1),
        small2[2],
    )


def solution(mesh):
    return jax.shard_map(
        shards,
        mesh=mesh,
        in_specs=(
            P(AXES, None), P(AXES, None), P(), P("dp"),
            P(None, "dp", "tensor"), P("tensor", "dp"), P("dp", "tensor"), P("tensor", "dp"),
        )
        + (P(),) * 11,
        out_specs=(
            P(AXES, None), P(AXES, None),
            P(None, "dp", "tensor"), P("tensor", "dp"), P("dp", "tensor"), P("tensor", "dp"),
        )
        + (P(),) * 11,
        check_vma=False,
    )
```

```python
from functools import partial

import jax
import jax.numpy as jnp
import numpy as np
from jax import lax
from jax.experimental import pallas as pl
from jax.experimental.pallas import tpu as pltpu
from jax.sharding import PartitionSpec as P

HD = 64
EPSILON = 1e-06
NEGATIVE = -1e30
F32, BF = jnp.float32, jnp.bfloat16
AXES = ("dp", "tensor")
VMEM_LIMIT = 60 * 1024 * 1024
MLP_BEGIN = 11
MLP_SLOTS = tuple(range(3, 48, 3))
SUM_SLOTS = (3, 3, 6, 6, 12, 15, 18, 21, 21, 24, 24, 27, 27, 30, 30, 33, 36, 39, 39)

FOLDS = (3, 6, 9, 12, 15)


def nn(left, right):
    return lax.dot_general(left, right, (((1,), (0,)), ((), ())), preferred_element_type=F32)


def nt(left, right):
    return lax.dot_general(left, right, (((1,), (1,)), ((), ())), preferred_element_type=F32)


def tn(left, right):
    return lax.dot_general(left, right, (((0,), (0,)), ((), ())), preferred_element_type=F32)


def normed_of(values):
    center = values - jnp.mean(values, -1, keepdims=True)
    inverse = lax.rsqrt(jnp.mean(center * center, -1, keepdims=True) + EPSILON)
    return center * inverse, inverse


def norm_back(grad, normed, inverse, gain):
    scaled = grad * gain
    inner = (
        scaled
        - jnp.mean(scaled, -1, keepdims=True)
        - normed * jnp.mean(scaled * normed, -1, keepdims=True)
    )
    return inverse * inner


def spread_rows(source_ref, target_ref, w, length, padded, live=None):
    tail = w * padded + length // 16 * 16
    target_ref[tail : w * padded + padded, :] = jnp.zeros((w * padded + padded - tail, target_ref.shape[1]), target_ref.dtype)
    values = source_ref[w * length : w * length + length, :]
    if live is not None:
        values = jnp.where(live > 0.5, values.astype(F32), 0.0).astype(values.dtype)
    target_ref[w * padded : w * padded + length, :] = values


def row(ref):
    return ref[...].reshape(1, -1)


def flat(values):
    return values.reshape(-1, values.shape[-1])


def lanes_of(shape):
    return lax.broadcasted_iota(jnp.int32, shape, 1)


def of_slot(values, slot):
    return jnp.sum(jnp.where(lanes_of(values.shape) == slot, values, 0.0), -1, keepdims=True)


def alive_of(slots_ref, slot):
    return of_slot(jnp.where(slots_ref[...] >= 0, 1.0, 0.0), slot)


def shift_lanes(values, amounts, left):
    for bit in (1, 2, 4, 8):
        moved = pltpu.roll(values, 128 - bit if left else bit, 1)
        values = jnp.where((amounts & bit) != 0, moved, values)
    return values


MESH = pl.DeviceIdType.MESH


class Place:
    def __init__(self, height):
        self.height = height
        self.dp, self.tensor = lax.axis_index("dp"), lax.axis_index("tensor")
        self.z, self.y = lax.div(self.dp, 2), lax.rem(self.dp, 2)
        self.x, self.c = lax.div(self.tensor, 2), lax.rem(self.tensor, 2)

    def plane(self, colour, a, b):
        return lax.rem(self.y + (1 - colour) * b + colour * a, 2), lax.rem(self.x + (1 - colour) * a + colour * b, 2)

    def shard(self, colour, a, b, z):
        y, x = self.plane(colour, a, b)
        return z * 2 + y, x * 2 + colour

    def near(self, k):
        upper = lax.div(self.z, self.height // 2)
        zz = self.z + upper * (self.height - 1 - 2 * self.z)
        q = (zz, 1 - zz, 2, 3)[k]
        return q + upper * (self.height - 1 - 2 * q)

    def peer(self, kind):
        if kind == "core":
            return self.dp, self.x * 2 + 1 - self.c
        if kind in ("z1", "z2", "z3"):
            return self.near(int(kind[1])) * 2 + self.y, self.tensor
        if kind == "up":
            return self.dp + 2, self.tensor
        if kind == "down":
            return self.dp - 2, self.tensor
        if kind == "y":
            return self.z * 2 + 1 - self.y, self.tensor
        if kind == "x":
            return self.dp, (1 - self.x) * 2 + self.c
        if kind == "pair":
            return (self.z + 1 - 2 * lax.rem(self.z, 2)) * 2 + self.y, self.tensor
        if kind == "half":
            return lax.rem(self.z + 2, 4) * 2 + self.y, self.tensor
        return self.shard(self.c, int(kind == "far"), int(kind == "near"), self.z)

    def has(self, kind):
        if kind == "up":
            return self.z < self.height - 1
        if kind == "down":
            return self.z > 0
        return None

    def greet(self):
        barrier = pltpu.get_barrier_semaphore()
        for kind in ("core", "near", "far", "z1", "z2", "z3"):
            pl.semaphore_signal(barrier, inc=1, device_id=self.peer(kind), device_id_type=MESH)
        pl.semaphore_wait(barrier, 6)


def under(condition, action):
    if condition is None:
        action()
    else:
        pl.when(condition)(action)


def both(one, two):
    return two if one is None else one if two is None else jnp.logical_and(one, two)


class Gather:
    SENDS = 36

    def __init__(self, at, own_ref, all_ref, send_sem, recv_sem, first=0, count=None):
        self.at, self.own_ref = at, own_ref
        self.all_ref = all_ref if count is None else all_ref.at[:, :, first : first + count]
        self.send_sem, self.recv_sem = send_sem, recv_sem
        z = [lambda k=k: self.step(("z", k)) for k in range(4)]
        near = [lambda k=k: self.step(("near", k)) for k in range(4)]
        far = [[lambda b=b, k=k: self.step(("far", b, k)) for k in range(4)] for b in range(2)]
        self.steps = [
            near[0], z[1], far[0][0], near[1], far[1][0], z[2], far[0][1],
            near[2], far[1][1], z[3], far[0][2], near[3], far[1][2], far[0][3], far[1][3],
        ]
        slot = 0
        self.slots = {}
        for key in [("z", k) for k in range(4)] + [("near", k) for k in range(4)] + [("far", b, k) for b in range(2) for k in range(4)]:
            self.slots[key] = slot
            slot += len(self.kinds(key))

    def kinds(self, key):
        return {"z": ("up", "down", "near", "far", "core"), "near": ("far", "core"), "far": ("core",)}[key[0]]

    def shard(self, key):
        at = self.at
        if key[0] == "z":
            return at.shard(at.c, 0, 0, at.near(key[1]))
        if key[0] == "near":
            return at.shard(at.c, 0, 1, at.near(key[1]))
        return at.shard(at.c, 1, key[1], at.near(key[2]))

    def copy(self, source, shard, kind, slot):
        dp, tensor = shard
        return pltpu.make_async_remote_copy(
            src_ref=source, dst_ref=self.all_ref.at[dp, tensor], send_sem=self.send_sem.at[slot],
            recv_sem=self.recv_sem.at[dp * 4 + tensor], device_id=self.at.peer(kind), device_id_type=MESH)

    def sends(self, key):
        shard = self.shard(key)
        source = self.own_ref if key == ("z", 0) else self.all_ref.at[shard[0], shard[1]]
        away = self.at.near(key[1]) - self.at.z if key[0] == "z" else 0
        sends = []
        for i, kind in enumerate(self.kinds(key)):
            condition = self.at.has(kind)
            if kind in ("up", "down"):
                condition = jnp.logical_and(condition, away <= 0 if kind == "up" else away >= 0)
            sends.append((condition, self.copy(source, shard, kind, self.slots[key] + i)))
        return sends

    def take(self, shard):
        self.copy(self.all_ref.at[shard[0], shard[1]], shard, "core", 0).wait_recv()

    def begin(self):
        for condition, copy in self.sends(("z", 0)):
            under(condition, copy.start)

    def step(self, key):
        self.take(self.shard(key))
        for condition, copy in self.sends(key):
            under(condition, copy.start)

    def arrive(self):
        at = self.at
        for a in range(2):
            for b in range(2):
                for k in range(4):
                    self.take(at.shard(1 - at.c, a, b, at.near(k)))

    def finish(self):
        for key in self.slots:
            for condition, copy in self.sends(key):
                under(condition, copy.wait_send)


def gather_scratch():
    return [pltpu.SemaphoreType.DMA((Gather.SENDS,)), pltpu.SemaphoreType.DMA((32,))]


class Scatter:
    def __init__(self, all_ref, own_ref, held, core_in, far_in, near_in, up_in, down_in, sems, height=4):
        self.all_ref, self.own_ref, self.held, self.core_in = all_ref, own_ref, held, core_in
        self.far_in, self.near_in, self.up_in, self.down_in, self.sems = far_in, near_in, up_in, down_in, sems
        self.at = Place(height)
        core = {(a, b): (lambda a=a, b=b: self.from_core(a, b)) for a in range(2) for b in range(2)}
        far = [[lambda b=b, k=k: self.from_far(b, k) for k in range(4)] for b in range(2)]
        near = [lambda k=k: self.from_near(k) for k in range(4)]
        line = [lambda k=k: self.from_line(k) for k in range(4)]
        self.steps = [
            core[1, 1], core[1, 0], core[0, 1], core[0, 0], far[1][3], far[0][3], far[1][2], near[3], far[0][2], line[3],
            far[1][1], near[2], far[0][1], line[2], far[1][0], near[1], far[0][0], line[1], near[0],
        ]
        self.last = line[0]

    def remote(self, source, target, name, index, kind):
        send, recv = self.sems[name]
        return pltpu.make_async_remote_copy(
            src_ref=source, dst_ref=target, send_sem=send.at[index], recv_sem=recv.at[index],
            device_id=self.at.peer(kind), device_id_type=MESH)

    def core_copy(self, a, b):
        at = self.at
        y, x = at.plane(1 - at.c, a, b)
        source = self.all_ref.at[:, y, x * 2 + 1 - at.c]
        return self.remote(source, self.core_in.at[a, b], "core", a * 2 + b, "core")

    def local_copy(self, a, b):
        at = self.at
        y, x = at.plane(at.c, a, b)
        return pltpu.make_async_copy(self.all_ref.at[:, y, x * 2 + at.c], self.held.at[a, b], self.sems["local"].at[a * 2 + b])

    def far_copy(self, b, z):
        return self.remote(self.held.at[1, b, z], self.far_in.at[b, z], "far", b * 4 + z, "far")

    def near_copy(self, z):
        return self.remote(self.held.at[0, 1, z], self.near_in.at[z], "near", z, "near")

    def down_copy(self, z):
        return self.remote(self.held.at[0, 0, z], self.down_in.at[z], "down", z, "down")

    def up_copy(self, z):
        return self.remote(self.held.at[0, 0, z], self.up_in.at[z], "up", z, "up")

    def begin(self):
        self.at.greet()
        for a in (1, 0):
            for b in (1, 0):
                self.core_copy(a, b).start()
                self.local_copy(a, b).start()

    def from_core(self, a, b):
        self.local_copy(a, b).wait()
        self.core_copy(a, b).wait_recv()
        for z in range(4):
            self.held[a, b, z] = self.held[a, b, z] + self.core_in[a, b, z]
        if (a, b) == (1, 0):
            for k in (3, 2, 1, 0):
                for side in (1, 0):
                    self.far_copy(side, self.at.near(k)).start()

    def from_far(self, b, k):
        z = self.at.near(k)
        self.far_copy(b, z).wait_recv()
        self.held[0, b, z] = self.held[0, b, z] + self.far_in[b, z]
        if b == 1:
            self.near_copy(z).start()

    def from_near(self, k):
        z = self.at.near(k)
        self.near_copy(z).wait_recv()
        self.held[0, 0, z] = self.held[0, 0, z] + self.near_in[z]

    def from_line(self, k):
        at = self.at
        if k > 0:
            z = at.near(k)

            def downward():
                def add():
                    self.down_copy(z).wait_recv()
                    self.held[0, 0, z] = self.held[0, 0, z] + self.down_in[z]

                under(at.has("up"), add)
                self.down_copy(z).start()

            def upward():
                def add():
                    self.up_copy(z).wait_recv()
                    self.held[0, 0, z] = self.held[0, 0, z] + self.up_in[z]

                under(at.has("down"), add)
                self.up_copy(z).start()

            pl.when(z < at.z)(downward)
            pl.when(z > at.z)(upward)
            return
        self.own_ref[...] = self.held[0, 0, at.z].astype(F32)

        def add_down():
            self.down_copy(at.z).wait_recv()
            self.own_ref[...] += self.down_in[at.z].astype(F32)

        def add_up():
            self.up_copy(at.z).wait_recv()
            self.own_ref[...] += self.up_in[at.z].astype(F32)

        under(at.has("up"), add_down)
        under(at.has("down"), add_up)

    def finish(self):
        at = self.at
        self.last()
        for a in range(2):
            for b in range(2):
                self.core_copy(a, b).wait_send()
        for b in range(2):
            for z in range(4):
                self.far_copy(b, z).wait_send()
        for z in range(4):
            self.near_copy(z).wait_send()
            pl.when(z < at.z)(lambda: self.down_copy(z).wait_send())
            pl.when(z > at.z)(lambda: self.up_copy(z).wait_send())


def scatter_scratch(pieces, strip, columns):
    block = (pieces, strip, columns)
    shapes = [(2, 2, 4), (2, 2, 4), (2, 4), (4,), (4,), (4,)]
    sems = [4, 4, 8, 8, 4, 4, 4, 4, 4, 4, 4]
    return [pltpu.VMEM(lead + block, BF) for lead in shapes] + [pltpu.SemaphoreType.DMA((n,)) for n in sems]


SCATTER_REFS = 17


def make_scatter(all_ref, own_ref, refs):
    held, core_in, far_in, near_in, up_in, down_in = refs[:6]
    core_s, core_r, far_s, far_r, near_s, near_r, up_s, up_r, down_s, down_r, local = refs[6:]
    sems = {
        "core": (core_s, core_r), "far": (far_s, far_r), "near": (near_s, near_r),
        "up": (up_s, up_r), "down": (down_s, down_r), "local": local,
    }
    return Scatter(all_ref, own_ref, held, core_in, far_in, near_in, up_in, down_in, sems)


def packed(refs):
    small1_ref, small2_ref, gbias_att_ref, gbias_up_ref = refs
    places = []
    for ref, rows in ((small1_ref, range(3)), (small2_ref, range(3))):
        places += [(ref, (row, lane)) for row in rows for lane in range(0, ref.shape[1], 128)]
    for ref in (gbias_att_ref, gbias_up_ref):
        places += [(ref, (row, 0, lane)) for row in range(ref.shape[0]) for lane in range(0, ref.shape[2], 128)]
    return places


def reduce_kernel(
    all_ref, small1_ref, small2_ref, gbias_att_ref, gbias_up_ref, grel_ref,
    own_ref, total_ref, small_ref, small_in, small_send, small_recv, *refs,
):
    scatter = make_scatter(all_ref, own_ref, refs)
    at = scatter.at
    rounds = ("core", "y", "x", "pair", "half")

    def exchange(index):
        return pltpu.make_async_remote_copy(
            src_ref=small_ref if index == 0 else small_in.at[5 + index], dst_ref=small_in.at[index],
            send_sem=small_send.at[index], recv_sem=small_recv.at[index],
            device_id=at.peer(rounds[index]), device_id_type=MESH)

    def fold(index):
        exchange(index).wait_recv()
        own = small_ref[...] if index == 0 else small_in[5 + index]
        if index < 4:
            small_in[6 + index] = own + small_in[index]
            exchange(index + 1).start()
        else:
            total_ref[...] = own + small_in[index]

    scatter.begin()
    for row, (ref, index) in enumerate(packed((small1_ref, small2_ref, gbias_att_ref, gbias_up_ref))):
        if len(index) == 2:
            small_ref[row : row + 1, :] = ref[index[0] : index[0] + 1, index[1] : index[1] + 128]
        else:
            small_ref[row : row + 1, :] = ref[index[0], 0:1, index[2] : index[2] + 128]
    small_ref[small_ref.shape[0] - 64 :, :] = grel_ref[64:, :]
    exchange(0).start()
    for number, step in enumerate(scatter.steps):
        step()
        if number in FOLDS:
            fold(FOLDS.index(number))
    scatter.finish()
    for index in range(5):
        exchange(index).wait_send()


def attend_kernel(*refs, windows, padded, keys, size, linked):
    step = pl.program_id(0)
    duties = {}
    refs = list(refs)
    if linked:
        own_ref, more_ref, att_ref, mlp_ref, w_ref, keep_sem = refs[10], refs[11], refs[18], refs[19], refs[26], refs[-1]
        at = Place(4)
        att = Gather(at, own_ref, w_ref, *refs[27:29])
        mlp = Gather(at, more_ref, mlp_ref, *refs[29:31])
        mine = pltpu.make_async_copy(more_ref, mlp_ref.at[at.dp, at.tensor], keep_sem.at[0])
        keep = pltpu.make_async_copy(w_ref, att_ref, keep_sem.at[1])
        refs = refs[:1] + [w_ref] + refs[1:10] + refs[12:18] + refs[20:26]

        @pl.when(step == 0)
        def _():
            at.greet()
            att.begin()
            w_ref[at.dp, at.tensor] = own_ref[...]
            mine.start()

        duties = {slot: [act for act, when in zip(mlp.steps, MLP_SLOTS) if when == slot] for slot in MLP_SLOTS}
    (
        raw_ref, w_ref, gain_ref, shift_ref, query_bias_ref, value_bias_ref, rel_ref, slots_ref, pad_ref, feat_ref, amount_ref,
        query_ref, key_ref, value_ref, out_ref, acc_ref, x_ref,
        h1_ref, qk_ref, vv_ref, table_ref, key_feat_ref, bias_ref,
    ) = refs

    @pl.when(step == 0)
    def _():
        length, count = pad_ref.shape
        span = 2 * size - 1
        part = lax.axis_index("tensor")

        def norm_rows(w):
            spread_rows(raw_ref, x_ref, w, length, padded)
            here = slice(w * padded, w * padded + padded)
            normed, _ = normed_of(x_ref[here, :].astype(F32))
            h1_ref[here, :] = (normed * row(gain_ref) + row(shift_ref)).astype(BF)
            acc_ref[here, :] = jnp.zeros((padded, acc_ref.shape[1]), F32)

        def tables():
            place = lax.broadcasted_iota(jnp.int32, (64, 128), 0)
            lane = lanes_of((64, 128))
            wanted = jnp.where(place < span, 64 + span - 1 - place, jnp.where(place < 2 * span, 96 + 2 * span - 1 - place, -1))
            chosen = jnp.where(lane == wanted, 1.0, 0.0).astype(BF)
            rel = rel_ref[...]
            high = rel.astype(BF)
            rest = (rel - high.astype(F32)).astype(BF)
            table_ref[...] = jnp.zeros_like(table_ref)
            for number, piece in enumerate((high, rest)):
                turned = tn(piece, chosen)[:64].astype(BF)
                for head in range(3):
                    table_ref[number, head * 64 : head * 64 + 64, head * 128 : head * 128 + 128] = turned
            bias_ref[...] = jnp.zeros_like(bias_ref)
            for t in range(bias_ref.shape[0]):
                bias_ref[t, 0:1, 0:192] = row(query_bias_ref)[:, t * 192 : t * 192 + 192]
                bias_ref[t, 0:1, 384:576] = row(value_bias_ref)[:, t * 192 : t * 192 + 192]

        def features():
            picked = jnp.where(lax.broadcasted_iota(jnp.int32, (count, 128), 0) == slots_ref[...], 1.0, 0.0).astype(BF)
            usable = nn(pad_ref[...].astype(F32).astype(BF), picked)
            for w in range(windows):
                mask = jnp.where(of_slot(usable, part * windows + w) > 0.5, 0.0, NEGATIVE)
                start = w * padded
                key_feat_ref[start : start + padded, :] = feat_ref[...]
                key_feat_ref[start : start + length, :] = jnp.where(
                    lanes_of((length, 128)) == 79, mask, feat_ref[:length, :].astype(F32)).astype(BF)

        chores = [lambda w=w: norm_rows(w) for w in range(windows)] + [tables, features]
        if linked:
            for number, act in enumerate(att.steps):
                act()
                if number == MLP_BEGIN:
                    mlp.begin()
                if number < len(chores):
                    chores[number]()
            att.arrive()
            keep.start()
        else:
            for chore in chores:
                chore()

    h1 = h1_ref[...]
    chunk = step if linked else 0
    wa, wb = flat(w_ref[:, chunk, 0]), flat(w_ref[:, chunk, 1])
    qk_ref[...] = (nn(h1, wa) + bias_ref[step, 0:1, :384]).astype(BF)
    vv_ref[...] = (nn(h1, wb[:, :256]) + bias_ref[step, 0:1, 384:640]).astype(BF)
    lane = lanes_of((padded, 128))
    low = lane < 64
    field = lane & 31
    amounts = amount_ref[...]
    pad_lane = lanes_of((keys - padded, 128))
    pad_key = jnp.where(pad_lane == 79, NEGATIVE, 0.0).astype(BF)

    def window(w, carry):
        rows = pl.ds(pl.multiple_of(w * padded, 16), padded)
        qk = qk_ref[rows, :]
        vv = vv_ref[rows, :]
        spread = nn(qk[:, :256], table_ref[0]) + nn(qk[:, :256], table_ref[1])
        wide = qk.astype(F32)
        wide_v = vv.astype(F32)
        parts = [wide[:, :128], wide[:, 128:256], wide[:, 256:384]]
        turned = [pltpu.roll(part, 64, 1) for part in parts]
        queries = [parts[0], turned[0], parts[1]]
        keys_low = [turned[1], parts[2], turned[2]]
        values = [wide_v[:, :128], pltpu.roll(wide_v[:, :128], 64, 1), wide_v[:, 128:256]]
        key_feat = key_feat_ref[rows, :].astype(F32)
        ones = jnp.where((lane == 64) | (lane == 65), 1.0, 0.0)
        outs = []
        for head in range(3):
            for slot in duties:
                if slot % 3 == head:
                    for act in duties[slot]:
                        pl.when(step * windows + w == slot // 3)(act)
            moved = shift_lanes(spread[:, head * 128 : head * 128 + 128], amounts, True)
            high = moved.astype(BF).astype(F32)
            rest = pltpu.roll(moved - high, 16, 1)
            feat = jnp.where(field < 16, high, rest)
            feat = jnp.where(field < 14, feat, jnp.where((field >= 16) & (field < 30), feat, 0.0))
            feat = jnp.where(lane == 79, 1.0, feat)
            query = jnp.where(low, queries[head] * 0.125, feat)
            key_ref[0, head, w, :padded, :] = jnp.where(low, keys_low[head], key_feat).astype(BF)
            key_ref[0, head, w, padded:, :] = pad_key
            value_ref[0, head, w, :padded, :] = jnp.where(low, values[head], ones).astype(BF)
            value_ref[0, head, w, padded:, :] = jnp.zeros((keys - padded, 128), BF)
            scores = nt(query.astype(BF), key_ref[0, head, w])
            top = jnp.max(scores, -1, keepdims=True)
            expo = jnp.exp(scores - top).astype(BF)
            mixed = nn(expo, value_ref[0, head, w])
            total = mixed[:, 64:65]
            outs.append(mixed / total)
            logsum = -(top + jnp.log(total))
            first = logsum.astype(BF).astype(F32)
            second = (logsum - first).astype(BF).astype(F32)
            third = logsum - first - second
            query = jnp.where(lane == 78, first, query)
            query = jnp.where(lane == 94, second, query)
            query = jnp.where(lane == 95, third, query)
            query_ref[0, head, rows, :] = query.astype(BF)
        out_ref[0, rows, :128] = jnp.where(low, 0.0, pltpu.roll(outs[0], 64, 1)).astype(BF)
        out_ref[0, rows, 128:] = jnp.where(low, outs[1], pltpu.roll(outs[2], 64, 1)).astype(BF)
        return carry

    lax.fori_loop(0, windows, window, 0)
    acc_ref[...] += nt(out_ref[0], flat(w_ref[:, chunk, 1])[:, 128:])
    if linked:

        @pl.when(step == pl.num_programs(0) - 1)
        def _():
            for slot in duties:
                if slot >= 48:
                    for act in duties[slot]:
                        act()
            mlp.arrive()
            mine.wait()
            keep.wait()
            att.finish()
            mlp.finish()


def mlp_kernel(
    x_ref, attn_ref, cotangent_ref, slots_ref, w_ref, bias_proj_ref, gain_ref, shift_ref, bias_down_ref, bias_up_ref,
    result_ref, gx1_ref, grad_ref, gbias_up_ref, small_ref,
    x1_ref, h2_ref, h2t_ref, gyt_ref, y_ref, dh_ref, gy_ref, bias_ref,
    *, windows, padded,
):
    first = lax.axis_index("tensor") * windows
    columns = w_ref.shape[4]
    step = pl.program_id(0)
    last = pl.num_programs(0) - 1

    @pl.when(step == 0)
    def _():
        for w in range(windows):
            spread_rows(cotangent_ref, gy_ref, w, cotangent_ref.shape[0] // windows, padded, alive_of(slots_ref, first + w))
        x1 = x_ref[...].astype(F32) + (attn_ref[...] + row(bias_proj_ref))
        x1_ref[...] = x1
        normed, _ = normed_of(x1)
        h2 = (normed * row(gain_ref) + row(shift_ref)).astype(BF)
        for tile in range(bias_ref.shape[0]):
            bias_ref[tile] = row(bias_up_ref)[:, tile * columns : tile * columns + columns]
        h2_ref[...] = h2
        h2t_ref[...] = h2.T
        gyt_ref[...] = gy_ref[...].T
        y_ref[...] = jnp.zeros_like(y_ref)
        dh_ref[...] = jnp.zeros_like(dh_ref)

    up, down = flat(w_ref[:, 0, 0]), flat(w_ref[:, 0, 1])
    strips = (grad_ref.shape[0], grad_ref.shape[3], columns)
    upper = nn(h2_ref[...], up) + bias_ref[step]
    half = 0.5 * (1.0 + lax.erf(upper * np.float32(np.sqrt(0.5))))
    slope = half + upper * (np.float32(1.0 / np.sqrt(2 * np.pi)) * jnp.exp(-0.5 * upper * upper))
    active = (upper * half).astype(BF)
    grad_upper = (nn(gy_ref[...], down) * slope).astype(BF)
    y_ref[...] += nt(active, down)
    dh_ref[...] += nt(grad_upper, up)
    grad_ref[:, 0, 1] = nn(gyt_ref[...], active).astype(BF).reshape(strips)
    grad_ref[:, 0, 0] = nn(h2t_ref[...], grad_upper).astype(BF).reshape(strips)
    gbias_up_ref[0] = jnp.sum(grad_upper.astype(F32), 0, keepdims=True)

    @pl.when(step == last)
    def _():
        x1 = x1_ref[...]
        result = x1 + (y_ref[...] + row(bias_down_ref))
        length = result_ref.shape[0] // windows
        for w in range(windows):
            part = alive_of(slots_ref, first + w) * result[w * padded : w * padded + length]
            result_ref[w * length : w * length + length, :] = part.astype(BF)
        normed, inverse = normed_of(x1)
        gy = gy_ref[...].astype(F32)
        dh = dh_ref[...]
        gx1_ref[...] = gy + norm_back(dh, normed, inverse, row(gain_ref))
        small_ref[0:1, :] = jnp.sum(dh * normed, 0, keepdims=True)
        small_ref[1:2, :] = jnp.sum(dh, 0, keepdims=True)
        small_ref[2:3, :] = jnp.sum(gy, 0, keepdims=True)
        small_ref[3:8, :] = jnp.zeros_like(small_ref[3:8, :])


def attend_back_kernel(*refs, windows, padded, keys, size, linked):
    step = pl.program_id(0)
    last = pl.num_programs(0) - 1
    scatter = None
    if linked:
        scatter = make_scatter(refs[11], refs[17], refs[27:])
        refs = refs[:11] + refs[12:17] + refs[18:27]
        pl.when(step == 0)(scatter.begin)
    (
        x_ref, gx1_ref, w_ref, gain_ref, shift_ref, rel_ref, amount_ref,
        query_ref, key_ref, value_ref, out_ref,
        grad_x_ref, grad_ref, small_ref, gbias_ref, grel_ref,
        h1t_ref, gbt_ref, gb_ref, dh_ref, do_ref, gqk_ref, gv_ref, spread_ref, table_ref,
    ) = refs

    @pl.when(step == 0)
    def _():
        normed, _ = normed_of(x_ref[...].astype(F32))
        h1t_ref[...] = (normed * row(gain_ref) + row(shift_ref)).astype(BF).T
        span = 2 * size - 1
        place = lax.broadcasted_iota(jnp.int32, (64, 128), 0)
        wanted = jnp.where(place < span, span - 1 - place, jnp.where(place < 2 * span, 32 + 2 * span - 1 - place, -1))
        chosen = jnp.where((lanes_of((64, 128)) & 63) == wanted, 1.0, 0.0).astype(BF)
        table_ref[...] = tn(chosen, rel_ref[...].astype(BF)).astype(BF)
        gb = gx1_ref[...].astype(BF)
        gb_ref[...] = gb
        gbt_ref[...] = gb.T
        dh_ref[...] = jnp.zeros_like(dh_ref)
        grel_ref[...] = jnp.zeros_like(grel_ref)
        small_ref[0:1, :] = jnp.sum(gb.astype(F32), 0, keepdims=True)

    do_ref[...] = nn(gb_ref[...], flat(w_ref[:, 0, 1])[:, 128:]).astype(BF)
    lane = lanes_of((padded, 128))
    low = lane < 64
    field = lane & 31
    amounts = amount_ref[...]
    kept = (lane >= 64) & (field < 14)

    def window(w, carry):
        rows = pl.ds(pl.multiple_of(w * padded, 16), padded)
        do = do_ref[rows, :].astype(F32)
        out = out_ref[0, rows, :].astype(F32)
        product = do * out
        grads = [pltpu.roll(do[:, :128], 64, 1), do[:, 128:], pltpu.roll(do[:, 128:], 64, 1)]
        sums = [
            jnp.sum(jnp.where(low, 0.0, product[:, :128]), -1, keepdims=True),
            jnp.sum(jnp.where(low, product[:, 128:], 0.0), -1, keepdims=True),
            jnp.sum(jnp.where(low, 0.0, product[:, 128:]), -1, keepdims=True),
        ]
        gq, gk, gv = [], [], []
        for head in range(3):
            if linked:
                for slot, act in zip(SUM_SLOTS, scatter.steps):
                    if slot % 3 == head:
                        pl.when(step * windows + w == slot // 3)(act)
            delta = -sums[head]
            first = delta.astype(BF).astype(F32)
            grad_out = jnp.where(low, grads[head], jnp.where(lane == 64, first, jnp.where(lane == 65, delta - first, 0.0))).astype(BF)
            query, key, value = query_ref[0, head, rows, :], key_ref[0, head, w], value_ref[0, head, w]
            prob = jnp.exp(nt(query, key))
            grad_scores = (prob * nt(grad_out, value)).astype(BF)
            gv.append(tn(prob.astype(BF), grad_out)[:padded])
            gk.append(tn(grad_scores, query)[:padded])
            both = nn(grad_scores, key)
            back = shift_lanes(jnp.where(kept, both, 0.0), amounts, False)
            high = back.astype(BF).astype(F32)
            pack = jnp.where(low, pltpu.roll(back - high, 64, 1), high).astype(BF)
            spread_ref[head, rows, :] = pack
            gq.append(both * 0.125 + nn(pack, table_ref[...]))
        gqk_ref[rows, :128] = jnp.where(low, gq[0], pltpu.roll(gq[1], 64, 1)).astype(BF)
        gqk_ref[rows, 128:256] = jnp.where(low, gq[2], pltpu.roll(gk[0], 64, 1)).astype(BF)
        gqk_ref[rows, 256:] = jnp.where(low, gk[1], pltpu.roll(gk[2], 64, 1)).astype(BF)
        gv_ref[rows, :128] = jnp.where(low, gv[0], pltpu.roll(gv[1], 64, 1)).astype(BF)
        gv_ref[rows, 128:] = jnp.where(low, gv[2], 0.0).astype(BF)
        return carry

    lax.fori_loop(0, windows, window, 0)
    for head in range(3):
        grel_ref[...] += tn(spread_ref[head], query_ref[0, head])
    gqk, gv = gqk_ref[...], gv_ref[...]
    gbias_ref[0, :, :384] = jnp.sum(gqk.astype(F32), 0, keepdims=True)
    gbias_ref[0, :, 384:] = jnp.sum(gv.astype(F32), 0, keepdims=True)
    dh_ref[...] += nt(gqk, flat(w_ref[:, 0, 0])) + nt(gv, flat(w_ref[:, 0, 1])[:, :256])
    h1t = h1t_ref[...]
    strips = (grad_ref.shape[0], grad_ref.shape[3], -1)
    grad_ref[:, 0, 0] = nn(h1t, gqk).astype(BF).reshape(strips)
    one, two = nn(h1t, gv), nn(gbt_ref[...], out_ref[0])
    grad_ref[:, 0, 1, :, :128] = one[:, :128].astype(BF).reshape(strips)
    grad_ref[:, 0, 1, :, 128:256] = (one[:, 128:] + two[:, :128]).astype(BF).reshape(strips)
    grad_ref[:, 0, 1, :, 256:] = two[:, 128:].astype(BF).reshape(strips)

    @pl.when(step == last)
    def _():
        normed, inverse = normed_of(x_ref[...].astype(F32))
        dh = dh_ref[...]
        grad_x = (gx1_ref[...] + norm_back(dh, normed, inverse, row(gain_ref))).astype(BF)
        length = grad_x_ref.shape[0] // windows
        for w in range(windows):
            grad_x_ref[w * length : w * length + length, :] = grad_x[w * padded : w * padded + length]
        small_ref[1:2, :] = jnp.sum(dh * normed, 0, keepdims=True)
        small_ref[2:3, :] = jnp.sum(dh, 0, keepdims=True)
        small_ref[3:8, :] = jnp.zeros_like(small_ref[3:8, :])
        if linked:
            for slot, act in zip(SUM_SLOTS, scatter.steps):
                if slot >= 48:
                    act()
            scatter.finish()


def unpack_kernel(
    total_ref, att_ref, mlp_ref,
    qkv_ref, proj_ref, up_ref, down_ref, gain1_ref, shift1_ref, q_ref, v_ref, rel_h_ref, rel_w_ref,
    proj_bias_ref, gain2_ref, shift2_ref, up_bias_ref, down_bias_ref,
    *, span,
):
    qkv_ref[0] = att_ref[0, :, :192]
    qkv_ref[1] = att_ref[0, :, 192:]
    qkv_ref[2] = att_ref[1, :, :192]
    proj_ref[...] = att_ref[1, :, 192:].T
    up_ref[...] = mlp_ref[0]
    down_ref[...] = mlp_ref[1]
    for first, ref in ((0, proj_bias_ref), (6, gain1_ref), (12, shift1_ref), (18, gain2_ref), (24, shift2_ref), (30, down_bias_ref), (56, up_bias_ref)):
        for lane in range(0, ref.shape[0], 128):
            ref[pl.ds(lane, 128)] = total_ref[first + lane // 128]
    for start, ref in ((36, q_ref), (39, v_ref)):
        pieces = []
        for t in range(ref.shape[0] // 192):
            first = start + 5 * t
            pieces.append((total_ref[first : first + 1, :], total_ref[first + 1 : first + 2, :]))
        for pair in range(len(pieces) // 2):
            one, two = pieces[2 * pair], pieces[2 * pair + 1]
            low = lanes_of((1, 128)) < 64
            turned = [pltpu.roll(jnp.broadcast_to(v, (8, 128)), 64, 1)[:1] for v in two]
            parts = [one[0], jnp.where(low, one[1], turned[0]), jnp.where(low, turned[0], turned[1])]
            for i, values in enumerate(parts):
                ref[pl.ds(pair * 384 + i * 128, 128)] = values[0]
    rel = total_ref[total_ref.shape[0] - 64 :, :]
    high = rel.astype(BF)
    middle = (rel - high.astype(F32)).astype(BF)
    rest = (rel - high.astype(F32) - middle.astype(F32)).astype(BF)
    for ref, first in ((rel_h_ref, 0), (rel_w_ref, 32)):
        place = lax.broadcasted_iota(jnp.int32, (32, 64), 0)
        chosen = jnp.where(lanes_of((32, 64)) == first + span - 1 - place, 1.0, 0.0).astype(BF)
        values = nn(chosen, high) + nn(chosen, middle) + nn(chosen, rest)
        ref[...] = 8.0 * values[:span, :64]


def whole(shape):
    return pl.BlockSpec(shape, lambda *index: (0,) * len(shape))


def once(shape):
    return pl.BlockSpec(shape, lambda *index: (0,) * len(shape), pipeline_mode=pl.Buffered(1))


def shards(
    block_input, cotangent, pad_mask, slot_window, qkv_w, proj_w, fc1_w, fc2_w,
    norm1_gain, norm1_bias, q_bias, v_bias, rel_h, rel_w, proj_bias,
    norm2_gain, norm2_bias, fc1_bias, fc2_bias,
):
    part = lax.axis_index("tensor")
    count_dp, count_t = lax.axis_size("dp"), lax.axis_size("tensor")
    length = pad_mask.shape[1]
    local_rows, width = block_input.shape
    windows = local_rows // length
    size = rel_h.shape[0] // 2 + 1
    padded = -(-length // 16) * 16
    keys = -(-length // 128) * 128
    rows = windows * padded
    strip = width // count_dp

    slots = jnp.pad(slot_window, (0, 128 - slot_window.shape[0]), constant_values=-1).reshape(1, 128)
    rel = jnp.pad(jnp.concatenate([rel_h, rel_w]), ((0, 64 - 2 * rel_h.shape[0]), (0, 64)))

    place = np.arange(padded)
    row_of, col_of = place // size, place % size
    inside = place < length
    amount = np.zeros((padded, 128), np.int32)
    amount[:, :] = np.where(
        (np.arange(128) % 64 < 32)[None, :], (size - 1 - row_of)[:, None], (size - 1 - col_of)[:, None]
    ) * inside[:, None]
    amount = jnp.asarray(amount)
    feat = np.zeros((padded, 128), np.float32)
    for a in range(size):
        for base, pos in ((64, row_of), (96, col_of)):
            feat[:, base + a] = (pos == a) & inside
            feat[:, base + 16 + a] = (pos == a) & inside
    feat[:, [78, 94, 95]] = 1.0
    feat[:, 79] = np.where(inside, 0.0, NEGATIVE)
    feat = jnp.asarray(feat.astype(BF))
    span = rel_h.shape[0]

    q_w, k_w, v_w = qkv_w[0], qkv_w[1], qkv_w[2]
    shard_att = jnp.stack([jnp.concatenate([q_w, k_w], 1), jnp.concatenate([v_w, proj_w.T], 1)])
    shard_mlp = jnp.stack([fc1_w, fc2_w.T])
    columns = fc1_w.shape[1]
    linked = count_dp == 8 and count_t == 4 and strip % 16 == 0 and windows == 4
    any_spec, vmem_spec = pl.BlockSpec(memory_space=pl.ANY), pl.BlockSpec(memory_space=pltpu.VMEM)
    blocks, depth = (count_dp, strip) if linked else (1, width)

    def talk(number, **more):
        return pltpu.CompilerParams(
            vmem_limit_bytes=VMEM_LIMIT, collective_id=number, has_side_effects=True, **more)

    def gather_all(pieces):
        every = lax.all_gather(pieces, AXES, axis=0, tiled=False).reshape(count_dp, count_t, *pieces.shape)
        return every.transpose(1, 2, 0, 3, 4).reshape(1, count_t, 2, width, pieces.shape[2])

    if not linked:
        w_att, w_mlp = gather_all(shard_att), gather_all(shard_mlp)

    vec = once((width,))
    params = pltpu.CompilerParams(dimension_semantics=("arbitrary",), vmem_limit_bytes=VMEM_LIMIT)

    query, key, value, out, attn, x, *rest = pl.pallas_call(
        partial(attend_kernel, windows=windows, padded=padded, keys=keys, size=size, linked=linked),
        grid=(count_t,),
        in_specs=[
            once((local_rows, width)),
        ] + [pl.BlockSpec((blocks, 1, 2, depth, 384), lambda t: (0, t, 0, 0, 0))] * (not linked) + [
            vec, vec, vec, vec, once((64, 128)), once((1, 128)), once(pad_mask.shape[::-1]),
            once((padded, 128)), once((padded, 128)),
        ] + [once((2, strip, 384)), once((2, strip, columns))] * linked,
        out_specs=[
            pl.BlockSpec((1, 3, rows, 128), lambda t: (t, 0, 0, 0)),
            pl.BlockSpec((1, 3, windows, keys, 128), lambda t: (t, 0, 0, 0, 0)),
            pl.BlockSpec((1, 3, windows, keys, 128), lambda t: (t, 0, 0, 0, 0)),
            pl.BlockSpec((1, rows, 256), lambda t: (t, 0, 0)),
            whole((rows, width)), whole((rows, width)),
        ] + [any_spec, any_spec] * linked,
        out_shape=[
            jax.ShapeDtypeStruct((count_t, 3, rows, 128), BF),
            jax.ShapeDtypeStruct((count_t, 3, windows, keys, 128), BF),
            jax.ShapeDtypeStruct((count_t, 3, windows, keys, 128), BF),
            jax.ShapeDtypeStruct((count_t, rows, 256), BF),
            jax.ShapeDtypeStruct((rows, width), F32),
            jax.ShapeDtypeStruct((rows, width), BF),
        ] + [jax.ShapeDtypeStruct((count_dp, count_t, 2, strip, n), BF) for n in (384, columns)] * linked,
        scratch_shapes=[
            pltpu.VMEM((rows, width), BF), pltpu.VMEM((rows, 384), BF), pltpu.VMEM((rows, 256), BF),
            pltpu.VMEM((2, 256, 384), BF), pltpu.VMEM((rows, 128), BF), pltpu.VMEM((count_t, 1, 640), F32),
        ]
        + ([pltpu.VMEM((count_dp, count_t, 2, strip, 384), BF)] + gather_scratch() * 2 + [pltpu.SemaphoreType.DMA((2,))]) * linked,
        compiler_params=talk(2, dimension_semantics=("arbitrary",)) if linked else params,
        name="attend",
    )(
        block_input, *([] if linked else [w_att]), norm1_gain, norm1_bias, q_bias, v_bias, rel, slots, pad_mask.T, feat, amount,
        *([shard_att, shard_mlp] * linked)
    )
    if linked:
        w_att, w_mlp = rest

    mlp_block = pl.BlockSpec((blocks, 1, 2, depth, columns), lambda j: (0, j, 0, 0, 0))
    result, gx1, grad_mlp, gbias_up, small2 = pl.pallas_call(
        partial(mlp_kernel, windows=windows, padded=padded),
        grid=(count_t,),
        in_specs=[
            once((rows, width)), once((rows, width)), once((local_rows, width)), once((1, 128)),
            mlp_block, vec, vec, vec, vec, once(fc1_bias.shape),
        ],
        out_specs=[
            whole((local_rows, width)), whole((rows, width)),
            mlp_block,
            pl.BlockSpec((1, 1, columns), lambda j: (j, 0, 0)),
            whole((8, width)),
        ],
        out_shape=[
            jax.ShapeDtypeStruct((local_rows, width), BF),
            jax.ShapeDtypeStruct((rows, width), F32),
            jax.ShapeDtypeStruct((blocks, count_t, 2, depth, columns), BF),
            jax.ShapeDtypeStruct((count_t, 1, columns), F32),
            jax.ShapeDtypeStruct((8, width), F32),
        ],
        scratch_shapes=[
            pltpu.VMEM((rows, width), F32), pltpu.VMEM((rows, width), BF),
            pltpu.VMEM((width, rows), BF), pltpu.VMEM((width, rows), BF),
            pltpu.VMEM((rows, width), F32), pltpu.VMEM((rows, width), F32), pltpu.VMEM((rows, width), BF),
            pltpu.VMEM((count_t, 1, columns), F32),
        ],
        compiler_params=params,
        name="mlp",
    )(x, attn, cotangent, slots, w_mlp, proj_bias, norm2_gain, norm2_bias, fc2_bias, fc1_bias)

    grad_x, grad_att, small1, gbias_att, grel, *rest = pl.pallas_call(
        partial(attend_back_kernel, windows=windows, padded=padded, keys=keys, size=size, linked=linked),
        grid=(count_t,),
        in_specs=[
            once((rows, width)), once((rows, width)),
            pl.BlockSpec((blocks, 1, 2, depth, 384), lambda t: (0, t, 0, 0, 0)),
            vec, vec, once((64, 128)), once((padded, 128)),
            pl.BlockSpec((1, 3, rows, 128), lambda t: (t, 0, 0, 0)),
            pl.BlockSpec((1, 3, windows, keys, 128), lambda t: (t, 0, 0, 0, 0)),
            pl.BlockSpec((1, 3, windows, keys, 128), lambda t: (t, 0, 0, 0, 0)),
            pl.BlockSpec((1, rows, 256), lambda t: (t, 0, 0)),
        ] + [any_spec] * linked,
        out_specs=[
            whole((local_rows, width)),
            pl.BlockSpec((blocks, 1, 2, depth, 384), lambda t: (0, t, 0, 0, 0)),
            whole((8, width)),
            pl.BlockSpec((1, 1, 640), lambda t: (t, 0, 0)),
            whole((128, 128)),
        ] + [whole((2, strip, columns))] * linked,
        out_shape=[
            jax.ShapeDtypeStruct((local_rows, width), BF),
            jax.ShapeDtypeStruct((blocks, count_t, 2, depth, 384), BF),
            jax.ShapeDtypeStruct((8, width), F32),
            jax.ShapeDtypeStruct((count_t, 1, 640), F32),
            jax.ShapeDtypeStruct((128, 128), F32),
        ] + [jax.ShapeDtypeStruct((2, strip, columns), F32)] * linked,
        scratch_shapes=[
            pltpu.VMEM((width, rows), BF), pltpu.VMEM((width, rows), BF), pltpu.VMEM((rows, width), BF),
            pltpu.VMEM((rows, width), F32), pltpu.VMEM((rows, 256), BF),
            pltpu.VMEM((rows, 384), BF), pltpu.VMEM((rows, 256), BF), pltpu.VMEM((3, rows, 128), BF),
            pltpu.VMEM((128, 128), BF),
        ] + (scatter_scratch(2, strip, columns) if linked else []),
        compiler_params=talk(3, dimension_semantics=("arbitrary",)) if linked else params,
        name="attend_back",
    )(
        x, gx1, w_att, norm1_gain, norm1_bias, rel, amount, query, key, value, out,
        *([grad_mlp.reshape(count_dp // 2, 2, count_t, 2, strip, columns)] * linked if linked else [])
    )

    if linked:
        sum_mlp = rest[0]
        count = 36 + 5 * count_t + fc1_bias.shape[0] // 128 + 64
        sum_att, total = pl.pallas_call(
            reduce_kernel,
            in_specs=[any_spec] + [vmem_spec] * 5, out_specs=[vmem_spec, vmem_spec],
            out_shape=[jax.ShapeDtypeStruct((2, strip, 384), F32), jax.ShapeDtypeStruct((count, 128), F32)],
            scratch_shapes=[
                pltpu.VMEM((count, 128), F32), pltpu.VMEM((10, count, 128), F32),
                pltpu.SemaphoreType.DMA((5,)), pltpu.SemaphoreType.DMA((5,)),
            ] + scatter_scratch(2, strip, 384),
            compiler_params=talk(4),
            name="reduce_attention",
        )(grad_att.reshape(count_dp // 2, 2, count_t, 2, strip, 384), small1, small2, gbias_att, gbias_up, grel)
        like = (
            qkv_w, proj_w, fc1_w, fc2_w.T, norm1_gain, norm1_bias, q_bias, v_bias, rel_h, rel_w,
            proj_bias, norm2_gain, norm2_bias, fc1_bias, fc2_bias,
        )
        shapes = [jax.ShapeDtypeStruct(v.shape, F32) for v in like]
        outs = pl.pallas_call(
            partial(unpack_kernel, span=span),
            in_specs=[vmem_spec] * 3, out_specs=[vmem_spec] * len(shapes), out_shape=shapes,
            compiler_params=pltpu.CompilerParams(vmem_limit_bytes=VMEM_LIMIT),
            name="unpack",
        )(total, sum_att, sum_mlp)
        return (result, grad_x, *outs[:3], outs[3].T, *outs[4:])
    parts = [
        small1[:3].reshape(-1, 128), small2[:3].reshape(-1, 128), gbias_att.reshape(-1, 128), gbias_up.reshape(-1, 128), grel[64:],
    ]
    def scatter_all(grads):
        grads = grads.reshape(count_t, 2, count_dp, strip, grads.shape[4]).transpose(2, 0, 1, 3, 4)
        grads = grads.reshape(count_dp * count_t, *grads.shape[2:])
        return lax.psum_scatter(grads, AXES, scatter_dimension=0, tiled=False).astype(F32)

    sum_mlp, sum_att = scatter_all(grad_mlp), scatter_all(grad_att)
    small = lax.psum(jnp.concatenate(parts), AXES)
    cuts = np.cumsum([part.shape[0] for part in parts])[:-1]
    small1, small2, gbias_att, gbias_up, grad_rel = jnp.split(small, cuts)
    small1, small2 = small1.reshape(3, width), small2.reshape(3, width)
    gbias_att = gbias_att.reshape(count_t, 1, 640)
    grad_rel = 8.0 * grad_rel[:, :64]
    head_q, head_k = sum_att[0, :, :192], sum_att[0, :, 192:]
    head_v, head_p = sum_att[1, :, :192], sum_att[1, :, 192:]
    return (
        result,
        grad_x,
        jnp.stack([head_q, head_k, head_v]),
        head_p.T,
        sum_mlp[0],
        sum_mlp[1].T,
        small1[1],
        small1[2],
        gbias_att[:, 0, :192].reshape(-1),
        gbias_att[:, 0, 384:576].reshape(-1),
        grad_rel[:span][::-1],
        grad_rel[32 : 32 + span][::-1],
        small1[0],
        small2[0],
        small2[1],
        gbias_up.reshape(-1),
        small2[2],
    )


def solution(mesh):
    return jax.shard_map(
        shards,
        mesh=mesh,
        in_specs=(
            P(AXES, None), P(AXES, None), P(), P("dp"),
            P(None, "dp", "tensor"), P("tensor", "dp"), P("dp", "tensor"), P("tensor", "dp"),
        )
        + (P(),) * 11,
        out_specs=(
            P(AXES, None), P(AXES, None),
            P(None, "dp", "tensor"), P("tensor", "dp"), P("dp", "tensor"), P("tensor", "dp"),
        )
        + (P(),) * 11,
        check_vma=False,
    )
```

```python
from functools import partial

import jax
import jax.numpy as jnp
import numpy as np
from jax import lax
from jax.experimental import pallas as pl
from jax.experimental.pallas import tpu as pltpu
from jax.sharding import PartitionSpec as P

HD = 64
EPSILON = 1e-06
NEGATIVE = -1e30
F32, BF = jnp.float32, jnp.bfloat16
AXES = ("dp", "tensor")
VMEM_LIMIT = 60 * 1024 * 1024
MLP_BEGIN = 11
MLP_SLOTS = tuple(range(1, 16))
SUM_SLOTS = (1, 1, 2, 2, 4, 5, 6, 7, 7, 8, 8, 9, 9, 10, 10, 11, 12, 13, 13)

FOLDS = (3, 6, 9, 12, 15)


def nn(left, right):
    return lax.dot_general(left, right, (((1,), (0,)), ((), ())), preferred_element_type=F32)


def nt(left, right):
    return lax.dot_general(left, right, (((1,), (1,)), ((), ())), preferred_element_type=F32)


def tn(left, right):
    return lax.dot_general(left, right, (((0,), (0,)), ((), ())), preferred_element_type=F32)


def normed_of(values):
    center = values - jnp.mean(values, -1, keepdims=True)
    inverse = lax.rsqrt(jnp.mean(center * center, -1, keepdims=True) + EPSILON)
    return center * inverse, inverse


def norm_back(grad, normed, inverse, gain):
    scaled = grad * gain
    inner = (
        scaled
        - jnp.mean(scaled, -1, keepdims=True)
        - normed * jnp.mean(scaled * normed, -1, keepdims=True)
    )
    return inverse * inner


def spread_rows(source_ref, target_ref, w, length, padded, live=None):
    tail = w * padded + length // 16 * 16
    target_ref[tail : w * padded + padded, :] = jnp.zeros((w * padded + padded - tail, target_ref.shape[1]), target_ref.dtype)
    values = source_ref[w * length : w * length + length, :]
    if live is not None:
        values = jnp.where(live > 0.5, values.astype(F32), 0.0).astype(values.dtype)
    target_ref[w * padded : w * padded + length, :] = values


def row(ref):
    return ref[...].reshape(1, -1)


def flat(values):
    return values.reshape(-1, values.shape[-1])


def lanes_of(shape):
    return lax.broadcasted_iota(jnp.int32, shape, 1)


def of_slot(values, slot):
    return jnp.sum(jnp.where(lanes_of(values.shape) == slot, values, 0.0), -1, keepdims=True)


def alive_of(slots_ref, slot):
    return of_slot(jnp.where(slots_ref[...] >= 0, 1.0, 0.0), slot)


def shift_lanes(values, amounts, left):
    for bit in (1, 2, 4, 8):
        moved = pltpu.roll(values, 128 - bit if left else bit, 1)
        values = jnp.where((amounts & bit) != 0, moved, values)
    return values


MESH = pl.DeviceIdType.MESH


class Place:
    def __init__(self, height):
        self.height = height
        self.dp, self.tensor = lax.axis_index("dp"), lax.axis_index("tensor")
        self.z, self.y = lax.div(self.dp, 2), lax.rem(self.dp, 2)
        self.x, self.c = lax.div(self.tensor, 2), lax.rem(self.tensor, 2)

    def plane(self, colour, a, b):
        return lax.rem(self.y + (1 - colour) * b + colour * a, 2), lax.rem(self.x + (1 - colour) * a + colour * b, 2)

    def shard(self, colour, a, b, z):
        y, x = self.plane(colour, a, b)
        return z * 2 + y, x * 2 + colour

    def near(self, k):
        upper = lax.div(self.z, self.height // 2)
        zz = self.z + upper * (self.height - 1 - 2 * self.z)
        q = (zz, 1 - zz, 2, 3)[k]
        return q + upper * (self.height - 1 - 2 * q)

    def peer(self, kind):
        if kind == "core":
            return self.dp, self.x * 2 + 1 - self.c
        if kind in ("z1", "z2", "z3"):
            return self.near(int(kind[1])) * 2 + self.y, self.tensor
        if kind == "up":
            return self.dp + 2, self.tensor
        if kind == "down":
            return self.dp - 2, self.tensor
        if kind == "y":
            return self.z * 2 + 1 - self.y, self.tensor
        if kind == "x":
            return self.dp, (1 - self.x) * 2 + self.c
        if kind == "pair":
            return (self.z + 1 - 2 * lax.rem(self.z, 2)) * 2 + self.y, self.tensor
        if kind == "half":
            return lax.rem(self.z + 2, 4) * 2 + self.y, self.tensor
        return self.shard(self.c, int(kind == "far"), int(kind == "near"), self.z)

    def has(self, kind):
        if kind == "up":
            return self.z < self.height - 1
        if kind == "down":
            return self.z > 0
        return None

    def greet(self):
        barrier = pltpu.get_barrier_semaphore()
        for kind in ("core", "near", "far", "z1", "z2", "z3"):
            pl.semaphore_signal(barrier, inc=1, device_id=self.peer(kind), device_id_type=MESH)
        pl.semaphore_wait(barrier, 6)


def under(condition, action):
    if condition is None:
        action()
    else:
        pl.when(condition)(action)


def both(one, two):
    return two if one is None else one if two is None else jnp.logical_and(one, two)


class Gather:
    SENDS = 36

    def __init__(self, at, own_ref, all_ref, send_sem, recv_sem, first=0, count=None):
        self.at, self.own_ref = at, own_ref
        self.all_ref = all_ref if count is None else all_ref.at[:, :, first : first + count]
        self.send_sem, self.recv_sem = send_sem, recv_sem
        z = [lambda k=k: self.step(("z", k)) for k in range(4)]
        near = [lambda k=k: self.step(("near", k)) for k in range(4)]
        far = [[lambda b=b, k=k: self.step(("far", b, k)) for k in range(4)] for b in range(2)]
        self.steps = [
            near[0], z[1], far[0][0], near[1], far[1][0], z[2], far[0][1],
            near[2], far[1][1], z[3], far[0][2], near[3], far[1][2], far[0][3], far[1][3],
        ]
        slot = 0
        self.slots = {}
        for key in [("z", k) for k in range(4)] + [("near", k) for k in range(4)] + [("far", b, k) for b in range(2) for k in range(4)]:
            self.slots[key] = slot
            slot += len(self.kinds(key))

    def kinds(self, key):
        return {"z": ("up", "down", "near", "far", "core"), "near": ("far", "core"), "far": ("core",)}[key[0]]

    def shard(self, key):
        at = self.at
        if key[0] == "z":
            return at.shard(at.c, 0, 0, at.near(key[1]))
        if key[0] == "near":
            return at.shard(at.c, 0, 1, at.near(key[1]))
        return at.shard(at.c, 1, key[1], at.near(key[2]))

    def copy(self, source, shard, kind, slot):
        dp, tensor = shard
        return pltpu.make_async_remote_copy(
            src_ref=source, dst_ref=self.all_ref.at[dp, tensor], send_sem=self.send_sem.at[slot],
            recv_sem=self.recv_sem.at[dp * 4 + tensor], device_id=self.at.peer(kind), device_id_type=MESH)

    def sends(self, key):
        shard = self.shard(key)
        source = self.own_ref if key == ("z", 0) else self.all_ref.at[shard[0], shard[1]]
        away = self.at.near(key[1]) - self.at.z if key[0] == "z" else 0
        sends = []
        for i, kind in enumerate(self.kinds(key)):
            condition = self.at.has(kind)
            if kind in ("up", "down"):
                condition = jnp.logical_and(condition, away <= 0 if kind == "up" else away >= 0)
            sends.append((condition, self.copy(source, shard, kind, self.slots[key] + i)))
        return sends

    def take(self, shard):
        self.copy(self.all_ref.at[shard[0], shard[1]], shard, "core", 0).wait_recv()

    def begin(self):
        for condition, copy in self.sends(("z", 0)):
            under(condition, copy.start)

    def step(self, key):
        self.take(self.shard(key))
        for condition, copy in self.sends(key):
            under(condition, copy.start)

    def arrive(self):
        at = self.at
        for a in range(2):
            for b in range(2):
                for k in range(4):
                    self.take(at.shard(1 - at.c, a, b, at.near(k)))

    def finish(self):
        for key in self.slots:
            for condition, copy in self.sends(key):
                under(condition, copy.wait_send)


def gather_scratch():
    return [pltpu.SemaphoreType.DMA((Gather.SENDS,)), pltpu.SemaphoreType.DMA((32,))]


class Scatter:
    def __init__(self, all_ref, own_ref, held, core_in, far_in, near_in, up_in, down_in, sems, height=4):
        self.all_ref, self.own_ref, self.held, self.core_in = all_ref, own_ref, held, core_in
        self.far_in, self.near_in, self.up_in, self.down_in, self.sems = far_in, near_in, up_in, down_in, sems
        self.at = Place(height)
        core = {(a, b): (lambda a=a, b=b: self.from_core(a, b)) for a in range(2) for b in range(2)}
        far = [[lambda b=b, k=k: self.from_far(b, k) for k in range(4)] for b in range(2)]
        near = [lambda k=k: self.from_near(k) for k in range(4)]
        line = [lambda k=k: self.from_line(k) for k in range(4)]
        self.steps = [
            core[1, 1], core[1, 0], core[0, 1], core[0, 0], far[1][3], far[0][3], far[1][2], near[3], far[0][2], line[3],
            far[1][1], near[2], far[0][1], line[2], far[1][0], near[1], far[0][0], line[1], near[0],
        ]
        self.last = line[0]

    def remote(self, source, target, name, index, kind):
        send, recv = self.sems[name]
        return pltpu.make_async_remote_copy(
            src_ref=source, dst_ref=target, send_sem=send.at[index], recv_sem=recv.at[index],
            device_id=self.at.peer(kind), device_id_type=MESH)

    def core_copy(self, a, b):
        at = self.at
        y, x = at.plane(1 - at.c, a, b)
        source = self.all_ref.at[:, y, x * 2 + 1 - at.c]
        return self.remote(source, self.core_in.at[a, b], "core", a * 2 + b, "core")

    def local_copy(self, a, b):
        at = self.at
        y, x = at.plane(at.c, a, b)
        return pltpu.make_async_copy(self.all_ref.at[:, y, x * 2 + at.c], self.held.at[a, b], self.sems["local"].at[a * 2 + b])

    def far_copy(self, b, z):
        return self.remote(self.held.at[1, b, z], self.far_in.at[b, z], "far", b * 4 + z, "far")

    def near_copy(self, z):
        return self.remote(self.held.at[0, 1, z], self.near_in.at[z], "near", z, "near")

    def down_copy(self, z):
        return self.remote(self.held.at[0, 0, z], self.down_in.at[z], "down", z, "down")

    def up_copy(self, z):
        return self.remote(self.held.at[0, 0, z], self.up_in.at[z], "up", z, "up")

    def begin(self):
        self.at.greet()
        for a in (1, 0):
            for b in (1, 0):
                self.core_copy(a, b).start()
                self.local_copy(a, b).start()

    def from_core(self, a, b):
        self.local_copy(a, b).wait()
        self.core_copy(a, b).wait_recv()
        for z in range(4):
            self.held[a, b, z] = self.held[a, b, z] + self.core_in[a, b, z]
        if (a, b) == (1, 0):
            for k in (3, 2, 1, 0):
                for side in (1, 0):
                    self.far_copy(side, self.at.near(k)).start()

    def from_far(self, b, k):
        z = self.at.near(k)
        self.far_copy(b, z).wait_recv()
        self.held[0, b, z] = self.held[0, b, z] + self.far_in[b, z]
        if b == 1:
            self.near_copy(z).start()

    def from_near(self, k):
        z = self.at.near(k)
        self.near_copy(z).wait_recv()
        self.held[0, 0, z] = self.held[0, 0, z] + self.near_in[z]

    def from_line(self, k):
        at = self.at
        if k > 0:
            z = at.near(k)

            def downward():
                def add():
                    self.down_copy(z).wait_recv()
                    self.held[0, 0, z] = self.held[0, 0, z] + self.down_in[z]

                under(at.has("up"), add)
                self.down_copy(z).start()

            def upward():
                def add():
                    self.up_copy(z).wait_recv()
                    self.held[0, 0, z] = self.held[0, 0, z] + self.up_in[z]

                under(at.has("down"), add)
                self.up_copy(z).start()

            pl.when(z < at.z)(downward)
            pl.when(z > at.z)(upward)
            return
        self.own_ref[...] = self.held[0, 0, at.z].astype(F32)

        def add_down():
            self.down_copy(at.z).wait_recv()
            self.own_ref[...] += self.down_in[at.z].astype(F32)

        def add_up():
            self.up_copy(at.z).wait_recv()
            self.own_ref[...] += self.up_in[at.z].astype(F32)

        under(at.has("up"), add_down)
        under(at.has("down"), add_up)

    def finish(self):
        at = self.at
        self.last()
        for a in range(2):
            for b in range(2):
                self.core_copy(a, b).wait_send()
        for b in range(2):
            for z in range(4):
                self.far_copy(b, z).wait_send()
        for z in range(4):
            self.near_copy(z).wait_send()
            pl.when(z < at.z)(lambda: self.down_copy(z).wait_send())
            pl.when(z > at.z)(lambda: self.up_copy(z).wait_send())


def scatter_scratch(pieces, strip, columns):
    block = (pieces, strip, columns)
    shapes = [(2, 2, 4), (2, 2, 4), (2, 4), (4,), (4,), (4,)]
    sems = [4, 4, 8, 8, 4, 4, 4, 4, 4, 4, 4]
    return [pltpu.VMEM(lead + block, BF) for lead in shapes] + [pltpu.SemaphoreType.DMA((n,)) for n in sems]


SCATTER_REFS = 17


def make_scatter(all_ref, own_ref, refs):
    held, core_in, far_in, near_in, up_in, down_in = refs[:6]
    core_s, core_r, far_s, far_r, near_s, near_r, up_s, up_r, down_s, down_r, local = refs[6:]
    sems = {
        "core": (core_s, core_r), "far": (far_s, far_r), "near": (near_s, near_r),
        "up": (up_s, up_r), "down": (down_s, down_r), "local": local,
    }
    return Scatter(all_ref, own_ref, held, core_in, far_in, near_in, up_in, down_in, sems)


def packed(refs):
    small1_ref, small2_ref, gbias_att_ref, gbias_up_ref = refs
    places = []
    for ref, rows in ((small1_ref, range(3)), (small2_ref, range(3))):
        places += [(ref, (row, lane)) for row in rows for lane in range(0, ref.shape[1], 128)]
    for ref in (gbias_att_ref, gbias_up_ref):
        places += [(ref, (row, 0, lane)) for row in range(ref.shape[0]) for lane in range(0, ref.shape[2], 128)]
    return places


def reduce_kernel(
    all_ref, small1_ref, small2_ref, gbias_att_ref, gbias_up_ref, grel_ref,
    own_ref, total_ref, small_ref, small_in, small_send, small_recv, *refs,
):
    scatter = make_scatter(all_ref, own_ref, refs)
    at = scatter.at
    rounds = ("core", "y", "x", "pair", "half")

    def exchange(index):
        return pltpu.make_async_remote_copy(
            src_ref=small_ref if index == 0 else small_in.at[5 + index], dst_ref=small_in.at[index],
            send_sem=small_send.at[index], recv_sem=small_recv.at[index],
            device_id=at.peer(rounds[index]), device_id_type=MESH)

    def fold(index):
        exchange(index).wait_recv()
        own = small_ref[...] if index == 0 else small_in[5 + index]
        if index < 4:
            small_in[6 + index] = own + small_in[index]
            exchange(index + 1).start()
        else:
            total_ref[...] = own + small_in[index]

    scatter.begin()
    for row, (ref, index) in enumerate(packed((small1_ref, small2_ref, gbias_att_ref, gbias_up_ref))):
        if len(index) == 2:
            small_ref[row : row + 1, :] = ref[index[0] : index[0] + 1, index[1] : index[1] + 128]
        else:
            small_ref[row : row + 1, :] = ref[index[0], 0:1, index[2] : index[2] + 128]
    small_ref[small_ref.shape[0] - 64 :, :] = grel_ref[64:, :]
    exchange(0).start()
    for number, step in enumerate(scatter.steps):
        step()
        if number in FOLDS:
            fold(FOLDS.index(number))
    scatter.finish()
    for index in range(5):
        exchange(index).wait_send()


def attend_kernel(*refs, windows, padded, keys, size, linked):
    step = pl.program_id(0)
    duties = {}
    refs = list(refs)
    if linked:
        own_ref, more_ref, att_ref, mlp_ref, w_ref, keep_sem = refs[10], refs[11], refs[18], refs[19], refs[26], refs[-1]
        at = Place(4)
        att = Gather(at, own_ref, w_ref, *refs[27:29])
        mlp = Gather(at, more_ref, mlp_ref, *refs[29:31])
        mine = pltpu.make_async_copy(more_ref, mlp_ref.at[at.dp, at.tensor], keep_sem.at[0])
        keep = pltpu.make_async_copy(w_ref, att_ref, keep_sem.at[1])
        refs = refs[:1] + [w_ref] + refs[1:10] + refs[12:18] + refs[20:26]

        @pl.when(step == 0)
        def _():
            at.greet()
            att.begin()
            w_ref[at.dp, at.tensor] = own_ref[...]
            mine.start()

        duties = {slot: [act for act, when in zip(mlp.steps, MLP_SLOTS) if when == slot] for slot in MLP_SLOTS}
    (
        raw_ref, w_ref, gain_ref, shift_ref, query_bias_ref, value_bias_ref, rel_ref, slots_ref, pad_ref, feat_ref, amount_ref,
        query_ref, key_ref, value_ref, out_ref, acc_ref, x_ref,
        h1_ref, qk_ref, vv_ref, table_ref, key_feat_ref, bias_ref,
    ) = refs

    @pl.when(step == 0)
    def _():
        length, count = pad_ref.shape
        span = 2 * size - 1
        part = lax.axis_index("tensor")

        def norm_rows(w):
            spread_rows(raw_ref, x_ref, w, length, padded)
            here = slice(w * padded, w * padded + padded)
            normed, _ = normed_of(x_ref[here, :].astype(F32))
            h1_ref[here, :] = (normed * row(gain_ref) + row(shift_ref)).astype(BF)
            acc_ref[here, :] = jnp.zeros((padded, acc_ref.shape[1]), F32)

        def tables():
            place = lax.broadcasted_iota(jnp.int32, (64, 128), 0)
            lane = lanes_of((64, 128))
            wanted = jnp.where(place < span, 64 + span - 1 - place, jnp.where(place < 2 * span, 96 + 2 * span - 1 - place, -1))
            chosen = jnp.where(lane == wanted, 1.0, 0.0).astype(BF)
            rel = rel_ref[...]
            high = rel.astype(BF)
            rest = (rel - high.astype(F32)).astype(BF)
            table_ref[...] = jnp.zeros_like(table_ref)
            for number, piece in enumerate((high, rest)):
                turned = tn(piece, chosen)[:64].astype(BF)
                for head in range(3):
                    table_ref[number, head * 64 : head * 64 + 64, head * 128 : head * 128 + 128] = turned
            bias_ref[...] = jnp.zeros_like(bias_ref)
            for t in range(bias_ref.shape[0]):
                bias_ref[t, 0:1, 0:192] = row(query_bias_ref)[:, t * 192 : t * 192 + 192]
                bias_ref[t, 0:1, 384:576] = row(value_bias_ref)[:, t * 192 : t * 192 + 192]

        def features():
            picked = jnp.where(lax.broadcasted_iota(jnp.int32, (count, 128), 0) == slots_ref[...], 1.0, 0.0).astype(BF)
            usable = nn(pad_ref[...].astype(F32).astype(BF), picked)
            for w in range(windows):
                mask = jnp.where(of_slot(usable, part * windows + w) > 0.5, 0.0, NEGATIVE)
                start = w * padded
                key_feat_ref[start : start + padded, :] = feat_ref[...]
                key_feat_ref[start : start + length, :] = jnp.where(
                    lanes_of((length, 128)) == 79, mask, feat_ref[:length, :].astype(F32)).astype(BF)

        chores = [lambda w=w: norm_rows(w) for w in range(windows)] + [tables, features]
        if linked:
            for number, act in enumerate(att.steps):
                act()
                if number == MLP_BEGIN:
                    mlp.begin()
                if number < len(chores):
                    chores[number]()
            att.arrive()
            keep.start()
        else:
            for chore in chores:
                chore()

    h1 = h1_ref[...]
    chunk = step if linked else 0
    wa, wb = flat(w_ref[:, chunk, 0]), flat(w_ref[:, chunk, 1])
    qk_ref[...] = (nn(h1, wa) + bias_ref[step, 0:1, :384]).astype(BF)
    vv_ref[...] = (nn(h1, wb[:, :256]) + bias_ref[step, 0:1, 384:640]).astype(BF)
    lane = lanes_of((padded, 128))
    low = lane < 64
    field = lane & 31
    amounts = amount_ref[...]
    pad_lane = lanes_of((keys - padded, 128))
    pad_key = jnp.where(pad_lane == 79, NEGATIVE, 0.0).astype(BF)

    def window(w, carry):
        for slot in duties:
            for act in duties[slot]:
                pl.when(step * windows + w == slot)(act)
        rows = pl.ds(pl.multiple_of(w * padded, 16), padded)
        qk = qk_ref[rows, :]
        vv = vv_ref[rows, :]
        spread = nn(qk[:, :256], table_ref[0]) + nn(qk[:, :256], table_ref[1])
        wide = qk.astype(F32)
        wide_v = vv.astype(F32)
        parts = [wide[:, :128], wide[:, 128:256], wide[:, 256:384]]
        turned = [pltpu.roll(part, 64, 1) for part in parts]
        queries = [parts[0], turned[0], parts[1]]
        keys_low = [turned[1], parts[2], turned[2]]
        values = [wide_v[:, :128], pltpu.roll(wide_v[:, :128], 64, 1), wide_v[:, 128:256]]
        key_feat = key_feat_ref[rows, :].astype(F32)
        ones = jnp.where((lane == 64) | (lane == 65), 1.0, 0.0)
        outs = []
        for head in range(3):
            moved = shift_lanes(spread[:, head * 128 : head * 128 + 128], amounts, True)
            high = moved.astype(BF).astype(F32)
            rest = pltpu.roll(moved - high, 16, 1)
            feat = jnp.where(field < 16, high, rest)
            feat = jnp.where(field < 14, feat, jnp.where((field >= 16) & (field < 30), feat, 0.0))
            feat = jnp.where(lane == 79, 1.0, feat)
            query = jnp.where(low, queries[head] * 0.125, feat)
            key_ref[0, head, w, :padded, :] = jnp.where(low, keys_low[head], key_feat).astype(BF)
            key_ref[0, head, w, padded:, :] = pad_key
            value_ref[0, head, w, :padded, :] = jnp.where(low, values[head], ones).astype(BF)
            value_ref[0, head, w, padded:, :] = jnp.zeros((keys - padded, 128), BF)
            scores = nt(query.astype(BF), key_ref[0, head, w])
            top = jnp.max(scores, -1, keepdims=True)
            expo = jnp.exp(scores - top).astype(BF)
            mixed = nn(expo, value_ref[0, head, w])
            total = mixed[:, 64:65]
            outs.append(mixed / total)
            logsum = -(top + jnp.log(total))
            first = logsum.astype(BF).astype(F32)
            second = (logsum - first).astype(BF).astype(F32)
            third = logsum - first - second
            query = jnp.where(lane == 78, first, query)
            query = jnp.where(lane == 94, second, query)
            query = jnp.where(lane == 95, third, query)
            query_ref[0, head, rows, :] = query.astype(BF)
        out_ref[0, rows, :128] = jnp.where(low, 0.0, pltpu.roll(outs[0], 64, 1)).astype(BF)
        out_ref[0, rows, 128:] = jnp.where(low, outs[1], pltpu.roll(outs[2], 64, 1)).astype(BF)
        return carry

    lax.fori_loop(0, windows, window, 0)
    acc_ref[...] += nt(out_ref[0], flat(w_ref[:, chunk, 1])[:, 128:])
    if linked:

        @pl.when(step == pl.num_programs(0) - 1)
        def _():
            for slot in duties:
                if slot >= 16:
                    for act in duties[slot]:
                        act()
            mlp.arrive()
            mine.wait()
            keep.wait()
            att.finish()
            mlp.finish()


def mlp_kernel(
    x_ref, attn_ref, cotangent_ref, slots_ref, w_ref, bias_proj_ref, gain_ref, shift_ref, bias_down_ref, bias_up_ref,
    result_ref, gx1_ref, grad_ref, gbias_up_ref, small_ref,
    x1_ref, h2_ref, h2t_ref, gyt_ref, y_ref, dh_ref, gy_ref, bias_ref,
    *, windows, padded,
):
    first = lax.axis_index("tensor") * windows
    columns = w_ref.shape[4]
    step = pl.program_id(0)
    last = pl.num_programs(0) - 1

    @pl.when(step == 0)
    def _():
        for w in range(windows):
            spread_rows(cotangent_ref, gy_ref, w, cotangent_ref.shape[0] // windows, padded, alive_of(slots_ref, first + w))
        x1 = x_ref[...].astype(F32) + (attn_ref[...] + row(bias_proj_ref))
        x1_ref[...] = x1
        normed, _ = normed_of(x1)
        h2 = (normed * row(gain_ref) + row(shift_ref)).astype(BF)
        for tile in range(bias_ref.shape[0]):
            bias_ref[tile] = row(bias_up_ref)[:, tile * columns : tile * columns + columns]
        h2_ref[...] = h2
        h2t_ref[...] = h2.T
        gyt_ref[...] = gy_ref[...].T
        y_ref[...] = jnp.zeros_like(y_ref)
        dh_ref[...] = jnp.zeros_like(dh_ref)

    up, down = flat(w_ref[:, 0, 0]), flat(w_ref[:, 0, 1])
    strips = (grad_ref.shape[0], grad_ref.shape[3], columns)
    upper = nn(h2_ref[...], up) + bias_ref[step]
    half = 0.5 * (1.0 + lax.erf(upper * np.float32(np.sqrt(0.5))))
    slope = half + upper * (np.float32(1.0 / np.sqrt(2 * np.pi)) * jnp.exp(-0.5 * upper * upper))
    active = (upper * half).astype(BF)
    grad_upper = (nn(gy_ref[...], down) * slope).astype(BF)
    y_ref[...] += nt(active, down)
    dh_ref[...] += nt(grad_upper, up)
    grad_ref[:, 0, 1] = nn(gyt_ref[...], active).astype(BF).reshape(strips)
    grad_ref[:, 0, 0] = nn(h2t_ref[...], grad_upper).astype(BF).reshape(strips)
    gbias_up_ref[0] = jnp.sum(grad_upper.astype(F32), 0, keepdims=True)

    @pl.when(step == last)
    def _():
        x1 = x1_ref[...]
        result = x1 + (y_ref[...] + row(bias_down_ref))
        length = result_ref.shape[0] // windows
        for w in range(windows):
            part = alive_of(slots_ref, first + w) * result[w * padded : w * padded + length]
            result_ref[w * length : w * length + length, :] = part.astype(BF)
        normed, inverse = normed_of(x1)
        gy = gy_ref[...].astype(F32)
        dh = dh_ref[...]
        gx1_ref[...] = gy + norm_back(dh, normed, inverse, row(gain_ref))
        small_ref[0:1, :] = jnp.sum(dh * normed, 0, keepdims=True)
        small_ref[1:2, :] = jnp.sum(dh, 0, keepdims=True)
        small_ref[2:3, :] = jnp.sum(gy, 0, keepdims=True)
        small_ref[3:8, :] = jnp.zeros_like(small_ref[3:8, :])


def attend_back_kernel(*refs, windows, padded, keys, size, linked):
    step = pl.program_id(0)
    last = pl.num_programs(0) - 1
    scatter = None
    if linked:
        scatter = make_scatter(refs[11], refs[17], refs[27:])
        refs = refs[:11] + refs[12:17] + refs[18:27]
        pl.when(step == 0)(scatter.begin)
    (
        x_ref, gx1_ref, w_ref, gain_ref, shift_ref, rel_ref, amount_ref,
        query_ref, key_ref, value_ref, out_ref,
        grad_x_ref, grad_ref, small_ref, gbias_ref, grel_ref,
        h1t_ref, gbt_ref, gb_ref, dh_ref, do_ref, gqk_ref, gv_ref, spread_ref, table_ref,
    ) = refs

    @pl.when(step == 0)
    def _():
        normed, _ = normed_of(x_ref[...].astype(F32))
        h1t_ref[...] = (normed * row(gain_ref) + row(shift_ref)).astype(BF).T
        span = 2 * size - 1
        place = lax.broadcasted_iota(jnp.int32, (64, 128), 0)
        wanted = jnp.where(place < span, span - 1 - place, jnp.where(place < 2 * span, 32 + 2 * span - 1 - place, -1))
        chosen = jnp.where((lanes_of((64, 128)) & 63) == wanted, 1.0, 0.0).astype(BF)
        table_ref[...] = tn(chosen, rel_ref[...].astype(BF)).astype(BF)
        gb = gx1_ref[...].astype(BF)
        gb_ref[...] = gb
        gbt_ref[...] = gb.T
        dh_ref[...] = jnp.zeros_like(dh_ref)
        grel_ref[...] = jnp.zeros_like(grel_ref)
        small_ref[0:1, :] = jnp.sum(gb.astype(F32), 0, keepdims=True)

    do_ref[...] = nn(gb_ref[...], flat(w_ref[:, 0, 1])[:, 128:]).astype(BF)
    lane = lanes_of((padded, 128))
    low = lane < 64
    field = lane & 31
    amounts = amount_ref[...]
    kept = (lane >= 64) & (field < 14)

    def window(w, carry):
        if linked:
            for slot, act in zip(SUM_SLOTS, scatter.steps):
                pl.when(step * windows + w == slot)(act)
        rows = pl.ds(pl.multiple_of(w * padded, 16), padded)
        do = do_ref[rows, :].astype(F32)
        out = out_ref[0, rows, :].astype(F32)
        product = do * out
        grads = [pltpu.roll(do[:, :128], 64, 1), do[:, 128:], pltpu.roll(do[:, 128:], 64, 1)]
        sums = [
            jnp.sum(jnp.where(low, 0.0, product[:, :128]), -1, keepdims=True),
            jnp.sum(jnp.where(low, product[:, 128:], 0.0), -1, keepdims=True),
            jnp.sum(jnp.where(low, 0.0, product[:, 128:]), -1, keepdims=True),
        ]
        gq, gk, gv = [], [], []
        for head in range(3):
            delta = -sums[head]
            first = delta.astype(BF).astype(F32)
            grad_out = jnp.where(low, grads[head], jnp.where(lane == 64, first, jnp.where(lane == 65, delta - first, 0.0))).astype(BF)
            query, key, value = query_ref[0, head, rows, :], key_ref[0, head, w], value_ref[0, head, w]
            prob = jnp.exp(nt(query, key))
            grad_scores = (prob * nt(grad_out, value)).astype(BF)
            gv.append(tn(prob.astype(BF), grad_out)[:padded])
            gk.append(tn(grad_scores, query)[:padded])
            both = nn(grad_scores, key)
            back = shift_lanes(jnp.where(kept, both, 0.0), amounts, False)
            high = back.astype(BF).astype(F32)
            pack = jnp.where(low, pltpu.roll(back - high, 64, 1), high).astype(BF)
            spread_ref[head, rows, :] = pack
            gq.append(both * 0.125 + nn(pack, table_ref[...]))
        gqk_ref[rows, :128] = jnp.where(low, gq[0], pltpu.roll(gq[1], 64, 1)).astype(BF)
        gqk_ref[rows, 128:256] = jnp.where(low, gq[2], pltpu.roll(gk[0], 64, 1)).astype(BF)
        gqk_ref[rows, 256:] = jnp.where(low, gk[1], pltpu.roll(gk[2], 64, 1)).astype(BF)
        gv_ref[rows, :128] = jnp.where(low, gv[0], pltpu.roll(gv[1], 64, 1)).astype(BF)
        gv_ref[rows, 128:] = jnp.where(low, gv[2], 0.0).astype(BF)
        return carry

    lax.fori_loop(0, windows, window, 0)
    for head in range(3):
        grel_ref[...] += tn(spread_ref[head], query_ref[0, head])
    gqk, gv = gqk_ref[...], gv_ref[...]
    gbias_ref[0, :, :384] = jnp.sum(gqk.astype(F32), 0, keepdims=True)
    gbias_ref[0, :, 384:] = jnp.sum(gv.astype(F32), 0, keepdims=True)
    dh_ref[...] += nt(gqk, flat(w_ref[:, 0, 0])) + nt(gv, flat(w_ref[:, 0, 1])[:, :256])
    h1t = h1t_ref[...]
    strips = (grad_ref.shape[0], grad_ref.shape[3], -1)
    grad_ref[:, 0, 0] = nn(h1t, gqk).astype(BF).reshape(strips)
    one, two = nn(h1t, gv), nn(gbt_ref[...], out_ref[0])
    grad_ref[:, 0, 1, :, :128] = one[:, :128].astype(BF).reshape(strips)
    grad_ref[:, 0, 1, :, 128:256] = (one[:, 128:] + two[:, :128]).astype(BF).reshape(strips)
    grad_ref[:, 0, 1, :, 256:] = two[:, 128:].astype(BF).reshape(strips)

    @pl.when(step == last)
    def _():
        normed, inverse = normed_of(x_ref[...].astype(F32))
        dh = dh_ref[...]
        grad_x = (gx1_ref[...] + norm_back(dh, normed, inverse, row(gain_ref))).astype(BF)
        length = grad_x_ref.shape[0] // windows
        for w in range(windows):
            grad_x_ref[w * length : w * length + length, :] = grad_x[w * padded : w * padded + length]
        small_ref[1:2, :] = jnp.sum(dh * normed, 0, keepdims=True)
        small_ref[2:3, :] = jnp.sum(dh, 0, keepdims=True)
        small_ref[3:8, :] = jnp.zeros_like(small_ref[3:8, :])
        if linked:
            for slot, act in zip(SUM_SLOTS, scatter.steps):
                if slot >= 16:
                    act()
            scatter.finish()


def unpack_kernel(
    total_ref, att_ref, mlp_ref,
    qkv_ref, proj_ref, up_ref, down_ref, gain1_ref, shift1_ref, q_ref, v_ref, rel_h_ref, rel_w_ref,
    proj_bias_ref, gain2_ref, shift2_ref, up_bias_ref, down_bias_ref,
    *, span,
):
    qkv_ref[0] = att_ref[0, :, :192]
    qkv_ref[1] = att_ref[0, :, 192:]
    qkv_ref[2] = att_ref[1, :, :192]
    proj_ref[...] = att_ref[1, :, 192:].T
    up_ref[...] = mlp_ref[0]
    down_ref[...] = mlp_ref[1]
    for first, ref in ((0, proj_bias_ref), (6, gain1_ref), (12, shift1_ref), (18, gain2_ref), (24, shift2_ref), (30, down_bias_ref), (56, up_bias_ref)):
        for lane in range(0, ref.shape[0], 128):
            ref[pl.ds(lane, 128)] = total_ref[first + lane // 128]
    for start, ref in ((36, q_ref), (39, v_ref)):
        pieces = []
        for t in range(ref.shape[0] // 192):
            first = start + 5 * t
            pieces.append((total_ref[first : first + 1, :], total_ref[first + 1 : first + 2, :]))
        for pair in range(len(pieces) // 2):
            one, two = pieces[2 * pair], pieces[2 * pair + 1]
            low = lanes_of((1, 128)) < 64
            turned = [pltpu.roll(jnp.broadcast_to(v, (8, 128)), 64, 1)[:1] for v in two]
            parts = [one[0], jnp.where(low, one[1], turned[0]), jnp.where(low, turned[0], turned[1])]
            for i, values in enumerate(parts):
                ref[pl.ds(pair * 384 + i * 128, 128)] = values[0]
    rel = total_ref[total_ref.shape[0] - 64 :, :]
    high = rel.astype(BF)
    middle = (rel - high.astype(F32)).astype(BF)
    rest = (rel - high.astype(F32) - middle.astype(F32)).astype(BF)
    for ref, first in ((rel_h_ref, 0), (rel_w_ref, 32)):
        place = lax.broadcasted_iota(jnp.int32, (32, 64), 0)
        chosen = jnp.where(lanes_of((32, 64)) == first + span - 1 - place, 1.0, 0.0).astype(BF)
        values = nn(chosen, high) + nn(chosen, middle) + nn(chosen, rest)
        ref[...] = 8.0 * values[:span, :64]


def whole(shape):
    return pl.BlockSpec(shape, lambda *index: (0,) * len(shape))


def once(shape):
    return pl.BlockSpec(shape, lambda *index: (0,) * len(shape), pipeline_mode=pl.Buffered(1))


def shards(
    block_input, cotangent, pad_mask, slot_window, qkv_w, proj_w, fc1_w, fc2_w,
    norm1_gain, norm1_bias, q_bias, v_bias, rel_h, rel_w, proj_bias,
    norm2_gain, norm2_bias, fc1_bias, fc2_bias,
):
    part = lax.axis_index("tensor")
    count_dp, count_t = lax.axis_size("dp"), lax.axis_size("tensor")
    length = pad_mask.shape[1]
    local_rows, width = block_input.shape
    windows = local_rows // length
    size = rel_h.shape[0] // 2 + 1
    padded = -(-length // 16) * 16
    keys = -(-length // 128) * 128
    rows = windows * padded
    strip = width // count_dp

    slots = jnp.pad(slot_window, (0, 128 - slot_window.shape[0]), constant_values=-1).reshape(1, 128)
    rel = jnp.pad(jnp.concatenate([rel_h, rel_w]), ((0, 64 - 2 * rel_h.shape[0]), (0, 64)))

    place = np.arange(padded)
    row_of, col_of = place // size, place % size
    inside = place < length
    amount = np.zeros((padded, 128), np.int32)
    amount[:, :] = np.where(
        (np.arange(128) % 64 < 32)[None, :], (size - 1 - row_of)[:, None], (size - 1 - col_of)[:, None]
    ) * inside[:, None]
    amount = jnp.asarray(amount)
    feat = np.zeros((padded, 128), np.float32)
    for a in range(size):
        for base, pos in ((64, row_of), (96, col_of)):
            feat[:, base + a] = (pos == a) & inside
            feat[:, base + 16 + a] = (pos == a) & inside
    feat[:, [78, 94, 95]] = 1.0
    feat[:, 79] = np.where(inside, 0.0, NEGATIVE)
    feat = jnp.asarray(feat.astype(BF))
    span = rel_h.shape[0]

    q_w, k_w, v_w = qkv_w[0], qkv_w[1], qkv_w[2]
    shard_att = jnp.stack([jnp.concatenate([q_w, k_w], 1), jnp.concatenate([v_w, proj_w.T], 1)])
    shard_mlp = jnp.stack([fc1_w, fc2_w.T])
    columns = fc1_w.shape[1]
    linked = count_dp == 8 and count_t == 4 and strip % 16 == 0 and windows == 4
    any_spec, vmem_spec = pl.BlockSpec(memory_space=pl.ANY), pl.BlockSpec(memory_space=pltpu.VMEM)
    blocks, depth = (count_dp, strip) if linked else (1, width)

    def talk(number, **more):
        return pltpu.CompilerParams(
            vmem_limit_bytes=VMEM_LIMIT, collective_id=number, has_side_effects=True, **more)

    def gather_all(pieces):
        every = lax.all_gather(pieces, AXES, axis=0, tiled=False).reshape(count_dp, count_t, *pieces.shape)
        return every.transpose(1, 2, 0, 3, 4).reshape(1, count_t, 2, width, pieces.shape[2])

    if not linked:
        w_att, w_mlp = gather_all(shard_att), gather_all(shard_mlp)

    vec = once((width,))
    params = pltpu.CompilerParams(dimension_semantics=("arbitrary",), vmem_limit_bytes=VMEM_LIMIT)

    query, key, value, out, attn, x, *rest = pl.pallas_call(
        partial(attend_kernel, windows=windows, padded=padded, keys=keys, size=size, linked=linked),
        grid=(count_t,),
        in_specs=[
            once((local_rows, width)),
        ] + [pl.BlockSpec((blocks, 1, 2, depth, 384), lambda t: (0, t, 0, 0, 0))] * (not linked) + [
            vec, vec, vec, vec, once((64, 128)), once((1, 128)), once(pad_mask.shape[::-1]),
            once((padded, 128)), once((padded, 128)),
        ] + [once((2, strip, 384)), once((2, strip, columns))] * linked,
        out_specs=[
            pl.BlockSpec((1, 3, rows, 128), lambda t: (t, 0, 0, 0)),
            pl.BlockSpec((1, 3, windows, keys, 128), lambda t: (t, 0, 0, 0, 0)),
            pl.BlockSpec((1, 3, windows, keys, 128), lambda t: (t, 0, 0, 0, 0)),
            pl.BlockSpec((1, rows, 256), lambda t: (t, 0, 0)),
            whole((rows, width)), whole((rows, width)),
        ] + [any_spec, any_spec] * linked,
        out_shape=[
            jax.ShapeDtypeStruct((count_t, 3, rows, 128), BF),
            jax.ShapeDtypeStruct((count_t, 3, windows, keys, 128), BF),
            jax.ShapeDtypeStruct((count_t, 3, windows, keys, 128), BF),
            jax.ShapeDtypeStruct((count_t, rows, 256), BF),
            jax.ShapeDtypeStruct((rows, width), F32),
            jax.ShapeDtypeStruct((rows, width), BF),
        ] + [jax.ShapeDtypeStruct((count_dp, count_t, 2, strip, n), BF) for n in (384, columns)] * linked,
        scratch_shapes=[
            pltpu.VMEM((rows, width), BF), pltpu.VMEM((rows, 384), BF), pltpu.VMEM((rows, 256), BF),
            pltpu.VMEM((2, 256, 384), BF), pltpu.VMEM((rows, 128), BF), pltpu.VMEM((count_t, 1, 640), F32),
        ]
        + ([pltpu.VMEM((count_dp, count_t, 2, strip, 384), BF)] + gather_scratch() * 2 + [pltpu.SemaphoreType.DMA((2,))]) * linked,
        compiler_params=talk(2, dimension_semantics=("arbitrary",)) if linked else params,
        name="attend",
    )(
        block_input, *([] if linked else [w_att]), norm1_gain, norm1_bias, q_bias, v_bias, rel, slots, pad_mask.T, feat, amount,
        *([shard_att, shard_mlp] * linked)
    )
    if linked:
        w_att, w_mlp = rest

    mlp_block = pl.BlockSpec((blocks, 1, 2, depth, columns), lambda j: (0, j, 0, 0, 0))
    result, gx1, grad_mlp, gbias_up, small2 = pl.pallas_call(
        partial(mlp_kernel, windows=windows, padded=padded),
        grid=(count_t,),
        in_specs=[
            once((rows, width)), once((rows, width)), once((local_rows, width)), once((1, 128)),
            mlp_block, vec, vec, vec, vec, once(fc1_bias.shape),
        ],
        out_specs=[
            whole((local_rows, width)), whole((rows, width)),
            mlp_block,
            pl.BlockSpec((1, 1, columns), lambda j: (j, 0, 0)),
            whole((8, width)),
        ],
        out_shape=[
            jax.ShapeDtypeStruct((local_rows, width), BF),
            jax.ShapeDtypeStruct((rows, width), F32),
            jax.ShapeDtypeStruct((blocks, count_t, 2, depth, columns), BF),
            jax.ShapeDtypeStruct((count_t, 1, columns), F32),
            jax.ShapeDtypeStruct((8, width), F32),
        ],
        scratch_shapes=[
            pltpu.VMEM((rows, width), F32), pltpu.VMEM((rows, width), BF),
            pltpu.VMEM((width, rows), BF), pltpu.VMEM((width, rows), BF),
            pltpu.VMEM((rows, width), F32), pltpu.VMEM((rows, width), F32), pltpu.VMEM((rows, width), BF),
            pltpu.VMEM((count_t, 1, columns), F32),
        ],
        compiler_params=params,
        name="mlp",
    )(x, attn, cotangent, slots, w_mlp, proj_bias, norm2_gain, norm2_bias, fc2_bias, fc1_bias)

    grad_x, grad_att, small1, gbias_att, grel, *rest = pl.pallas_call(
        partial(attend_back_kernel, windows=windows, padded=padded, keys=keys, size=size, linked=linked),
        grid=(count_t,),
        in_specs=[
            once((rows, width)), once((rows, width)),
            pl.BlockSpec((blocks, 1, 2, depth, 384), lambda t: (0, t, 0, 0, 0)),
            vec, vec, once((64, 128)), once((padded, 128)),
            pl.BlockSpec((1, 3, rows, 128), lambda t: (t, 0, 0, 0)),
            pl.BlockSpec((1, 3, windows, keys, 128), lambda t: (t, 0, 0, 0, 0)),
            pl.BlockSpec((1, 3, windows, keys, 128), lambda t: (t, 0, 0, 0, 0)),
            pl.BlockSpec((1, rows, 256), lambda t: (t, 0, 0)),
        ] + [any_spec] * linked,
        out_specs=[
            whole((local_rows, width)),
            pl.BlockSpec((blocks, 1, 2, depth, 384), lambda t: (0, t, 0, 0, 0)),
            whole((8, width)),
            pl.BlockSpec((1, 1, 640), lambda t: (t, 0, 0)),
            whole((128, 128)),
        ] + [whole((2, strip, columns))] * linked,
        out_shape=[
            jax.ShapeDtypeStruct((local_rows, width), BF),
            jax.ShapeDtypeStruct((blocks, count_t, 2, depth, 384), BF),
            jax.ShapeDtypeStruct((8, width), F32),
            jax.ShapeDtypeStruct((count_t, 1, 640), F32),
            jax.ShapeDtypeStruct((128, 128), F32),
        ] + [jax.ShapeDtypeStruct((2, strip, columns), F32)] * linked,
        scratch_shapes=[
            pltpu.VMEM((width, rows), BF), pltpu.VMEM((width, rows), BF), pltpu.VMEM((rows, width), BF),
            pltpu.VMEM((rows, width), F32), pltpu.VMEM((rows, 256), BF),
            pltpu.VMEM((rows, 384), BF), pltpu.VMEM((rows, 256), BF), pltpu.VMEM((3, rows, 128), BF),
            pltpu.VMEM((128, 128), BF),
        ] + (scatter_scratch(2, strip, columns) if linked else []),
        compiler_params=talk(3, dimension_semantics=("arbitrary",)) if linked else params,
        name="attend_back",
    )(
        x, gx1, w_att, norm1_gain, norm1_bias, rel, amount, query, key, value, out,
        *([grad_mlp.reshape(count_dp // 2, 2, count_t, 2, strip, columns)] * linked if linked else [])
    )

    if linked:
        sum_mlp = rest[0]
        count = 36 + 5 * count_t + fc1_bias.shape[0] // 128 + 64
        sum_att, total = pl.pallas_call(
            reduce_kernel,
            in_specs=[any_spec] + [vmem_spec] * 5, out_specs=[vmem_spec, vmem_spec],
            out_shape=[jax.ShapeDtypeStruct((2, strip, 384), F32), jax.ShapeDtypeStruct((count, 128), F32)],
            scratch_shapes=[
                pltpu.VMEM((count, 128), F32), pltpu.VMEM((10, count, 128), F32),
                pltpu.SemaphoreType.DMA((5,)), pltpu.SemaphoreType.DMA((5,)),
            ] + scatter_scratch(2, strip, 384),
            compiler_params=talk(4),
            name="reduce_attention",
        )(grad_att.reshape(count_dp // 2, 2, count_t, 2, strip, 384), small1, small2, gbias_att, gbias_up, grel)
        like = (
            qkv_w, proj_w, fc1_w, fc2_w.T, norm1_gain, norm1_bias, q_bias, v_bias, rel_h, rel_w,
            proj_bias, norm2_gain, norm2_bias, fc1_bias, fc2_bias,
        )
        shapes = [jax.ShapeDtypeStruct(v.shape, F32) for v in like]
        outs = pl.pallas_call(
            partial(unpack_kernel, span=span),
            in_specs=[vmem_spec] * 3, out_specs=[vmem_spec] * len(shapes), out_shape=shapes,
            compiler_params=pltpu.CompilerParams(vmem_limit_bytes=VMEM_LIMIT),
            name="unpack",
        )(total, sum_att, sum_mlp)
        return (result, grad_x, *outs[:3], outs[3].T, *outs[4:])
    parts = [
        small1[:3].reshape(-1, 128), small2[:3].reshape(-1, 128), gbias_att.reshape(-1, 128), gbias_up.reshape(-1, 128), grel[64:],
    ]
    def scatter_all(grads):
        grads = grads.reshape(count_t, 2, count_dp, strip, grads.shape[4]).transpose(2, 0, 1, 3, 4)
        grads = grads.reshape(count_dp * count_t, *grads.shape[2:])
        return lax.psum_scatter(grads, AXES, scatter_dimension=0, tiled=False).astype(F32)

    sum_mlp, sum_att = scatter_all(grad_mlp), scatter_all(grad_att)
    small = lax.psum(jnp.concatenate(parts), AXES)
    cuts = np.cumsum([part.shape[0] for part in parts])[:-1]
    small1, small2, gbias_att, gbias_up, grad_rel = jnp.split(small, cuts)
    small1, small2 = small1.reshape(3, width), small2.reshape(3, width)
    gbias_att = gbias_att.reshape(count_t, 1, 640)
    grad_rel = 8.0 * grad_rel[:, :64]
    head_q, head_k = sum_att[0, :, :192], sum_att[0, :, 192:]
    head_v, head_p = sum_att[1, :, :192], sum_att[1, :, 192:]
    return (
        result,
        grad_x,
        jnp.stack([head_q, head_k, head_v]),
        head_p.T,
        sum_mlp[0],
        sum_mlp[1].T,
        small1[1],
        small1[2],
        gbias_att[:, 0, :192].reshape(-1),
        gbias_att[:, 0, 384:576].reshape(-1),
        grad_rel[:span][::-1],
        grad_rel[32 : 32 + span][::-1],
        small1[0],
        small2[0],
        small2[1],
        gbias_up.reshape(-1),
        small2[2],
    )


def solution(mesh):
    return jax.shard_map(
        shards,
        mesh=mesh,
        in_specs=(
            P(AXES, None), P(AXES, None), P(), P("dp"),
            P(None, "dp", "tensor"), P("tensor", "dp"), P("dp", "tensor"), P("tensor", "dp"),
        )
        + (P(),) * 11,
        out_specs=(
            P(AXES, None), P(AXES, None),
            P(None, "dp", "tensor"), P("tensor", "dp"), P("dp", "tensor"), P("tensor", "dp"),
        )
        + (P(),) * 11,
        check_vma=False,
    )
```
